256 devices in a mesh: dp: 32 (over z, y), row: 2 (over core), col: 4 (over x).
Axes of the slice: x: 4, y: 4, z: 8, core: 2. Of those that a mesh axis runs over, the one named last changes fastest.
Arguments:
- x_input: bfloat16 [32, 32, 64, 640], P('dp', 'row', 'col'), may hold values from -6 to 6
- pre_act: bfloat16 [32, 32, 64, 640], P('dp', 'row', 'col'), may hold values from -6 to 6
- out_grad: bfloat16 [32, 32, 64, 640], P('dp', 'row', 'col'), may hold values from -0.15625 to 0.15625
- conv_weight: bfloat16 [3, 3, 640, 640], replicated, may hold values from -0.078125 to 0.078125
- q_prev: float32 [5760, 2, 64], replicated, may hold values from -6 to 6
Outputs:
- p_basis: float32 [640, 2, 64], P('dp')
- q_next: float32 [5760, 2, 64], P('dp')
The draws below stay inside these ranges and needn't reach their ends.
All inputs are finite; a program needn't handle non-finite values.
Results may differ from the reference program's by a relative error of at most 0.0036.
Values may be sent and summed in bfloat16 or wider, within the bound.
A program may use at most 128 MiB of HBM per device.

```python
import jax
import jax.numpy as jnp
from jax import lax

C = 640
RANK = 64
IMAGES = 32
HIMG = 32
WIMG = 64
KROWS = 5760


def block_scale(key, shape, cuts, least, high):
    factor_of = 1.0
    for position, blocks in cuts:
        steps = jax.random.uniform(jax.random.fold_in(jax.random.fold_in(key, 6), position), (blocks,), jnp.float32, least / len(cuts), high / len(cuts))
        factor_of = factor_of * jnp.repeat(jnp.exp(steps), shape[position] // blocks).reshape((-1,) + (1,) * (len(shape) - 1 - position))
    return factor_of


def noise(own_key, dims, width, reach, cuts=(), dtype=jnp.bfloat16):
    array = width * jax.random.normal(own_key, dims, jnp.float32)
    if cuts:
        array = array * block_scale(own_key, dims, cuts, -0.22, 0.18)
    return jnp.clip(array, -reach, reach).astype(dtype)


def setup_inputs(seed: int = 0) -> dict:
    key_of = jax.random.split(jax.random.key(seed), 6)
    x_input = noise(key_of[0], (IMAGES, HIMG, WIMG, C), 1.0, 6.0, ((0, 32), (1, 2), (2, 4)))
    pre_act = noise(key_of[1], (IMAGES, HIMG, WIMG, C), 1.0, 6.0, ((0, 32), (1, 2), (2, 4)))
    out_grad = noise(key_of[2], (IMAGES, HIMG, WIMG, C), 0.01, 0.15625, ((0, 32), (1, 2), (2, 4)))
    conv_weight = noise(key_of[3], (3, 3, C, C), (9 * C) ** -0.5, 0.078125)
    q_prev = noise(key_of[4], (KROWS, 2, RANK), 1.0, 6.0, (), jnp.float32)
    return {"x_input": x_input, "pre_act": pre_act, "out_grad": out_grad, "conv_weight": conv_weight, "q_prev": q_prev}


def silu_slope(pre_float):
    sigma = jax.nn.sigmoid(pre_float)
    return sigma * (1.0 + pre_float * (1.0 - sigma))

def contract_first(left, right, exact):
    if exact:
        return lax.dot_general(left.astype(jnp.float32), right.astype(jnp.float32), (((0,), (0,)), ((), ())), precision=lax.Precision.HIGHEST, preferred_element_type=jnp.float32)
    return lax.dot_general(left.astype(jnp.float32), right.astype(jnp.float32), (((0,), (0,)), ((), ())), preferred_element_type=jnp.float32)

def reference(x_input, pre_act, out_grad, conv_weight, q_prev):
    images, height, breadth, channels = x_input.shape
    pixels = images * height * breadth
    padding = ((0, 0), (1, 1), (1, 1), (0, 0))
    pre_float = pre_act.astype(jnp.float32)
    hidden = jax.nn.silu(pre_float).astype(jnp.bfloat16)
    hidden_flat = hidden.reshape(pixels, channels)
    grad_pad = jnp.pad(out_grad, padding)
    back_grad = jnp.zeros((pixels, channels), jnp.float32)
    second_taps = []
    for shift_row in (-1, 0, 1):
        for shift_col in (-1, 0, 1):
            window = grad_pad[:, 1 - shift_row:1 - shift_row + height, 1 - shift_col:1 - shift_col + breadth, :].reshape(pixels, channels)
            back_grad = back_grad + lax.dot_general(window.astype(jnp.float32), conv_weight[shift_row + 1, shift_col + 1].astype(jnp.float32), (((1,), (1,)), ((), ())), preferred_element_type=jnp.float32)
            second_taps.append(contract_first(hidden_flat, window, False))
    pre_grad = (back_grad * silu_slope(pre_float.reshape(pixels, channels))).astype(jnp.bfloat16)
    deriv_pad = jnp.pad(pre_grad.reshape(images, height, breadth, channels), padding)
    input_flat = x_input.reshape(pixels, channels)
    first_taps = []
    for shift_row in (-1, 0, 1):
        for shift_col in (-1, 0, 1):
            window = deriv_pad[:, 1 - shift_row:1 - shift_row + height, 1 - shift_col:1 - shift_col + breadth, :].reshape(pixels, channels)
            first_taps.append(contract_first(input_flat, window, False))
    moments = [jnp.stack(first_taps).reshape(9 * channels, channels), jnp.stack(second_taps).reshape(9 * channels, channels)]
    bases = []
    nexts = []
    for layer in range(2):
        power_raw = contract_first(moments[layer], q_prev[:, layer, :], True)
        gram_matrix = jnp.dot(power_raw.T.astype(jnp.float32), power_raw.astype(jnp.float32), precision=lax.Precision.HIGHEST, preferred_element_type=jnp.float32)
        lower = jnp.linalg.cholesky(gram_matrix)
        ortho_basis = lax.linalg.triangular_solve(lower, power_raw, left_side=False, lower=True, transpose_a=True)
        bases.append(ortho_basis)
        nexts.append(jnp.dot(moments[layer].astype(jnp.float32), ortho_basis.astype(jnp.float32), precision=lax.Precision.HIGHEST, preferred_element_type=jnp.float32))
    return (jnp.stack(bases, axis=1), jnp.stack(nexts, axis=1))
```

```python
import jax
import jax.numpy as jnp
from jax import lax
from jax.sharding import PartitionSpec as P


def padded_2(value, sides, width):
    for axis, dim in sides:
        size, length = (lax.axis_size(axis), value.shape[dim])
        up = [(i, (i + 1) % size) for i in range(size - 1)]
        down = [(j, i) for i, j in up]
        last = lax.slice_in_dim(value, length - width, length, axis=dim)
        leading = lax.slice_in_dim(value, 0, width, axis=dim)
        before = lax.ppermute(last, axis, up)
        after = lax.ppermute(leading, axis, down)
        value = jnp.concatenate([before, value, after], axis=dim)
    return value


def silu_slope(pre_float):
    sigma = jax.nn.sigmoid(pre_float)
    return sigma * (1.0 + pre_float * (1.0 - sigma))


def contract_first(left, right, exact):
    if exact:
        return lax.dot_general(
            left,
            right,
            (((0,), (0,)), ((), ())),
            precision=lax.Precision.HIGHEST,
            preferred_element_type=jnp.float32,
        )
    return lax.dot_general(
        left, right, (((0,), (0,)), ((), ())), preferred_element_type=jnp.float32
    )


def tap_window(padded, shift_row, shift_col, height, breadth):
    return padded[
        1 + shift_row : 1 + shift_row + height, 1 + shift_col : 1 + shift_col + breadth, :
    ].reshape(height * breadth, padded.shape[2])


def column_terms(moments, q_prev):
    return jnp.stack(
        [contract_first(moments[layer], q_prev[:, layer, :], True) for layer in range(2)], axis=1
    )


def row_terms(moments, ortho_basis):
    return jnp.stack(
        [
            jnp.dot(
                moments[layer],
                ortho_basis[:, layer, :],
                precision=lax.Precision.HIGHEST,
                preferred_element_type=jnp.float32,
            )
            for layer in range(2)
        ],
        axis=1,
    )


def gram_of(power_raw):
    return jnp.einsum(
        "mqn,mqg->qng",
        power_raw,
        power_raw,
        precision=lax.Precision.HIGHEST,
        preferred_element_type=jnp.float32,
    )


def orthonormal(power_raw, gram_matrix):
    bases = []
    for layer in range(2):
        lower = jnp.linalg.cholesky(gram_matrix[layer])
        bases.append(
            lax.linalg.triangular_solve(
                lower, power_raw[:, layer, :], left_side=False, lower=True, transpose_a=True
            )
        )
    return jnp.stack(bases, axis=1)


def on_device(x_input, pre_act, out_grad, conv_weight, q_prev):
    height, breadth, channels = (x_input.shape[1], x_input.shape[2], x_input.shape[3])
    pixels = height * breadth
    input_tile = x_input.reshape(height, breadth, channels)
    grad_tile = out_grad.reshape(height, breadth, channels)
    pre_float = pre_act.reshape(pixels, channels).astype(jnp.float32)
    hidden_flat = jax.nn.silu(pre_float).astype(jnp.bfloat16)
    grad_pad = padded_2(grad_tile, (("row", 0), ("col", 1)), 1)
    back_grad = jnp.zeros((pixels, channels), jnp.float32)
    second_taps = []
    for shift_row in (-1, 0, 1):
        for shift_col in (-1, 0, 1):
            window = tap_window(grad_pad, -shift_row, -shift_col, height, breadth)
            back_grad = back_grad + lax.dot_general(
                window,
                conv_weight[shift_row + 1, shift_col + 1],
                (((1,), (1,)), ((), ())),
                preferred_element_type=jnp.float32,
            )
            second_taps.append(contract_first(hidden_flat, window, False))
    pre_grad = (back_grad * silu_slope(pre_float)).astype(jnp.bfloat16)
    first_taps = []
    deriv_pad = padded_2(pre_grad.reshape(height, breadth, channels), (("row", 0), ("col", 1)), 1)
    input_flat = input_tile.reshape(pixels, channels)
    for shift_row in (-1, 0, 1):
        for shift_col in (-1, 0, 1):
            first_taps.append(
                contract_first(
                    input_flat,
                    tap_window(deriv_pad, -shift_row, -shift_col, height, breadth),
                    False,
                )
            )
    moments = jnp.stack(
        [
            jnp.stack(first_taps).reshape(9 * channels, channels),
            jnp.stack(second_taps).reshape(9 * channels, channels),
        ]
    )
    kernel_rows = moments.shape[1]
    owner = lax.axis_index("dp")
    basis_count = channels // lax.axis_size("dp")
    factor_count = kernel_rows // lax.axis_size("dp")
    power_raw = column_terms(moments, q_prev)
    for axis in ("row", "col", "dp"):
        power_raw = lax.psum(power_raw, axis)
    ortho_basis = orthonormal(power_raw, gram_of(power_raw))
    factor_out = lax.psum_scatter(row_terms(moments, ortho_basis), "dp", scatter_dimension=0, tiled=True)
    for axis in ("row", "col"):
        factor_out = lax.psum(factor_out, axis)
    basis_out = lax.dynamic_slice_in_dim(ortho_basis, owner * basis_count, basis_count, 0)
    return (basis_out, factor_out)


def solution(mesh):
    placed = (
        P("dp", "row", "col", None),
        P("dp", "row", "col", None),
        P("dp", "row", "col", None),
        P(),
        P(),
    )
    return jax.shard_map(
        on_device,
        mesh=mesh,
        in_specs=placed,
        out_specs=(P("dp", None, None), P("dp", None, None)),
        check_vma=False,
    )
```

```python
import functools
import math

import jax
import jax.numpy as jnp
from jax import lax
from jax.experimental import pallas as pl
from jax.experimental.pallas import tpu as pltpu
from jax.sharding import PartitionSpec as P


def member_coords(j, axes, sizes):
    coords = {}
    for axis in reversed(axes):
        coords[axis] = lax.rem(j, sizes[axis])
        j = j // sizes[axis]
    return coords


def exchange_kernel(x_ref, o_ref, send_sem, recv_sem, local_sem, *, axes, sizes, gather):
    n = math.prod(sizes[a] for a in axes)
    me = 0
    for axis in axes:
        me = me * sizes[axis] + lax.axis_index(axis)
    barrier = pltpu.get_barrier_semaphore()
    for s in range(1, n):
        peer = member_coords(lax.rem(me + s, n), axes, sizes)
        pl.semaphore_signal(barrier, inc=1, device_id=peer, device_id_type=pl.DeviceIdType.MESH)
    pl.semaphore_wait(barrier, n - 1)
    copies = []
    for s in range(1, n):
        dst = lax.rem(me + s, n)
        copy = pltpu.make_async_remote_copy(
            src_ref=x_ref if gather else x_ref.at[dst],
            dst_ref=o_ref.at[me],
            send_sem=send_sem.at[s - 1],
            recv_sem=recv_sem.at[s - 1],
            device_id=member_coords(dst, axes, sizes),
            device_id_type=pl.DeviceIdType.MESH,
        )
        copy.start()
        copies.append(copy)
    local = pltpu.make_async_copy(x_ref if gather else x_ref.at[me], o_ref.at[me], local_sem)
    local.start()
    for copy in copies:
        copy.wait_send()
        copy.wait_recv()
    local.wait()


def exchange(x, axes, sizes, cid, gather=False):
    n = math.prod(sizes[a] for a in axes)
    out_shape = (n,) + (x.shape if gather else x.shape[1:])
    return pl.pallas_call(
        functools.partial(exchange_kernel, axes=axes, sizes=sizes, gather=gather),
        out_shape=jax.ShapeDtypeStruct(out_shape, x.dtype),
        in_specs=[pl.BlockSpec(memory_space=pl.ANY)],
        out_specs=pl.BlockSpec(memory_space=pl.ANY),
        scratch_shapes=[
            pltpu.SemaphoreType.DMA((max(n - 1, 1),)),
            pltpu.SemaphoreType.DMA((max(n - 1, 1),)),
            pltpu.SemaphoreType.DMA,
        ],
        compiler_params=pltpu.CompilerParams(collective_id=cid, has_side_effects=True),
    )(x)


def padded_2(value, sides, width):
    for axis, dim in sides:
        size, length = (lax.axis_size(axis), value.shape[dim])
        up = [(i, (i + 1) % size) for i in range(size - 1)]
        down = [(j, i) for i, j in up]
        last = lax.slice_in_dim(value, length - width, length, axis=dim)
        leading = lax.slice_in_dim(value, 0, width, axis=dim)
        before = lax.ppermute(last, axis, up)
        after = lax.ppermute(leading, axis, down)
        value = jnp.concatenate([before, value, after], axis=dim)
    return value


def silu_slope(pre_float):
    sigma = jax.nn.sigmoid(pre_float)
    return sigma * (1.0 + pre_float * (1.0 - sigma))


def contract_first(left, right, exact):
    if exact:
        return lax.dot_general(
            left,
            right,
            (((0,), (0,)), ((), ())),
            precision=lax.Precision.HIGHEST,
            preferred_element_type=jnp.float32,
        )
    return lax.dot_general(
        left, right, (((0,), (0,)), ((), ())), preferred_element_type=jnp.float32
    )


def tap_window(padded, shift_row, shift_col, height, breadth):
    return padded[
        1 + shift_row : 1 + shift_row + height, 1 + shift_col : 1 + shift_col + breadth, :
    ].reshape(height * breadth, padded.shape[2])


def column_terms(moments, q_prev):
    return jnp.stack(
        [contract_first(moments[layer], q_prev[:, layer, :], True) for layer in range(2)], axis=1
    )


def row_terms(moments, ortho_basis):
    return jnp.stack(
        [
            jnp.dot(
                moments[layer],
                ortho_basis[:, layer, :],
                precision=lax.Precision.HIGHEST,
                preferred_element_type=jnp.float32,
            )
            for layer in range(2)
        ],
        axis=1,
    )


def gram_of(power_raw):
    return jnp.einsum(
        "mqn,mqg->qng",
        power_raw,
        power_raw,
        precision=lax.Precision.HIGHEST,
        preferred_element_type=jnp.float32,
    )


def orthonormal(power_raw, gram_matrix):
    bases = []
    for layer in range(2):
        lower = jnp.linalg.cholesky(gram_matrix[layer])
        bases.append(
            lax.linalg.triangular_solve(
                lower, power_raw[:, layer, :], left_side=False, lower=True, transpose_a=True
            )
        )
    return jnp.stack(bases, axis=1)


def on_device(x_input, pre_act, out_grad, conv_weight, q_prev):
    height, breadth, channels = (x_input.shape[1], x_input.shape[2], x_input.shape[3])
    pixels = height * breadth
    input_tile = x_input.reshape(height, breadth, channels)
    grad_tile = out_grad.reshape(height, breadth, channels)
    pre_float = pre_act.reshape(pixels, channels).astype(jnp.float32)
    hidden_flat = jax.nn.silu(pre_float).astype(jnp.bfloat16)
    grad_pad = padded_2(grad_tile, (("row", 0), ("col", 1)), 1)
    back_grad = jnp.zeros((pixels, channels), jnp.float32)
    second_taps = []
    for shift_row in (-1, 0, 1):
        for shift_col in (-1, 0, 1):
            window = tap_window(grad_pad, -shift_row, -shift_col, height, breadth)
            back_grad = back_grad + lax.dot_general(
                window,
                conv_weight[shift_row + 1, shift_col + 1],
                (((1,), (1,)), ((), ())),
                preferred_element_type=jnp.float32,
            )
            second_taps.append(contract_first(hidden_flat, window, False))
    pre_grad = (back_grad * silu_slope(pre_float)).astype(jnp.bfloat16)
    first_taps = []
    deriv_pad = padded_2(pre_grad.reshape(height, breadth, channels), (("row", 0), ("col", 1)), 1)
    input_flat = input_tile.reshape(pixels, channels)
    for shift_row in (-1, 0, 1):
        for shift_col in (-1, 0, 1):
            first_taps.append(
                contract_first(
                    input_flat,
                    tap_window(deriv_pad, -shift_row, -shift_col, height, breadth),
                    False,
                )
            )
    moments = jnp.stack(
        [
            jnp.stack(first_taps).reshape(9 * channels, channels),
            jnp.stack(second_taps).reshape(9 * channels, channels),
        ]
    )
    sizes = {axis: lax.axis_size(axis) for axis in ("dp", "row", "col")}
    power_raw = all_sum_small(column_terms(moments, q_prev), sizes)
    ortho_basis = orthonormal(power_raw, gram_of(power_raw))
    basis_count = channels // sizes["dp"]
    basis_out = lax.dynamic_slice_in_dim(ortho_basis, lax.axis_index("dp") * basis_count, basis_count, 0)
    factor_out = block_sum(row_terms(moments, ortho_basis), sizes)
    return (basis_out, factor_out)


def all_sum_small(value, sizes):
    shape = value.shape
    rows, group = shape[0], sizes["row"] * sizes["col"]
    flat = value.reshape(rows, -1)
    part = exchange(flat.reshape(group, rows // group, -1), ("row", "col"), sizes, 0).sum(0)
    piece = part.reshape(sizes["dp"], -1, 64)
    piece = exchange(piece, ("dp",), sizes, 1).sum(0)
    part = exchange(piece, ("dp",), sizes, 2, gather=True).reshape(part.shape)
    flat = exchange(part, ("row", "col"), sizes, 3, gather=True).reshape(flat.shape)
    return flat.reshape(shape)


def block_sum(value, sizes):
    shape = value.shape
    blocks, group = sizes["dp"], sizes["row"] * sizes["col"]
    block_rows = shape[0] // blocks
    piece_rows = -(-block_rows // (group * 8)) * 8
    lanes = math.prod(shape[1:])
    padded = jnp.pad(value.reshape(blocks, block_rows, lanes), ((0, 0), (0, piece_rows * group - block_rows), (0, 0)))
    pieces = padded.reshape(blocks, sizes["row"], sizes["col"], piece_rows, lanes).transpose(1, 2, 0, 3, 4)
    pieces = exchange(pieces, ("row",), sizes, 4).sum(0)
    pieces = exchange(pieces, ("col",), sizes, 5).sum(0)
    piece = exchange(pieces, ("dp",), sizes, 6).sum(0)
    block = exchange(piece, ("row", "col"), sizes, 7, gather=True)
    return block.reshape(group * piece_rows, lanes)[:block_rows].reshape((block_rows,) + shape[1:])


def solution(mesh):
    placed = (
        P("dp", "row", "col", None),
        P("dp", "row", "col", None),
        P("dp", "row", "col", None),
        P(),
        P(),
    )
    return jax.shard_map(
        on_device,
        mesh=mesh,
        in_specs=placed,
        out_specs=(P("dp", None, None), P("dp", None, None)),
        check_vma=False,
    )
```

```python
import functools
import math

import jax
import jax.numpy as jnp
from jax import lax
from jax.experimental import pallas as pl
from jax.experimental.pallas import tpu as pltpu
from jax.sharding import PartitionSpec as P


def member_coords(j, axes, sizes):
    coords = {}
    for axis in reversed(axes):
        coords[axis] = lax.rem(j, sizes[axis])
        j = j // sizes[axis]
    return coords


def exchange_kernel(x_ref, o_ref, send_sem, recv_sem, local_sem, *, axes, sizes, gather, chunks):
    n = math.prod(sizes[a] for a in axes)
    me = 0
    for axis in axes:
        me = me * sizes[axis] + lax.axis_index(axis)
    step = o_ref.shape[1] // chunks
    barrier = pltpu.get_barrier_semaphore()
    for s in range(1, n):
        peer = member_coords(lax.rem(me + s, n), axes, sizes)
        pl.semaphore_signal(barrier, inc=1, device_id=peer, device_id_type=pl.DeviceIdType.MESH)
    pl.semaphore_wait(barrier, n - 1)

    def source(index, part):
        rows = pl.ds(part * step, step)
        return x_ref.at[rows] if gather else x_ref.at[index, rows]

    copies = []
    for s in range(1, n):
        dst = lax.rem(me + s, n)
        for part in range(chunks):
            copy = pltpu.make_async_remote_copy(
                src_ref=source(dst, part),
                dst_ref=o_ref.at[me, pl.ds(part * step, step)],
                send_sem=send_sem.at[s - 1, part],
                recv_sem=recv_sem.at[s - 1, part],
                device_id=member_coords(dst, axes, sizes),
                device_id_type=pl.DeviceIdType.MESH,
            )
            copy.start()
            copies.append(copy)
    local = pltpu.make_async_copy(x_ref if gather else x_ref.at[me], o_ref.at[me], local_sem)
    local.start()
    for copy in copies:
        copy.wait_send()
        copy.wait_recv()
    local.wait()


def exchange(x, axes, sizes, cid, gather=False):
    n = math.prod(sizes[a] for a in axes)
    slab = x.shape if gather else x.shape[1:]
    slab_bytes = math.prod(slab) * x.dtype.itemsize
    chunks = 1
    while chunks < 8 and slab[0] % (chunks * 2) == 0 and slab_bytes // (chunks * 2) >= 96 * 1024:
        chunks *= 2
    return pl.pallas_call(
        functools.partial(exchange_kernel, axes=axes, sizes=sizes, gather=gather, chunks=chunks),
        out_shape=jax.ShapeDtypeStruct((n,) + slab, x.dtype),
        in_specs=[pl.BlockSpec(memory_space=pl.ANY)],
        out_specs=pl.BlockSpec(memory_space=pl.ANY),
        scratch_shapes=[
            pltpu.SemaphoreType.DMA((max(n - 1, 1), chunks)),
            pltpu.SemaphoreType.DMA((max(n - 1, 1), chunks)),
            pltpu.SemaphoreType.DMA,
        ],
        compiler_params=pltpu.CompilerParams(collective_id=cid, has_side_effects=True),
    )(x)


def padded_2(value, sides, width):
    for axis, dim in sides:
        size, length = (lax.axis_size(axis), value.shape[dim])
        up = [(i, (i + 1) % size) for i in range(size - 1)]
        down = [(j, i) for i, j in up]
        last = lax.slice_in_dim(value, length - width, length, axis=dim)
        leading = lax.slice_in_dim(value, 0, width, axis=dim)
        before = lax.ppermute(last, axis, up)
        after = lax.ppermute(leading, axis, down)
        value = jnp.concatenate([before, value, after], axis=dim)
    return value


def silu_slope(pre_float):
    sigma = jax.nn.sigmoid(pre_float)
    return sigma * (1.0 + pre_float * (1.0 - sigma))


def contract_first(left, right, exact):
    if exact:
        return lax.dot_general(
            left,
            right,
            (((0,), (0,)), ((), ())),
            precision=lax.Precision.HIGHEST,
            preferred_element_type=jnp.float32,
        )
    return lax.dot_general(
        left, right, (((0,), (0,)), ((), ())), preferred_element_type=jnp.float32
    )


def tap_window(padded, shift_row, shift_col, height, breadth):
    return padded[
        1 + shift_row : 1 + shift_row + height, 1 + shift_col : 1 + shift_col + breadth, :
    ].reshape(height * breadth, padded.shape[2])


def column_terms(moments, q_prev):
    return jnp.stack(
        [contract_first(moments[layer], q_prev[:, layer, :], True) for layer in range(2)], axis=1
    )


def row_terms(moments, ortho_basis):
    return jnp.stack(
        [
            jnp.dot(
                moments[layer],
                ortho_basis[:, layer, :],
                precision=lax.Precision.HIGHEST,
                preferred_element_type=jnp.float32,
            )
            for layer in range(2)
        ],
        axis=1,
    )


def gram_of(power_raw):
    return jnp.einsum(
        "mqn,mqg->qng",
        power_raw,
        power_raw,
        precision=lax.Precision.HIGHEST,
        preferred_element_type=jnp.float32,
    )


def orthonormal(power_raw, gram_matrix):
    bases = []
    for layer in range(2):
        lower = jnp.linalg.cholesky(gram_matrix[layer])
        bases.append(
            lax.linalg.triangular_solve(
                lower, power_raw[:, layer, :], left_side=False, lower=True, transpose_a=True
            )
        )
    return jnp.stack(bases, axis=1)


def on_device(x_input, pre_act, out_grad, conv_weight, q_prev):
    height, breadth, channels = (x_input.shape[1], x_input.shape[2], x_input.shape[3])
    pixels = height * breadth
    input_tile = x_input.reshape(height, breadth, channels)
    grad_tile = out_grad.reshape(height, breadth, channels)
    pre_float = pre_act.reshape(pixels, channels).astype(jnp.float32)
    hidden_flat = jax.nn.silu(pre_float).astype(jnp.bfloat16)
    grad_pad = padded_2(grad_tile, (("row", 0), ("col", 1)), 1)
    back_grad = jnp.zeros((pixels, channels), jnp.float32)
    second_taps = []
    for shift_row in (-1, 0, 1):
        for shift_col in (-1, 0, 1):
            window = tap_window(grad_pad, -shift_row, -shift_col, height, breadth)
            back_grad = back_grad + lax.dot_general(
                window,
                conv_weight[shift_row + 1, shift_col + 1],
                (((1,), (1,)), ((), ())),
                preferred_element_type=jnp.float32,
            )
            second_taps.append(contract_first(hidden_flat, window, False))
    pre_grad = (back_grad * silu_slope(pre_float)).astype(jnp.bfloat16)
    first_taps = []
    deriv_pad = padded_2(pre_grad.reshape(height, breadth, channels), (("row", 0), ("col", 1)), 1)
    input_flat = input_tile.reshape(pixels, channels)
    for shift_row in (-1, 0, 1):
        for shift_col in (-1, 0, 1):
            first_taps.append(
                contract_first(
                    input_flat,
                    tap_window(deriv_pad, -shift_row, -shift_col, height, breadth),
                    False,
                )
            )
    moments = jnp.stack(
        [
            jnp.stack(first_taps).reshape(9 * channels, channels),
            jnp.stack(second_taps).reshape(9 * channels, channels),
        ]
    )
    sizes = {axis: lax.axis_size(axis) for axis in ("dp", "row", "col")}
    power_raw = all_sum_small(column_terms(moments, q_prev), sizes)
    ortho_basis = orthonormal(power_raw, gram_of(power_raw))
    basis_count = channels // sizes["dp"]
    basis_out = lax.dynamic_slice_in_dim(ortho_basis, lax.axis_index("dp") * basis_count, basis_count, 0)
    factor_out = block_sum(row_terms(moments, ortho_basis), sizes)
    return (basis_out, factor_out)


def all_sum_small(value, sizes):
    shape = value.shape
    rows, group = shape[0], sizes["row"] * sizes["col"]
    flat = value.reshape(rows, -1)
    part = exchange(flat.reshape(group, rows // group, -1), ("row", "col"), sizes, 0).sum(0)
    piece = part.reshape(sizes["dp"], -1, 64)
    piece = exchange(piece, ("dp",), sizes, 1).sum(0)
    part = exchange(piece, ("dp",), sizes, 2, gather=True).reshape(part.shape)
    flat = exchange(part, ("row", "col"), sizes, 3, gather=True).reshape(flat.shape)
    return flat.reshape(shape)


def block_sum(value, sizes):
    shape = value.shape
    blocks, group = sizes["dp"], sizes["row"] * sizes["col"]
    block_rows = shape[0] // blocks
    piece_rows = -(-block_rows // (group * 8)) * 8
    lanes = math.prod(shape[1:])
    padded = jnp.pad(value.reshape(blocks, block_rows, lanes), ((0, 0), (0, piece_rows * group - block_rows), (0, 0)))
    pieces = padded.reshape(blocks, sizes["row"], sizes["col"], piece_rows, lanes).transpose(1, 2, 0, 3, 4)
    pieces = exchange(pieces, ("row",), sizes, 4).sum(0)
    pieces = exchange(pieces, ("col",), sizes, 5).sum(0)
    piece = exchange(pieces, ("dp",), sizes, 6).sum(0)
    block = exchange(piece, ("row", "col"), sizes, 7, gather=True)
    return block.reshape(group * piece_rows, lanes)[:block_rows].reshape((block_rows,) + shape[1:])


def solution(mesh):
    placed = (
        P("dp", "row", "col", None),
        P("dp", "row", "col", None),
        P("dp", "row", "col", None),
        P(),
        P(),
    )
    return jax.shard_map(
        on_device,
        mesh=mesh,
        in_specs=placed,
        out_specs=(P("dp", None, None), P("dp", None, None)),
        check_vma=False,
    )
```

```python
import functools
import math

import jax
import jax.numpy as jnp
from jax import lax
from jax.experimental import pallas as pl
from jax.experimental.pallas import tpu as pltpu
from jax.sharding import PartitionSpec as P


def member_coords(j, axes, sizes):
    coords = {}
    for axis in reversed(axes):
        coords[axis] = lax.rem(j, sizes[axis])
        j = j // sizes[axis]
    return coords


def exchange_kernel(x_ref, o_ref, send_sem, recv_sem, local_sem, *, axes, sizes, gather, chunks):
    n = math.prod(sizes[a] for a in axes)
    me = 0
    for axis in axes:
        me = me * sizes[axis] + lax.axis_index(axis)
    step = o_ref.shape[1] // chunks
    barrier = pltpu.get_barrier_semaphore()
    for s in range(1, n):
        peer = member_coords(lax.rem(me + s, n), axes, sizes)
        pl.semaphore_signal(barrier, inc=1, device_id=peer, device_id_type=pl.DeviceIdType.MESH)
    pl.semaphore_wait(barrier, n - 1)

    def source(index, part):
        rows = pl.ds(part * step, step)
        return x_ref.at[rows] if gather else x_ref.at[index, rows]

    copies = []
    for s in range(1, n):
        dst = lax.rem(me + s, n)
        for part in range(chunks):
            copy = pltpu.make_async_remote_copy(
                src_ref=source(dst, part),
                dst_ref=o_ref.at[me, pl.ds(part * step, step)],
                send_sem=send_sem.at[s - 1, part],
                recv_sem=recv_sem.at[s - 1, part],
                device_id=member_coords(dst, axes, sizes),
                device_id_type=pl.DeviceIdType.MESH,
            )
            copy.start()
            copies.append(copy)
    local = pltpu.make_async_copy(x_ref if gather else x_ref.at[me], o_ref.at[me], local_sem)
    local.start()
    for copy in copies:
        copy.wait_send()
        copy.wait_recv()
    local.wait()


def exchange(x, axes, sizes, cid, gather=False):
    n = math.prod(sizes[a] for a in axes)
    slab = x.shape if gather else x.shape[1:]
    slab_bytes = math.prod(slab) * x.dtype.itemsize
    chunks = 1
    while chunks < 8 and slab[0] % (chunks * 2) == 0 and slab_bytes // (chunks * 2) >= 96 * 1024:
        chunks *= 2
    return pl.pallas_call(
        functools.partial(exchange_kernel, axes=axes, sizes=sizes, gather=gather, chunks=chunks),
        out_shape=jax.ShapeDtypeStruct((n,) + slab, x.dtype),
        in_specs=[pl.BlockSpec(memory_space=pl.ANY)],
        out_specs=pl.BlockSpec(memory_space=pl.ANY),
        scratch_shapes=[
            pltpu.SemaphoreType.DMA((max(n - 1, 1), chunks)),
            pltpu.SemaphoreType.DMA((max(n - 1, 1), chunks)),
            pltpu.SemaphoreType.DMA,
        ],
        compiler_params=pltpu.CompilerParams(collective_id=cid, has_side_effects=True),
    )(x)


def padded_2(value, sides, width):
    for axis, dim in sides:
        size, length = (lax.axis_size(axis), value.shape[dim])
        up = [(i, (i + 1) % size) for i in range(size - 1)]
        down = [(j, i) for i, j in up]
        last = lax.slice_in_dim(value, length - width, length, axis=dim)
        leading = lax.slice_in_dim(value, 0, width, axis=dim)
        before = lax.ppermute(last, axis, up)
        after = lax.ppermute(leading, axis, down)
        value = jnp.concatenate([before, value, after], axis=dim)
    return value


def silu_slope(pre_float):
    sigma = jax.nn.sigmoid(pre_float)
    return sigma * (1.0 + pre_float * (1.0 - sigma))


def exact_dot(left, right, contract):
    return lax.dot_general(
        left.astype(jnp.float32),
        right.astype(jnp.float32),
        (contract, ((), ())),
        precision=lax.Precision.HIGHEST,
        preferred_element_type=jnp.float32,
    )


TAPS = [(a, b) for a in (-1, 0, 1) for b in (-1, 0, 1)]


def on_device(x_input, pre_act, out_grad, conv_weight, q_prev, sizes):
    height, breadth, channels = (x_input.shape[1], x_input.shape[2], x_input.shape[3])
    pixels = height * breadth
    rank = q_prev.shape[2]
    taps = len(TAPS)
    sides = (("row", 0), ("col", 1))
    pre_float = pre_act.reshape(pixels, channels).astype(jnp.float32)
    hidden = jax.nn.silu(pre_float).astype(jnp.bfloat16)
    grad_pad = padded_2(out_grad.reshape(height, breadth, channels), sides, 1)
    input_pad = padded_2(x_input.reshape(height, breadth, channels), sides, 1)
    back_grad = jnp.zeros((pixels, channels), jnp.float32)
    for a, b in TAPS:
        window = grad_pad[1 - a : 1 - a + height, 1 - b : 1 - b + breadth].reshape(pixels, channels)
        back_grad = back_grad + lax.dot_general(
            window, conv_weight[a + 1, b + 1], (((1,), (1,)), ((), ())), preferred_element_type=jnp.float32
        )
    pre_grad = (back_grad * silu_slope(pre_float)).astype(jnp.bfloat16)

    grid = (height + 2, breadth + 2)
    grad_flat = grad_pad.reshape(-1, channels)
    input_flat = input_pad.reshape(-1, channels)
    q_taps = q_prev.reshape(taps, channels, 2, rank).transpose(2, 1, 0, 3).reshape(2, channels, taps * rank)

    first_terms = exact_dot(input_flat, q_taps[0], ((1,), (0,))).reshape(grid + (taps, rank))
    first_sum = sum(
        first_terms[1 + a : 1 + a + height, 1 + b : 1 + b + breadth, k] for k, (a, b) in enumerate(TAPS)
    ).reshape(pixels, rank)
    first_raw = exact_dot(pre_grad, first_sum, ((0,), (0,)))
    second_terms = exact_dot(hidden, q_taps[1], ((1,), (0,))).reshape(height, breadth, taps, rank)
    second_sum = sum(
        jnp.pad(second_terms[:, :, k], ((1 - a, 1 + a), (1 - b, 1 + b), (0, 0))) for k, (a, b) in enumerate(TAPS)
    ).reshape(-1, rank)
    second_raw = exact_dot(grad_flat, second_sum, ((0,), (0,)))

    power_raw = all_sum_small(jnp.stack([first_raw, second_raw], axis=1), sizes)

    first_image = exact_dot(pre_grad, power_raw[:, 0], ((1,), (0,))).reshape(height, breadth, rank)
    first_spread = jnp.concatenate(
        [
            jnp.pad(first_image, ((1 + a, 1 - a), (1 + b, 1 - b), (0, 0))).reshape(-1, rank)
            for a, b in TAPS
        ],
        axis=1,
    )
    first_rows = exact_dot(input_flat, first_spread, ((0,), (0,)))
    second_image = exact_dot(grad_flat, power_raw[:, 1], ((1,), (0,))).reshape(grid + (rank,))
    second_spread = jnp.concatenate(
        [
            second_image[1 - a : 1 - a + height, 1 - b : 1 - b + breadth].reshape(pixels, rank)
            for a, b in TAPS
        ],
        axis=1,
    )
    second_rows = exact_dot(hidden, second_spread, ((0,), (0,)))
    rows = jnp.stack([first_rows, second_rows]).reshape(2, channels, taps, rank)
    rows = rows.transpose(2, 1, 0, 3).reshape(taps * channels, 2, rank)
    row_block = block_sum(rows, sizes)

    gram = jnp.einsum(
        "mqn,mqg->qng", power_raw, power_raw, precision=lax.Precision.HIGHEST, preferred_element_type=jnp.float32
    )
    lower = jnp.linalg.cholesky(gram)
    basis_count = channels // sizes["dp"]
    raw_part = lax.dynamic_slice_in_dim(power_raw, lax.axis_index("dp") * basis_count, basis_count, 0)
    basis_out = lax.linalg.triangular_solve(
        lower, raw_part.transpose(1, 0, 2), left_side=False, lower=True, transpose_a=True
    ).transpose(1, 0, 2)
    factor_out = lax.linalg.triangular_solve(
        lower, row_block.transpose(1, 0, 2), left_side=False, lower=True, transpose_a=True
    ).transpose(1, 0, 2)
    return (basis_out, factor_out)


def all_sum_small(value, sizes):
    shape = value.shape
    rows, group = shape[0], sizes["row"] * sizes["col"]
    flat = value.reshape(rows, -1)
    part = exchange(flat.reshape(group, rows // group, -1), ("row", "col"), sizes, 0).sum(0)
    piece = part.reshape(sizes["dp"], -1, 64)
    piece = exchange(piece, ("dp",), sizes, 1).sum(0)
    part = exchange(piece, ("dp",), sizes, 2, gather=True).reshape(part.shape)
    flat = exchange(part, ("row", "col"), sizes, 3, gather=True).reshape(flat.shape)
    return flat.reshape(shape)


def block_sum(value, sizes):
    shape = value.shape
    blocks, group = sizes["dp"], sizes["row"] * sizes["col"]
    block_rows = shape[0] // blocks
    piece_rows = -(-block_rows // (group * 8)) * 8
    lanes = math.prod(shape[1:])
    padded = jnp.pad(value.reshape(blocks, block_rows, lanes), ((0, 0), (0, piece_rows * group - block_rows), (0, 0)))
    pieces = padded.reshape(blocks, sizes["row"], sizes["col"], piece_rows, lanes).transpose(1, 2, 0, 3, 4)
    pieces = exchange(pieces, ("row",), sizes, 4).sum(0)
    pieces = exchange(pieces, ("col",), sizes, 5).sum(0)
    piece = exchange(pieces, ("dp",), sizes, 6).sum(0)
    block = exchange(piece, ("row", "col"), sizes, 7, gather=True)
    return block.reshape(group * piece_rows, lanes)[:block_rows].reshape((block_rows,) + shape[1:])


def solution(mesh):
    placed = (
        P("dp", "row", "col", None),
        P("dp", "row", "col", None),
        P("dp", "row", "col", None),
        P(),
        P(),
    )
    sizes = dict(mesh.shape)
    return jax.shard_map(
        functools.partial(on_device, sizes=sizes),
        mesh=mesh,
        in_specs=placed,
        out_specs=(P("dp", None, None), P("dp", None, None)),
        check_vma=False,
    )
```

```python
import functools
import math

import jax
import jax.numpy as jnp
from jax import lax
from jax.experimental import pallas as pl
from jax.experimental.pallas import tpu as pltpu
from jax.sharding import PartitionSpec as P


def member_coords(j, axes, sizes):
    coords = {}
    for axis in reversed(axes):
        coords[axis] = lax.rem(j, sizes[axis])
        j = j // sizes[axis]
    return coords


def exchange_kernel(*refs, jobs, sizes):
    count = len(jobs)
    x_refs, o_refs = refs[:count], refs[count : 2 * count]
    sems = refs[2 * count :]
    barrier = pltpu.get_barrier_semaphore()
    plans = []
    total = 0
    for axes, gather in jobs:
        n = math.prod(sizes[a] for a in axes)
        me = 0
        for axis in axes:
            me = me * sizes[axis] + lax.axis_index(axis)
        for s in range(1, n):
            peer = member_coords(lax.rem(me + s, n), axes, sizes)
            pl.semaphore_signal(barrier, inc=1, device_id=peer, device_id_type=pl.DeviceIdType.MESH)
        total += n - 1
        plans.append((n, me))
    pl.semaphore_wait(barrier, total)
    copies, locals_ = [], []
    for job, ((axes, gather), (n, me)) in enumerate(zip(jobs, plans)):
        x_ref, o_ref = x_refs[job], o_refs[job]
        send_sem, recv_sem, local_sem = sems[3 * job : 3 * job + 3]
        for s in range(1, n):
            dst = lax.rem(me + s, n)
            copy = pltpu.make_async_remote_copy(
                src_ref=x_ref if gather else x_ref.at[dst],
                dst_ref=o_ref.at[me],
                send_sem=send_sem.at[s - 1],
                recv_sem=recv_sem.at[s - 1],
                device_id=member_coords(dst, axes, sizes),
                device_id_type=pl.DeviceIdType.MESH,
            )
            copy.start()
            copies.append(copy)
        local = pltpu.make_async_copy(x_ref if gather else x_ref.at[me], o_ref.at[me], local_sem)
        local.start()
        locals_.append(local)
    for copy in copies:
        copy.wait_send()
        copy.wait_recv()
    for local in locals_:
        local.wait()


def exchange_many(items, sizes, cid):
    jobs, shapes, scratch = [], [], []
    for x, axes, gather in items:
        n = math.prod(sizes[a] for a in axes)
        slab = x.shape if gather else x.shape[1:]
        jobs.append((axes, gather))
        shapes.append(jax.ShapeDtypeStruct((n,) + slab, x.dtype))
        scratch += [
            pltpu.SemaphoreType.DMA((max(n - 1, 1),)),
            pltpu.SemaphoreType.DMA((max(n - 1, 1),)),
            pltpu.SemaphoreType.DMA,
        ]
    return pl.pallas_call(
        functools.partial(exchange_kernel, jobs=tuple(jobs), sizes=sizes),
        out_shape=tuple(shapes),
        in_specs=[pl.BlockSpec(memory_space=pl.ANY)] * len(items),
        out_specs=tuple(pl.BlockSpec(memory_space=pl.ANY) for _ in items),
        scratch_shapes=scratch,
        compiler_params=pltpu.CompilerParams(collective_id=cid, has_side_effects=True),
    )(*[x for x, _, _ in items])


def exchange(x, axes, sizes, cid, gather=False):
    return exchange_many([(x, axes, gather)], sizes, cid)[0]


def padded_2(value, sides, width):
    for axis, dim in sides:
        size, length = (lax.axis_size(axis), value.shape[dim])
        up = [(i, (i + 1) % size) for i in range(size - 1)]
        down = [(j, i) for i, j in up]
        last = lax.slice_in_dim(value, length - width, length, axis=dim)
        leading = lax.slice_in_dim(value, 0, width, axis=dim)
        before = lax.ppermute(last, axis, up)
        after = lax.ppermute(leading, axis, down)
        value = jnp.concatenate([before, value, after], axis=dim)
    return value


def silu_slope(pre_float):
    sigma = jax.nn.sigmoid(pre_float)
    return sigma * (1.0 + pre_float * (1.0 - sigma))


def exact_dot(left, right, contract):
    return lax.dot_general(
        left.astype(jnp.float32),
        right.astype(jnp.float32),
        (contract, ((), ())),
        precision=lax.Precision.HIGHEST,
        preferred_element_type=jnp.float32,
    )


TAPS = [(a, b) for a in (-1, 0, 1) for b in (-1, 0, 1)]


def on_device(x_input, pre_act, out_grad, conv_weight, q_prev, sizes):
    height, breadth, channels = (x_input.shape[1], x_input.shape[2], x_input.shape[3])
    pixels = height * breadth
    rank = q_prev.shape[2]
    taps = len(TAPS)
    sides = (("row", 0), ("col", 1))
    pre_float = pre_act.reshape(pixels, channels).astype(jnp.float32)
    hidden = jax.nn.silu(pre_float).astype(jnp.bfloat16)
    grad_pad = padded_2(out_grad.reshape(height, breadth, channels), sides, 1)
    input_pad = padded_2(x_input.reshape(height, breadth, channels), sides, 1)
    back_grad = jnp.zeros((pixels, channels), jnp.float32)
    for a, b in TAPS:
        window = grad_pad[1 - a : 1 - a + height, 1 - b : 1 - b + breadth].reshape(pixels, channels)
        back_grad = back_grad + lax.dot_general(
            window, conv_weight[a + 1, b + 1], (((1,), (1,)), ((), ())), preferred_element_type=jnp.float32
        )
    pre_grad = (back_grad * silu_slope(pre_float)).astype(jnp.bfloat16)

    grid = (height + 2, breadth + 2)
    grad_flat = grad_pad.reshape(-1, channels)
    input_flat = input_pad.reshape(-1, channels)
    q_taps = q_prev.reshape(taps, channels, 2, rank).transpose(2, 1, 0, 3).reshape(2, channels, taps * rank)

    first_terms = exact_dot(input_flat, q_taps[0], ((1,), (0,))).reshape(grid + (taps, rank))
    first_sum = sum(
        first_terms[1 + a : 1 + a + height, 1 + b : 1 + b + breadth, k] for k, (a, b) in enumerate(TAPS)
    ).reshape(pixels, rank)
    first_raw = exact_dot(pre_grad, first_sum, ((0,), (0,)))
    second_terms = exact_dot(hidden, q_taps[1], ((1,), (0,))).reshape(height, breadth, taps, rank)
    second_sum = sum(
        jnp.pad(second_terms[:, :, k], ((1 - a, 1 + a), (1 - b, 1 + b), (0, 0))) for k, (a, b) in enumerate(TAPS)
    ).reshape(-1, rank)
    second_raw = exact_dot(grad_flat, second_sum, ((0,), (0,)))

    power_raw = all_sum_small(jnp.stack([first_raw, second_raw], axis=1), sizes)

    first_image = exact_dot(pre_grad, power_raw[:, 0], ((1,), (0,))).reshape(height, breadth, rank)
    first_spread = jnp.concatenate(
        [
            jnp.pad(first_image, ((1 + a, 1 - a), (1 + b, 1 - b), (0, 0))).reshape(-1, rank)
            for a, b in TAPS
        ],
        axis=1,
    )
    first_rows = exact_dot(input_flat, first_spread, ((0,), (0,)))
    second_image = exact_dot(grad_flat, power_raw[:, 1], ((1,), (0,))).reshape(grid + (rank,))
    second_spread = jnp.concatenate(
        [
            second_image[1 - a : 1 - a + height, 1 - b : 1 - b + breadth].reshape(pixels, rank)
            for a, b in TAPS
        ],
        axis=1,
    )
    second_rows = exact_dot(hidden, second_spread, ((0,), (0,)))
    rows = jnp.stack([first_rows, second_rows]).reshape(2, channels, taps, rank)
    rows = rows.transpose(2, 1, 0, 3).reshape(taps * channels, 2, rank)
    row_block = block_sum(rows, sizes)

    gram = jnp.einsum(
        "mqn,mqg->qng", power_raw, power_raw, precision=lax.Precision.HIGHEST, preferred_element_type=jnp.float32
    )
    lower = jnp.linalg.cholesky(gram)
    basis_count = channels // sizes["dp"]
    raw_part = lax.dynamic_slice_in_dim(power_raw, lax.axis_index("dp") * basis_count, basis_count, 0)
    basis_out = lax.linalg.triangular_solve(
        lower, raw_part.transpose(1, 0, 2), left_side=False, lower=True, transpose_a=True
    ).transpose(1, 0, 2)
    factor_out = lax.linalg.triangular_solve(
        lower, row_block.transpose(1, 0, 2), left_side=False, lower=True, transpose_a=True
    ).transpose(1, 0, 2)
    return (basis_out, factor_out)


def all_sum_small(value, sizes):
    shape = value.shape
    rows, group = shape[0], sizes["row"] * sizes["col"]
    flat = value.reshape(rows, -1)
    part = exchange(flat.reshape(group, rows // group, -1), ("row", "col"), sizes, 0).sum(0)
    piece = part.reshape(sizes["dp"], -1, 64)
    piece = exchange(piece, ("dp",), sizes, 1).sum(0)
    part = exchange(piece, ("dp",), sizes, 2, gather=True).reshape(part.shape)
    flat = exchange(part, ("row", "col"), sizes, 3, gather=True).reshape(flat.shape)
    return flat.reshape(shape)


def block_sum(value, sizes):
    shape = value.shape
    blocks, rows_n, cols_n = sizes["dp"], sizes["row"], sizes["col"]
    group = rows_n * cols_n
    block_rows = shape[0] // blocks
    piece_rows = -(-block_rows // (group * 8)) * 8
    lanes = math.prod(shape[1:])
    padded = jnp.pad(value.reshape(blocks, block_rows, lanes), ((0, 0), (0, piece_rows * group - block_rows), (0, 0)))
    pieces = padded.reshape(blocks, rows_n, cols_n, piece_rows, lanes)
    half = blocks // 2
    first = pieces[:half].transpose(1, 2, 0, 3, 4)
    second = pieces[half:].transpose(2, 1, 0, 3, 4)
    first, second = exchange_many([(first, ("row",), False), (second, ("col",), False)], sizes, 4)
    first, second = exchange_many(
        [(first.sum(0), ("col",), False), (second.sum(0), ("row",), False)], sizes, 5
    )
    pieces = jnp.concatenate([first.sum(0), second.sum(0)])
    piece = exchange(pieces, ("dp",), sizes, 6).sum(0)
    block = exchange(piece, ("row", "col"), sizes, 7, gather=True)
    return block.reshape(group * piece_rows, lanes)[:block_rows].reshape((block_rows,) + shape[1:])


def solution(mesh):
    placed = (
        P("dp", "row", "col", None),
        P("dp", "row", "col", None),
        P("dp", "row", "col", None),
        P(),
        P(),
    )
    sizes = dict(mesh.shape)
    return jax.shard_map(
        functools.partial(on_device, sizes=sizes),
        mesh=mesh,
        in_specs=placed,
        out_specs=(P("dp", None, None), P("dp", None, None)),
        check_vma=False,
    )
```

```python
import functools
import math

import jax
import jax.numpy as jnp
from jax import lax
from jax.experimental import pallas as pl
from jax.experimental.pallas import tpu as pltpu
from jax.sharding import PartitionSpec as P


def member_coords(j, axes, sizes):
    coords = {}
    for axis in reversed(axes):
        coords[axis] = lax.rem(j, sizes[axis])
        j = j // sizes[axis]
    return coords


def exchange_kernel(*refs, jobs, sizes):
    count = len(jobs)
    x_refs, o_refs = refs[:count], refs[count : 2 * count]
    sems = refs[2 * count :]
    barrier = pltpu.get_barrier_semaphore()
    plans = []
    total = 0
    for axes, gather in jobs:
        n = math.prod(sizes[a] for a in axes)
        me = 0
        for axis in axes:
            me = me * sizes[axis] + lax.axis_index(axis)
        for s in range(1, n):
            peer = member_coords(lax.rem(me + s, n), axes, sizes)
            pl.semaphore_signal(barrier, inc=1, device_id=peer, device_id_type=pl.DeviceIdType.MESH)
        total += n - 1
        plans.append((n, me))
    pl.semaphore_wait(barrier, total)
    copies, locals_ = [], []
    for job, ((axes, gather), (n, me)) in enumerate(zip(jobs, plans)):
        x_ref, o_ref = x_refs[job], o_refs[job]
        send_sem, recv_sem, local_sem = sems[3 * job : 3 * job + 3]
        for s in range(1, n):
            dst = lax.rem(me + s, n)
            copy = pltpu.make_async_remote_copy(
                src_ref=x_ref if gather else x_ref.at[dst],
                dst_ref=o_ref.at[me],
                send_sem=send_sem.at[s - 1],
                recv_sem=recv_sem.at[s - 1],
                device_id=member_coords(dst, axes, sizes),
                device_id_type=pl.DeviceIdType.MESH,
            )
            copy.start()
            copies.append(copy)
        local = pltpu.make_async_copy(x_ref if gather else x_ref.at[me], o_ref.at[me], local_sem)
        local.start()
        locals_.append(local)
    for copy in copies:
        copy.wait_send()
        copy.wait_recv()
    for local in locals_:
        local.wait()


def exchange_many(items, sizes, cid):
    jobs, shapes, scratch = [], [], []
    for x, axes, gather in items:
        n = math.prod(sizes[a] for a in axes)
        slab = x.shape if gather else x.shape[1:]
        jobs.append((axes, gather))
        shapes.append(jax.ShapeDtypeStruct((n,) + slab, x.dtype))
        scratch += [
            pltpu.SemaphoreType.DMA((max(n - 1, 1),)),
            pltpu.SemaphoreType.DMA((max(n - 1, 1),)),
            pltpu.SemaphoreType.DMA,
        ]
    return pl.pallas_call(
        functools.partial(exchange_kernel, jobs=tuple(jobs), sizes=sizes),
        out_shape=tuple(shapes),
        in_specs=[pl.BlockSpec(memory_space=pltpu.VMEM)] * len(items),
        out_specs=tuple(pl.BlockSpec(memory_space=pltpu.VMEM) for _ in items),
        scratch_shapes=scratch,
        compiler_params=pltpu.CompilerParams(
            collective_id=cid, has_side_effects=True, vmem_limit_bytes=48 * 1024 * 1024
        ),
    )(*[x for x, _, _ in items])


def exchange(x, axes, sizes, cid, gather=False):
    return exchange_many([(x, axes, gather)], sizes, cid)[0]


def padded_2(value, sides, width):
    for axis, dim in sides:
        size, length = (lax.axis_size(axis), value.shape[dim])
        up = [(i, (i + 1) % size) for i in range(size - 1)]
        down = [(j, i) for i, j in up]
        last = lax.slice_in_dim(value, length - width, length, axis=dim)
        leading = lax.slice_in_dim(value, 0, width, axis=dim)
        before = lax.ppermute(last, axis, up)
        after = lax.ppermute(leading, axis, down)
        value = jnp.concatenate([before, value, after], axis=dim)
    return value


def silu_slope(pre_float):
    sigma = jax.nn.sigmoid(pre_float)
    return sigma * (1.0 + pre_float * (1.0 - sigma))


def exact_dot(left, right, contract):
    return lax.dot_general(
        left.astype(jnp.float32),
        right.astype(jnp.float32),
        (contract, ((), ())),
        precision=lax.Precision.HIGHEST,
        preferred_element_type=jnp.float32,
    )


TAPS = [(a, b) for a in (-1, 0, 1) for b in (-1, 0, 1)]


def on_device(x_input, pre_act, out_grad, conv_weight, q_prev, sizes):
    height, breadth, channels = (x_input.shape[1], x_input.shape[2], x_input.shape[3])
    pixels = height * breadth
    rank = q_prev.shape[2]
    taps = len(TAPS)
    sides = (("row", 0), ("col", 1))
    pre_float = pre_act.reshape(pixels, channels).astype(jnp.float32)
    hidden = jax.nn.silu(pre_float).astype(jnp.bfloat16)
    grad_pad = padded_2(out_grad.reshape(height, breadth, channels), sides, 1)
    input_pad = padded_2(x_input.reshape(height, breadth, channels), sides, 1)
    back_grad = jnp.zeros((pixels, channels), jnp.float32)
    for a, b in TAPS:
        window = grad_pad[1 - a : 1 - a + height, 1 - b : 1 - b + breadth].reshape(pixels, channels)
        back_grad = back_grad + lax.dot_general(
            window, conv_weight[a + 1, b + 1], (((1,), (1,)), ((), ())), preferred_element_type=jnp.float32
        )
    pre_grad = (back_grad * silu_slope(pre_float)).astype(jnp.bfloat16)

    grid = (height + 2, breadth + 2)
    grad_flat = grad_pad.reshape(-1, channels)
    input_flat = input_pad.reshape(-1, channels)
    q_taps = q_prev.reshape(taps, channels, 2, rank).transpose(2, 1, 0, 3).reshape(2, channels, taps * rank)

    first_terms = exact_dot(input_flat, q_taps[0], ((1,), (0,))).reshape(grid + (taps, rank))
    first_sum = sum(
        first_terms[1 + a : 1 + a + height, 1 + b : 1 + b + breadth, k] for k, (a, b) in enumerate(TAPS)
    ).reshape(pixels, rank)
    first_raw = exact_dot(pre_grad, first_sum, ((0,), (0,)))
    second_terms = exact_dot(hidden, q_taps[1], ((1,), (0,))).reshape(height, breadth, taps, rank)
    second_sum = sum(
        jnp.pad(second_terms[:, :, k], ((1 - a, 1 + a), (1 - b, 1 + b), (0, 0))) for k, (a, b) in enumerate(TAPS)
    ).reshape(-1, rank)
    second_raw = exact_dot(grad_flat, second_sum, ((0,), (0,)))

    power_raw = all_sum_small(jnp.stack([first_raw, second_raw], axis=1), sizes)

    first_image = exact_dot(pre_grad, power_raw[:, 0], ((1,), (0,))).reshape(height, breadth, rank)
    first_spread = jnp.concatenate(
        [
            jnp.pad(first_image, ((1 + a, 1 - a), (1 + b, 1 - b), (0, 0))).reshape(-1, rank)
            for a, b in TAPS
        ],
        axis=1,
    )
    first_rows = exact_dot(input_flat, first_spread, ((0,), (0,)))
    second_image = exact_dot(grad_flat, power_raw[:, 1], ((1,), (0,))).reshape(grid + (rank,))
    second_spread = jnp.concatenate(
        [
            second_image[1 - a : 1 - a + height, 1 - b : 1 - b + breadth].reshape(pixels, rank)
            for a, b in TAPS
        ],
        axis=1,
    )
    second_rows = exact_dot(hidden, second_spread, ((0,), (0,)))
    rows = jnp.stack([first_rows, second_rows]).reshape(2, channels, taps, rank)
    rows = rows.transpose(2, 1, 0, 3).reshape(taps * channels, 2, rank)
    row_block = block_sum(rows, sizes)

    gram = jnp.einsum(
        "mqn,mqg->qng", power_raw, power_raw, precision=lax.Precision.HIGHEST, preferred_element_type=jnp.float32
    )
    lower = jnp.linalg.cholesky(gram)
    basis_count = channels // sizes["dp"]
    raw_part = lax.dynamic_slice_in_dim(power_raw, lax.axis_index("dp") * basis_count, basis_count, 0)
    basis_out = lax.linalg.triangular_solve(
        lower, raw_part.transpose(1, 0, 2), left_side=False, lower=True, transpose_a=True
    ).transpose(1, 0, 2)
    factor_out = lax.linalg.triangular_solve(
        lower, row_block.transpose(1, 0, 2), left_side=False, lower=True, transpose_a=True
    ).transpose(1, 0, 2)
    return (basis_out, factor_out)


def all_sum_small(value, sizes):
    shape = value.shape
    rows, group = shape[0], sizes["row"] * sizes["col"]
    flat = value.reshape(rows, -1)
    part = exchange(flat.reshape(group, rows // group, -1), ("row", "col"), sizes, 0).sum(0)
    piece = part.reshape(sizes["dp"], -1, 64)
    piece = exchange(piece, ("dp",), sizes, 1).sum(0)
    part = exchange(piece, ("dp",), sizes, 2, gather=True).reshape(part.shape)
    flat = exchange(part, ("row", "col"), sizes, 3, gather=True).reshape(flat.shape)
    return flat.reshape(shape)


def block_sum(value, sizes):
    shape = value.shape
    blocks, rows_n, cols_n = sizes["dp"], sizes["row"], sizes["col"]
    group = rows_n * cols_n
    block_rows = shape[0] // blocks
    piece_rows = -(-block_rows // (group * 8)) * 8
    lanes = math.prod(shape[1:])
    padded = jnp.pad(value.reshape(blocks, block_rows, lanes), ((0, 0), (0, piece_rows * group - block_rows), (0, 0)))
    pieces = padded.reshape(blocks, rows_n, cols_n, piece_rows, lanes)
    half = blocks // 2
    first = pieces[:half].transpose(1, 2, 0, 3, 4)
    second = pieces[half:].transpose(2, 1, 0, 3, 4)
    first, second = exchange_many([(first, ("row",), False), (second, ("col",), False)], sizes, 4)
    first, second = exchange_many(
        [(first.sum(0), ("col",), False), (second.sum(0), ("row",), False)], sizes, 5
    )
    pieces = jnp.concatenate([first.sum(0), second.sum(0)])
    piece = exchange(pieces, ("dp",), sizes, 6).sum(0)
    block = exchange(piece, ("row", "col"), sizes, 7, gather=True)
    return block.reshape(group * piece_rows, lanes)[:block_rows].reshape((block_rows,) + shape[1:])


def solution(mesh):
    placed = (
        P("dp", "row", "col", None),
        P("dp", "row", "col", None),
        P("dp", "row", "col", None),
        P(),
        P(),
    )
    sizes = dict(mesh.shape)
    return jax.shard_map(
        functools.partial(on_device, sizes=sizes),
        mesh=mesh,
        in_specs=placed,
        out_specs=(P("dp", None, None), P("dp", None, None)),
        check_vma=False,
    )
```

```python
import functools
import math

import jax
import jax.numpy as jnp
from jax import lax
from jax.experimental import pallas as pl
from jax.experimental.pallas import tpu as pltpu
from jax.sharding import PartitionSpec as P


def member_coords(j, axes, sizes):
    coords = {}
    for axis in reversed(axes):
        coords[axis] = lax.rem(j, sizes[axis])
        j = j // sizes[axis]
    return coords


def exchange_kernel(*refs, jobs, sizes):
    count = len(jobs)
    x_refs, o_refs = refs[:count], refs[count : 2 * count]
    sems = refs[2 * count :]
    barrier = pltpu.get_barrier_semaphore()
    plans = []
    total = 0
    for axes, gather in jobs:
        n = math.prod(sizes[a] for a in axes)
        me = 0
        for axis in axes:
            me = me * sizes[axis] + lax.axis_index(axis)
        for s in range(1, n):
            peer = member_coords(lax.rem(me + s, n), axes, sizes)
            pl.semaphore_signal(barrier, inc=1, device_id=peer, device_id_type=pl.DeviceIdType.MESH)
        total += n - 1
        plans.append((n, me))
    pl.semaphore_wait(barrier, total)
    copies, locals_ = [], []
    for job, ((axes, gather), (n, me)) in enumerate(zip(jobs, plans)):
        x_ref, o_ref = x_refs[job], o_refs[job]
        send_sem, recv_sem, local_sem = sems[3 * job : 3 * job + 3]
        for s in range(1, n):
            dst = lax.rem(me + s, n)
            copy = pltpu.make_async_remote_copy(
                src_ref=x_ref if gather else x_ref.at[dst],
                dst_ref=o_ref.at[me],
                send_sem=send_sem.at[s - 1],
                recv_sem=recv_sem.at[s - 1],
                device_id=member_coords(dst, axes, sizes),
                device_id_type=pl.DeviceIdType.MESH,
            )
            copy.start()
            copies.append(copy)
        local = pltpu.make_async_copy(x_ref if gather else x_ref.at[me], o_ref.at[me], local_sem)
        local.start()
        locals_.append(local)
    for copy in copies:
        copy.wait_send()
        copy.wait_recv()
    for local in locals_:
        local.wait()


def exchange_many(items, sizes, cid):
    jobs, shapes, scratch = [], [], []
    for x, axes, gather in items:
        n = math.prod(sizes[a] for a in axes)
        slab = x.shape if gather else x.shape[1:]
        jobs.append((axes, gather))
        shapes.append(jax.ShapeDtypeStruct((n,) + slab, x.dtype))
        scratch += [
            pltpu.SemaphoreType.DMA((max(n - 1, 1),)),
            pltpu.SemaphoreType.DMA((max(n - 1, 1),)),
            pltpu.SemaphoreType.DMA,
        ]
    return pl.pallas_call(
        functools.partial(exchange_kernel, jobs=tuple(jobs), sizes=sizes),
        out_shape=tuple(shapes),
        in_specs=[pl.BlockSpec(memory_space=pltpu.VMEM)] * len(items),
        out_specs=tuple(pl.BlockSpec(memory_space=pltpu.VMEM) for _ in items),
        scratch_shapes=scratch,
        compiler_params=pltpu.CompilerParams(
            collective_id=cid, has_side_effects=True, vmem_limit_bytes=48 * 1024 * 1024
        ),
    )(*[x for x, _, _ in items])


def exchange(x, axes, sizes, cid, gather=False):
    return exchange_many([(x, axes, gather)], sizes, cid)[0]


HALO_MOVES = ((1, 0), (-1, 0), (0, 1), (0, -1), (1, 1), (1, -1), (-1, 1), (-1, -1))


def halo_kernel(*refs, sizes):
    sends, recvs = refs[:3], refs[3:6]
    send_sem, recv_sem = refs[6:8]
    row, col = lax.axis_index("row"), lax.axis_index("col")

    def target(dr, dc):
        return {"row": lax.rem(row + dr + sizes["row"], sizes["row"]), "col": lax.rem(col + dc + sizes["col"], sizes["col"])}

    barrier = pltpu.get_barrier_semaphore()
    for dr, dc in HALO_MOVES:
        pl.semaphore_signal(barrier, inc=1, device_id=target(dr, dc), device_id_type=pl.DeviceIdType.MESH)
    pl.semaphore_wait(barrier, len(HALO_MOVES))
    copies = []
    for k, (dr, dc) in enumerate(HALO_MOVES):
        kind, slot = (0, k) if k < 2 else ((1, k - 2) if k < 4 else (2, k - 4))
        copy = pltpu.make_async_remote_copy(
            src_ref=sends[kind].at[slot],
            dst_ref=recvs[kind].at[slot],
            send_sem=send_sem.at[k],
            recv_sem=recv_sem.at[k],
            device_id=target(dr, dc),
            device_id_type=pl.DeviceIdType.MESH,
        )
        copy.start()
        copies.append(copy)
    for copy in copies:
        copy.wait_send()
        copy.wait_recv()


def padded_pair(tiles, sizes):
    rows_out = jnp.stack([tiles[:, -1], tiles[:, 0]])
    cols_out = jnp.stack([tiles[:, :, -1], tiles[:, :, 0]])
    corners_out = jnp.stack([tiles[:, -1, -1], tiles[:, -1, 0], tiles[:, 0, -1], tiles[:, 0, 0]])
    sends = (rows_out, cols_out, corners_out)
    recvs = pl.pallas_call(
        functools.partial(halo_kernel, sizes=sizes),
        out_shape=tuple(jax.ShapeDtypeStruct(x.shape, x.dtype) for x in sends),
        in_specs=[pl.BlockSpec(memory_space=pltpu.VMEM)] * 3,
        out_specs=tuple(pl.BlockSpec(memory_space=pltpu.VMEM) for _ in sends),
        scratch_shapes=[pltpu.SemaphoreType.DMA((len(HALO_MOVES),)), pltpu.SemaphoreType.DMA((len(HALO_MOVES),))],
        compiler_params=pltpu.CompilerParams(collective_id=8, has_side_effects=True),
    )(*sends)
    rows_in, cols_in, corners_in = recvs
    row, col = lax.axis_index("row"), lax.axis_index("col")
    up, down = row > 0, row < sizes["row"] - 1
    left, right = col > 0, col < sizes["col"] - 1
    zero = jnp.zeros((), tiles.dtype)
    top = jnp.where(up, rows_in[0], zero)
    bottom = jnp.where(down, rows_in[1], zero)
    west = jnp.where(left, cols_in[0], zero)
    east = jnp.where(right, cols_in[1], zero)
    top_left = jnp.where(up & left, corners_in[0], zero)
    top_right = jnp.where(up & right, corners_in[1], zero)
    bottom_left = jnp.where(down & left, corners_in[2], zero)
    bottom_right = jnp.where(down & right, corners_in[3], zero)
    first = jnp.concatenate([top_left[:, None], top, top_right[:, None]], axis=1)
    middle = jnp.concatenate([west[:, :, None], tiles, east[:, :, None]], axis=2)
    last = jnp.concatenate([bottom_left[:, None], bottom, bottom_right[:, None]], axis=1)
    return jnp.concatenate([first[:, None], middle, last[:, None]], axis=1)


def silu_slope(pre_float):
    sigma = jax.nn.sigmoid(pre_float)
    return sigma * (1.0 + pre_float * (1.0 - sigma))


def exact_dot(left, right, contract):
    return lax.dot_general(
        left.astype(jnp.float32),
        right.astype(jnp.float32),
        (contract, ((), ())),
        precision=lax.Precision.HIGHEST,
        preferred_element_type=jnp.float32,
    )


TAPS = [(a, b) for a in (-1, 0, 1) for b in (-1, 0, 1)]


def on_device(x_input, pre_act, out_grad, conv_weight, q_prev, sizes):
    height, breadth, channels = (x_input.shape[1], x_input.shape[2], x_input.shape[3])
    pixels = height * breadth
    rank = q_prev.shape[2]
    taps = len(TAPS)
    pre_float = pre_act.reshape(pixels, channels).astype(jnp.float32)
    hidden = jax.nn.silu(pre_float).astype(jnp.bfloat16)
    both_pad = padded_pair(
        jnp.stack([out_grad.reshape(height, breadth, channels), x_input.reshape(height, breadth, channels)]), sizes
    )
    grad_pad, input_pad = both_pad[0], both_pad[1]
    back_grad = jnp.zeros((pixels, channels), jnp.float32)
    for a, b in TAPS:
        window = grad_pad[1 - a : 1 - a + height, 1 - b : 1 - b + breadth].reshape(pixels, channels)
        back_grad = back_grad + lax.dot_general(
            window, conv_weight[a + 1, b + 1], (((1,), (1,)), ((), ())), preferred_element_type=jnp.float32
        )
    pre_grad = (back_grad * silu_slope(pre_float)).astype(jnp.bfloat16)

    grid = (height + 2, breadth + 2)
    grad_flat = grad_pad.reshape(-1, channels)
    input_flat = input_pad.reshape(-1, channels)
    q_taps = q_prev.reshape(taps, channels, 2, rank).transpose(2, 1, 0, 3).reshape(2, channels, taps * rank)

    first_terms = exact_dot(input_flat, q_taps[0], ((1,), (0,))).reshape(grid + (taps, rank))
    first_sum = sum(
        first_terms[1 + a : 1 + a + height, 1 + b : 1 + b + breadth, k] for k, (a, b) in enumerate(TAPS)
    ).reshape(pixels, rank)
    first_raw = exact_dot(pre_grad, first_sum, ((0,), (0,)))
    second_terms = exact_dot(hidden, q_taps[1], ((1,), (0,))).reshape(height, breadth, taps, rank)
    second_sum = sum(
        jnp.pad(second_terms[:, :, k], ((1 - a, 1 + a), (1 - b, 1 + b), (0, 0))) for k, (a, b) in enumerate(TAPS)
    ).reshape(-1, rank)
    second_raw = exact_dot(grad_flat, second_sum, ((0,), (0,)))

    power_raw = all_sum_small(jnp.stack([first_raw, second_raw], axis=1), sizes)

    first_image = exact_dot(pre_grad, power_raw[:, 0], ((1,), (0,))).reshape(height, breadth, rank)
    first_spread = jnp.concatenate(
        [
            jnp.pad(first_image, ((1 + a, 1 - a), (1 + b, 1 - b), (0, 0))).reshape(-1, rank)
            for a, b in TAPS
        ],
        axis=1,
    )
    first_rows = exact_dot(input_flat, first_spread, ((0,), (0,)))
    second_image = exact_dot(grad_flat, power_raw[:, 1], ((1,), (0,))).reshape(grid + (rank,))
    second_spread = jnp.concatenate(
        [
            second_image[1 - a : 1 - a + height, 1 - b : 1 - b + breadth].reshape(pixels, rank)
            for a, b in TAPS
        ],
        axis=1,
    )
    second_rows = exact_dot(hidden, second_spread, ((0,), (0,)))
    rows = jnp.stack([first_rows, second_rows]).reshape(2, channels, taps, rank)
    rows = rows.transpose(2, 1, 0, 3).reshape(taps * channels, 2, rank)
    row_block = block_sum(rows, sizes)

    gram = jnp.einsum(
        "mqn,mqg->qng", power_raw, power_raw, precision=lax.Precision.HIGHEST, preferred_element_type=jnp.float32
    )
    lower = jnp.linalg.cholesky(gram)
    basis_count = channels // sizes["dp"]
    raw_part = lax.dynamic_slice_in_dim(power_raw, lax.axis_index("dp") * basis_count, basis_count, 0)
    basis_out = lax.linalg.triangular_solve(
        lower, raw_part.transpose(1, 0, 2), left_side=False, lower=True, transpose_a=True
    ).transpose(1, 0, 2)
    factor_out = lax.linalg.triangular_solve(
        lower, row_block.transpose(1, 0, 2), left_side=False, lower=True, transpose_a=True
    ).transpose(1, 0, 2)
    return (basis_out, factor_out)


def all_sum_small(value, sizes):
    shape = value.shape
    rows, group = shape[0], sizes["row"] * sizes["col"]
    flat = value.reshape(rows, -1)
    part = exchange(flat.reshape(group, rows // group, -1), ("row", "col"), sizes, 0).sum(0)
    piece = part.reshape(sizes["dp"], -1, 64)
    piece = exchange(piece, ("dp",), sizes, 1).sum(0)
    part = exchange(piece, ("dp",), sizes, 2, gather=True).reshape(part.shape)
    flat = exchange(part, ("row", "col"), sizes, 3, gather=True).reshape(flat.shape)
    return flat.reshape(shape)


def block_sum(value, sizes):
    shape = value.shape
    blocks, rows_n, cols_n = sizes["dp"], sizes["row"], sizes["col"]
    group = rows_n * cols_n
    block_rows = shape[0] // blocks
    piece_rows = -(-block_rows // (group * 8)) * 8
    lanes = math.prod(shape[1:])
    padded = jnp.pad(value.reshape(blocks, block_rows, lanes), ((0, 0), (0, piece_rows * group - block_rows), (0, 0)))
    pieces = padded.reshape(blocks, rows_n, cols_n, piece_rows, lanes)
    half = blocks // 2
    first = pieces[:half].transpose(1, 2, 0, 3, 4)
    second = pieces[half:].transpose(2, 1, 0, 3, 4)
    first, second = exchange_many([(first, ("row",), False), (second, ("col",), False)], sizes, 4)
    first, second = exchange_many(
        [(first.sum(0), ("col",), False), (second.sum(0), ("row",), False)], sizes, 5
    )
    pieces = jnp.concatenate([first.sum(0), second.sum(0)])
    piece = exchange(pieces, ("dp",), sizes, 6).sum(0)
    block = exchange(piece, ("row", "col"), sizes, 7, gather=True)
    return block.reshape(group * piece_rows, lanes)[:block_rows].reshape((block_rows,) + shape[1:])


def solution(mesh):
    placed = (
        P("dp", "row", "col", None),
        P("dp", "row", "col", None),
        P("dp", "row", "col", None),
        P(),
        P(),
    )
    sizes = dict(mesh.shape)
    return jax.shard_map(
        functools.partial(on_device, sizes=sizes),
        mesh=mesh,
        in_specs=placed,
        out_specs=(P("dp", None, None), P("dp", None, None)),
        check_vma=False,
    )
```

```python
import functools
import math

import jax
import jax.numpy as jnp
from jax import lax
from jax.experimental import pallas as pl
from jax.experimental.pallas import tpu as pltpu
from jax.sharding import PartitionSpec as P


def member_coords(j, axes, sizes):
    coords = {}
    for axis in reversed(axes):
        coords[axis] = lax.rem(j, sizes[axis])
        j = j // sizes[axis]
    return coords


def exchange_kernel(*refs, jobs, sizes):
    count = len(jobs)
    x_refs, o_refs = refs[:count], refs[count : 2 * count]
    sems = refs[2 * count :]
    barrier = pltpu.get_barrier_semaphore()
    plans = []
    total = 0
    for axes, gather in jobs:
        n = math.prod(sizes[a] for a in axes)
        me = 0
        for axis in axes:
            me = me * sizes[axis] + lax.axis_index(axis)
        for s in range(1, n):
            peer = member_coords(lax.rem(me + s, n), axes, sizes)
            pl.semaphore_signal(barrier, inc=1, device_id=peer, device_id_type=pl.DeviceIdType.MESH)
        total += n - 1
        plans.append((n, me))
    pl.semaphore_wait(barrier, total)
    copies, locals_ = [], []
    for job, ((axes, gather), (n, me)) in enumerate(zip(jobs, plans)):
        x_ref, o_ref = x_refs[job], o_refs[job]
        send_sem, recv_sem, local_sem = sems[3 * job : 3 * job + 3]
        for s in range(1, n):
            dst = lax.rem(me + s, n)
            copy = pltpu.make_async_remote_copy(
                src_ref=x_ref if gather else x_ref.at[dst],
                dst_ref=o_ref.at[me],
                send_sem=send_sem.at[s - 1],
                recv_sem=recv_sem.at[s - 1],
                device_id=member_coords(dst, axes, sizes),
                device_id_type=pl.DeviceIdType.MESH,
            )
            copy.start()
            copies.append(copy)
        local = pltpu.make_async_copy(x_ref if gather else x_ref.at[me], o_ref.at[me], local_sem)
        local.start()
        locals_.append(local)
    for copy in copies:
        copy.wait_send()
        copy.wait_recv()
    for local in locals_:
        local.wait()


def exchange_many(items, sizes, cid):
    jobs, shapes, scratch = [], [], []
    for x, axes, gather in items:
        n = math.prod(sizes[a] for a in axes)
        slab = x.shape if gather else x.shape[1:]
        jobs.append((axes, gather))
        shapes.append(jax.ShapeDtypeStruct((n,) + slab, x.dtype))
        scratch += [
            pltpu.SemaphoreType.DMA((max(n - 1, 1),)),
            pltpu.SemaphoreType.DMA((max(n - 1, 1),)),
            pltpu.SemaphoreType.DMA,
        ]
    return pl.pallas_call(
        functools.partial(exchange_kernel, jobs=tuple(jobs), sizes=sizes),
        out_shape=tuple(shapes),
        in_specs=[pl.BlockSpec(memory_space=pltpu.VMEM)] * len(items),
        out_specs=tuple(pl.BlockSpec(memory_space=pltpu.VMEM) for _ in items),
        scratch_shapes=scratch,
        compiler_params=pltpu.CompilerParams(
            collective_id=cid, has_side_effects=True, vmem_limit_bytes=48 * 1024 * 1024
        ),
    )(*[x for x, _, _ in items])


def exchange(x, axes, sizes, cid, gather=False):
    return exchange_many([(x, axes, gather)], sizes, cid)[0]


HALO_MOVES = ((1, 0), (-1, 0), (0, 1), (0, -1), (1, 1), (1, -1), (-1, 1), (-1, -1))


def halo_kernel(*refs, sizes):
    sends, recvs = refs[:3], refs[3:6]
    send_sem, recv_sem = refs[6:8]
    row, col = lax.axis_index("row"), lax.axis_index("col")

    def target(dr, dc):
        return {"row": lax.rem(row + dr + sizes["row"], sizes["row"]), "col": lax.rem(col + dc + sizes["col"], sizes["col"])}

    barrier = pltpu.get_barrier_semaphore()
    for dr, dc in HALO_MOVES:
        pl.semaphore_signal(barrier, inc=1, device_id=target(dr, dc), device_id_type=pl.DeviceIdType.MESH)
    pl.semaphore_wait(barrier, len(HALO_MOVES))
    copies = []
    for k, (dr, dc) in enumerate(HALO_MOVES):
        kind, slot = (0, k) if k < 2 else ((1, k - 2) if k < 4 else (2, k - 4))
        copy = pltpu.make_async_remote_copy(
            src_ref=sends[kind].at[slot],
            dst_ref=recvs[kind].at[slot],
            send_sem=send_sem.at[k],
            recv_sem=recv_sem.at[k],
            device_id=target(dr, dc),
            device_id_type=pl.DeviceIdType.MESH,
        )
        copy.start()
        copies.append(copy)
    for copy in copies:
        copy.wait_send()
        copy.wait_recv()


def padded_pair(tiles, sizes):
    rows_out = jnp.stack([tiles[:, -1], tiles[:, 0]])
    cols_out = jnp.stack([tiles[:, :, -1], tiles[:, :, 0]])
    corners_out = jnp.stack([tiles[:, -1, -1], tiles[:, -1, 0], tiles[:, 0, -1], tiles[:, 0, 0]])
    sends = (rows_out, cols_out, corners_out)
    recvs = pl.pallas_call(
        functools.partial(halo_kernel, sizes=sizes),
        out_shape=tuple(jax.ShapeDtypeStruct(x.shape, x.dtype) for x in sends),
        in_specs=[pl.BlockSpec(memory_space=pltpu.VMEM)] * 3,
        out_specs=tuple(pl.BlockSpec(memory_space=pltpu.VMEM) for _ in sends),
        scratch_shapes=[pltpu.SemaphoreType.DMA((len(HALO_MOVES),)), pltpu.SemaphoreType.DMA((len(HALO_MOVES),))],
        compiler_params=pltpu.CompilerParams(collective_id=8, has_side_effects=True),
    )(*sends)
    rows_in, cols_in, corners_in = recvs
    row, col = lax.axis_index("row"), lax.axis_index("col")
    up, down = row > 0, row < sizes["row"] - 1
    left, right = col > 0, col < sizes["col"] - 1
    zero = jnp.zeros((), tiles.dtype)
    top = jnp.where(up, rows_in[0], zero)
    bottom = jnp.where(down, rows_in[1], zero)
    west = jnp.where(left, cols_in[0], zero)
    east = jnp.where(right, cols_in[1], zero)
    top_left = jnp.where(up & left, corners_in[0], zero)
    top_right = jnp.where(up & right, corners_in[1], zero)
    bottom_left = jnp.where(down & left, corners_in[2], zero)
    bottom_right = jnp.where(down & right, corners_in[3], zero)
    first = jnp.concatenate([top_left[:, None], top, top_right[:, None]], axis=1)
    middle = jnp.concatenate([west[:, :, None], tiles, east[:, :, None]], axis=2)
    last = jnp.concatenate([bottom_left[:, None], bottom, bottom_right[:, None]], axis=1)
    return jnp.concatenate([first[:, None], middle, last[:, None]], axis=1)


def silu_slope(pre_float):
    sigma = jax.nn.sigmoid(pre_float)
    return sigma * (1.0 + pre_float * (1.0 - sigma))


def exact_dot(left, right, contract):
    return lax.dot_general(
        left.astype(jnp.float32),
        right.astype(jnp.float32),
        (contract, ((), ())),
        precision=lax.Precision.HIGHEST,
        preferred_element_type=jnp.float32,
    )


TAPS = [(a, b) for a in (-1, 0, 1) for b in (-1, 0, 1)]


def on_device(x_input, pre_act, out_grad, conv_weight, q_prev, sizes):
    height, breadth, channels = (x_input.shape[1], x_input.shape[2], x_input.shape[3])
    pixels = height * breadth
    rank = q_prev.shape[2]
    taps = len(TAPS)
    pre_float = pre_act.reshape(pixels, channels).astype(jnp.float32)
    hidden = jax.nn.silu(pre_float).astype(jnp.bfloat16)
    both_pad = padded_pair(
        jnp.stack([out_grad.reshape(height, breadth, channels), x_input.reshape(height, breadth, channels)]), sizes
    )
    grad_pad, input_pad = both_pad[0], both_pad[1]
    back_grad = jnp.zeros((pixels, channels), jnp.float32)
    for a, b in TAPS:
        window = grad_pad[1 - a : 1 - a + height, 1 - b : 1 - b + breadth].reshape(pixels, channels)
        back_grad = back_grad + lax.dot_general(
            window, conv_weight[a + 1, b + 1], (((1,), (1,)), ((), ())), preferred_element_type=jnp.float32
        )
    pre_grad = (back_grad * silu_slope(pre_float)).astype(jnp.bfloat16)

    grid = (height + 2, breadth + 2)
    grad_flat = grad_pad.reshape(-1, channels)
    input_flat = input_pad.reshape(-1, channels)
    q_taps = q_prev.reshape(taps, channels, 2, rank).transpose(2, 1, 0, 3).reshape(2, channels, taps * rank)

    first_terms = exact_dot(input_flat, q_taps[0], ((1,), (0,))).reshape(grid + (taps, rank))
    first_sum = sum(
        first_terms[1 + a : 1 + a + height, 1 + b : 1 + b + breadth, k] for k, (a, b) in enumerate(TAPS)
    ).reshape(pixels, rank)
    first_raw = exact_dot(pre_grad, first_sum, ((0,), (0,)))
    second_terms = exact_dot(hidden, q_taps[1], ((1,), (0,))).reshape(height, breadth, taps, rank)
    second_sum = sum(
        jnp.pad(second_terms[:, :, k], ((1 - a, 1 + a), (1 - b, 1 + b), (0, 0))) for k, (a, b) in enumerate(TAPS)
    ).reshape(-1, rank)
    second_raw = exact_dot(grad_flat, second_sum, ((0,), (0,)))

    power_raw = all_sum_small(jnp.stack([first_raw, second_raw], axis=1), sizes)

    first_image = exact_dot(pre_grad, power_raw[:, 0], ((1,), (0,))).reshape(height, breadth, rank)
    first_spread = jnp.concatenate(
        [
            jnp.pad(first_image, ((1 + a, 1 - a), (1 + b, 1 - b), (0, 0))).reshape(-1, rank)
            for a, b in TAPS
        ],
        axis=1,
    )
    first_rows = exact_dot(input_flat, first_spread, ((0,), (0,)))
    second_image = exact_dot(grad_flat, power_raw[:, 1], ((1,), (0,))).reshape(grid + (rank,))
    second_spread = jnp.concatenate(
        [
            second_image[1 - a : 1 - a + height, 1 - b : 1 - b + breadth].reshape(pixels, rank)
            for a, b in TAPS
        ],
        axis=1,
    )
    second_rows = exact_dot(hidden, second_spread, ((0,), (0,)))
    rows = jnp.stack([first_rows, second_rows]).reshape(2, channels, taps, rank)
    rows = rows.transpose(2, 1, 0, 3).reshape(taps * channels, 2, rank)
    row_block = block_sum(rows, sizes)

    gram = jnp.einsum(
        "mqn,mqg->qng", power_raw, power_raw, precision=lax.Precision.HIGHEST, preferred_element_type=jnp.float32
    )
    lower = jnp.linalg.cholesky(gram)
    basis_count = channels // sizes["dp"]
    raw_part = lax.dynamic_slice_in_dim(power_raw, lax.axis_index("dp") * basis_count, basis_count, 0)
    basis_out = lax.linalg.triangular_solve(
        lower, raw_part.transpose(1, 0, 2), left_side=False, lower=True, transpose_a=True
    ).transpose(1, 0, 2)
    factor_out = lax.linalg.triangular_solve(
        lower, row_block.transpose(1, 0, 2), left_side=False, lower=True, transpose_a=True
    ).transpose(1, 0, 2)
    return (basis_out, factor_out)


def allsum_kernel(p_ref, o_ref, recv1, send2, recv2, piece, recv3, chunk, *sems, sizes):
    group_axes, ring_axes = ("row", "col"), ("dp",)
    n_group = sizes["row"] * sizes["col"]
    n_ring = sizes["dp"]
    me_group = lax.axis_index("row") * sizes["col"] + lax.axis_index("col")
    me_ring = lax.axis_index("dp")
    barrier = pltpu.get_barrier_semaphore()
    for s in range(1, n_group):
        peer = member_coords(lax.rem(me_group + s, n_group), group_axes, sizes)
        pl.semaphore_signal(barrier, inc=1, device_id=peer, device_id_type=pl.DeviceIdType.MESH)
    for s in range(1, n_ring):
        peer = member_coords(lax.rem(me_ring + s, n_ring), ring_axes, sizes)
        pl.semaphore_signal(barrier, inc=1, device_id=peer, device_id_type=pl.DeviceIdType.MESH)
    pl.semaphore_wait(barrier, n_group - 1 + n_ring - 1)

    def phase(source, target, me, n, axes, send_sem, recv_sem, local_sem, gather):
        copies = []
        for s in range(1, n):
            dst = lax.rem(me + s, n)
            copy = pltpu.make_async_remote_copy(
                src_ref=source if gather else source.at[dst],
                dst_ref=target.at[me],
                send_sem=send_sem.at[s - 1],
                recv_sem=recv_sem.at[s - 1],
                device_id=member_coords(dst, axes, sizes),
                device_id_type=pl.DeviceIdType.MESH,
            )
            copy.start()
            copies.append(copy)
        local = pltpu.make_async_copy(source if gather else source.at[me], target.at[me], local_sem)
        local.start()
        for copy in copies:
            copy.wait_send()
            copy.wait_recv()
        local.wait()

    phase(p_ref, recv1, me_group, n_group, group_axes, sems[0], sems[1], sems[8], False)
    total = recv1[0]
    for j in range(1, n_group):
        total = total + recv1[j]
    for j in range(n_ring):
        send2[j] = total[j : j + 1]
    phase(send2, recv2, me_ring, n_ring, ring_axes, sems[2], sems[3], sems[9], False)
    reduced = recv2[0]
    for j in range(1, n_ring):
        reduced = reduced + recv2[j]
    piece[...] = reduced
    phase(piece, recv3, me_ring, n_ring, ring_axes, sems[4], sems[5], sems[10], True)
    for j in range(n_ring):
        chunk[j : j + 1] = recv3[j]
    phase(chunk, o_ref, me_group, n_group, group_axes, sems[6], sems[7], sems[11], True)


def all_sum_small(value, sizes):
    shape = value.shape
    n_group = sizes["row"] * sizes["col"]
    n_ring = sizes["dp"]
    width = value.size // (n_group * n_ring)
    parts = value.reshape(n_group, n_ring, width)
    vmem = pl.BlockSpec(memory_space=pltpu.VMEM)
    out = pl.pallas_call(
        functools.partial(allsum_kernel, sizes=sizes),
        out_shape=jax.ShapeDtypeStruct(parts.shape, parts.dtype),
        in_specs=[vmem],
        out_specs=vmem,
        scratch_shapes=[
            pltpu.VMEM((n_group, n_ring, width), jnp.float32),
            pltpu.VMEM((n_ring, 1, width), jnp.float32),
            pltpu.VMEM((n_ring, 1, width), jnp.float32),
            pltpu.VMEM((1, width), jnp.float32),
            pltpu.VMEM((n_ring, 1, width), jnp.float32),
            pltpu.VMEM((n_ring, width), jnp.float32),
        ]
        + [pltpu.SemaphoreType.DMA((n - 1,)) for n in (n_group, n_group, n_ring, n_ring, n_ring, n_ring, n_group, n_group)]
        + [pltpu.SemaphoreType.DMA] * 4,
        compiler_params=pltpu.CompilerParams(collective_id=0, has_side_effects=True),
    )(parts)
    return out.reshape(shape)


def block_sum(value, sizes):
    shape = value.shape
    blocks, rows_n, cols_n = sizes["dp"], sizes["row"], sizes["col"]
    group = rows_n * cols_n
    block_rows = shape[0] // blocks
    piece_rows = -(-block_rows // (group * 8)) * 8
    lanes = math.prod(shape[1:])
    padded = jnp.pad(value.reshape(blocks, block_rows, lanes), ((0, 0), (0, piece_rows * group - block_rows), (0, 0)))
    pieces = padded.reshape(blocks, rows_n, cols_n, piece_rows, lanes)
    half = blocks // 2
    first = pieces[:half].transpose(1, 2, 0, 3, 4)
    second = pieces[half:].transpose(2, 1, 0, 3, 4)
    first, second = exchange_many([(first, ("row",), False), (second, ("col",), False)], sizes, 4)
    first, second = exchange_many(
        [(first.sum(0), ("col",), False), (second.sum(0), ("row",), False)], sizes, 5
    )
    pieces = jnp.concatenate([first.sum(0), second.sum(0)])
    piece = exchange(pieces, ("dp",), sizes, 6).sum(0)
    block = exchange(piece, ("row", "col"), sizes, 7, gather=True)
    return block.reshape(group * piece_rows, lanes)[:block_rows].reshape((block_rows,) + shape[1:])


def solution(mesh):
    placed = (
        P("dp", "row", "col", None),
        P("dp", "row", "col", None),
        P("dp", "row", "col", None),
        P(),
        P(),
    )
    sizes = dict(mesh.shape)
    return jax.shard_map(
        functools.partial(on_device, sizes=sizes),
        mesh=mesh,
        in_specs=placed,
        out_specs=(P("dp", None, None), P("dp", None, None)),
        check_vma=False,
    )
```

```python
import functools
import math

import jax
import jax.numpy as jnp
from jax import lax
from jax.experimental import pallas as pl
from jax.experimental.pallas import tpu as pltpu
from jax.sharding import PartitionSpec as P


def split_of(sizes):
    return 4 if sizes["dp"] % 4 == 0 else 1


def member_index(axis, sizes):
    if axis == "dp_y":
        return lax.rem(lax.axis_index("dp"), split_of(sizes))
    if axis == "dp_z":
        return lax.axis_index("dp") // split_of(sizes)
    return lax.axis_index(axis)


def axis_length(axis, sizes):
    if axis == "dp_y":
        return split_of(sizes)
    if axis == "dp_z":
        return sizes["dp"] // split_of(sizes)
    return sizes[axis]


def member_coords(j, axes, sizes):
    coords = {}
    for axis in reversed(axes):
        index = lax.rem(j, axis_length(axis, sizes))
        j = j // axis_length(axis, sizes)
        if axis == "dp_y":
            coords["dp"] = lax.axis_index("dp") // split_of(sizes) * split_of(sizes) + index
        elif axis == "dp_z":
            coords["dp"] = index * split_of(sizes) + lax.rem(lax.axis_index("dp"), split_of(sizes))
        else:
            coords[axis] = index
    return coords


def exchange_kernel(*refs, jobs, sizes):
    count = len(jobs)
    x_refs, o_refs = refs[:count], refs[count : 2 * count]
    sems = refs[2 * count :]
    barrier = pltpu.get_barrier_semaphore()
    plans = []
    total = 0
    for axes, gather in jobs:
        n = math.prod(sizes[a] for a in axes)
        me = 0
        for axis in axes:
            me = me * sizes[axis] + lax.axis_index(axis)
        for s in range(1, n):
            peer = member_coords(lax.rem(me + s, n), axes, sizes)
            pl.semaphore_signal(barrier, inc=1, device_id=peer, device_id_type=pl.DeviceIdType.MESH)
        total += n - 1
        plans.append((n, me))
    pl.semaphore_wait(barrier, total)
    copies, locals_ = [], []
    for job, ((axes, gather), (n, me)) in enumerate(zip(jobs, plans)):
        x_ref, o_ref = x_refs[job], o_refs[job]
        send_sem, recv_sem, local_sem = sems[3 * job : 3 * job + 3]
        for s in range(1, n):
            dst = lax.rem(me + s, n)
            copy = pltpu.make_async_remote_copy(
                src_ref=x_ref if gather else x_ref.at[dst],
                dst_ref=o_ref.at[me],
                send_sem=send_sem.at[s - 1],
                recv_sem=recv_sem.at[s - 1],
                device_id=member_coords(dst, axes, sizes),
                device_id_type=pl.DeviceIdType.MESH,
            )
            copy.start()
            copies.append(copy)
        local = pltpu.make_async_copy(x_ref if gather else x_ref.at[me], o_ref.at[me], local_sem)
        local.start()
        locals_.append(local)
    for copy in copies:
        copy.wait_send()
        copy.wait_recv()
    for local in locals_:
        local.wait()


def exchange_many(items, sizes, cid):
    jobs, shapes, scratch = [], [], []
    for x, axes, gather in items:
        n = math.prod(sizes[a] for a in axes)
        slab = x.shape if gather else x.shape[1:]
        jobs.append((axes, gather))
        shapes.append(jax.ShapeDtypeStruct((n,) + slab, x.dtype))
        scratch += [
            pltpu.SemaphoreType.DMA((max(n - 1, 1),)),
            pltpu.SemaphoreType.DMA((max(n - 1, 1),)),
            pltpu.SemaphoreType.DMA,
        ]
    return pl.pallas_call(
        functools.partial(exchange_kernel, jobs=tuple(jobs), sizes=sizes),
        out_shape=tuple(shapes),
        in_specs=[pl.BlockSpec(memory_space=pltpu.VMEM)] * len(items),
        out_specs=tuple(pl.BlockSpec(memory_space=pltpu.VMEM) for _ in items),
        scratch_shapes=scratch,
        compiler_params=pltpu.CompilerParams(
            collective_id=cid, has_side_effects=True, vmem_limit_bytes=48 * 1024 * 1024
        ),
    )(*[x for x, _, _ in items])


def exchange(x, axes, sizes, cid, gather=False):
    return exchange_many([(x, axes, gather)], sizes, cid)[0]


HALO_MOVES = ((1, 0), (-1, 0), (0, 1), (0, -1), (1, 1), (1, -1), (-1, 1), (-1, -1))


def halo_kernel(*refs, sizes):
    sends, recvs = refs[:3], refs[3:6]
    send_sem, recv_sem = refs[6:8]
    row, col = lax.axis_index("row"), lax.axis_index("col")

    def target(dr, dc):
        return {"row": lax.rem(row + dr + sizes["row"], sizes["row"]), "col": lax.rem(col + dc + sizes["col"], sizes["col"])}

    barrier = pltpu.get_barrier_semaphore()
    for dr, dc in HALO_MOVES:
        pl.semaphore_signal(barrier, inc=1, device_id=target(dr, dc), device_id_type=pl.DeviceIdType.MESH)
    pl.semaphore_wait(barrier, len(HALO_MOVES))
    copies = []
    for k, (dr, dc) in enumerate(HALO_MOVES):
        kind, slot = (0, k) if k < 2 else ((1, k - 2) if k < 4 else (2, k - 4))
        copy = pltpu.make_async_remote_copy(
            src_ref=sends[kind].at[slot],
            dst_ref=recvs[kind].at[slot],
            send_sem=send_sem.at[k],
            recv_sem=recv_sem.at[k],
            device_id=target(dr, dc),
            device_id_type=pl.DeviceIdType.MESH,
        )
        copy.start()
        copies.append(copy)
    for copy in copies:
        copy.wait_send()
        copy.wait_recv()


def padded_pair(tiles, sizes):
    rows_out = jnp.stack([tiles[:, -1], tiles[:, 0]])
    cols_out = jnp.stack([tiles[:, :, -1], tiles[:, :, 0]])
    corners_out = jnp.stack([tiles[:, -1, -1], tiles[:, -1, 0], tiles[:, 0, -1], tiles[:, 0, 0]])
    sends = (rows_out, cols_out, corners_out)
    recvs = pl.pallas_call(
        functools.partial(halo_kernel, sizes=sizes),
        out_shape=tuple(jax.ShapeDtypeStruct(x.shape, x.dtype) for x in sends),
        in_specs=[pl.BlockSpec(memory_space=pltpu.VMEM)] * 3,
        out_specs=tuple(pl.BlockSpec(memory_space=pltpu.VMEM) for _ in sends),
        scratch_shapes=[pltpu.SemaphoreType.DMA((len(HALO_MOVES),)), pltpu.SemaphoreType.DMA((len(HALO_MOVES),))],
        compiler_params=pltpu.CompilerParams(collective_id=8, has_side_effects=True),
    )(*sends)
    rows_in, cols_in, corners_in = recvs
    row, col = lax.axis_index("row"), lax.axis_index("col")
    up, down = row > 0, row < sizes["row"] - 1
    left, right = col > 0, col < sizes["col"] - 1
    zero = jnp.zeros((), tiles.dtype)
    top = jnp.where(up, rows_in[0], zero)
    bottom = jnp.where(down, rows_in[1], zero)
    west = jnp.where(left, cols_in[0], zero)
    east = jnp.where(right, cols_in[1], zero)
    top_left = jnp.where(up & left, corners_in[0], zero)
    top_right = jnp.where(up & right, corners_in[1], zero)
    bottom_left = jnp.where(down & left, corners_in[2], zero)
    bottom_right = jnp.where(down & right, corners_in[3], zero)
    first = jnp.concatenate([top_left[:, None], top, top_right[:, None]], axis=1)
    middle = jnp.concatenate([west[:, :, None], tiles, east[:, :, None]], axis=2)
    last = jnp.concatenate([bottom_left[:, None], bottom, bottom_right[:, None]], axis=1)
    return jnp.concatenate([first[:, None], middle, last[:, None]], axis=1)


def silu_slope(pre_float):
    sigma = jax.nn.sigmoid(pre_float)
    return sigma * (1.0 + pre_float * (1.0 - sigma))


def exact_dot(left, right, contract):
    return lax.dot_general(
        left.astype(jnp.float32),
        right.astype(jnp.float32),
        (contract, ((), ())),
        precision=lax.Precision.HIGHEST,
        preferred_element_type=jnp.float32,
    )


TAPS = [(a, b) for a in (-1, 0, 1) for b in (-1, 0, 1)]


def on_device(x_input, pre_act, out_grad, conv_weight, q_prev, sizes):
    height, breadth, channels = (x_input.shape[1], x_input.shape[2], x_input.shape[3])
    pixels = height * breadth
    rank = q_prev.shape[2]
    taps = len(TAPS)
    pre_float = pre_act.reshape(pixels, channels).astype(jnp.float32)
    hidden = jax.nn.silu(pre_float).astype(jnp.bfloat16)
    both_pad = padded_pair(
        jnp.stack([out_grad.reshape(height, breadth, channels), x_input.reshape(height, breadth, channels)]), sizes
    )
    grad_pad, input_pad = both_pad[0], both_pad[1]
    back_grad = jnp.zeros((pixels, channels), jnp.float32)
    for a, b in TAPS:
        window = grad_pad[1 - a : 1 - a + height, 1 - b : 1 - b + breadth].reshape(pixels, channels)
        back_grad = back_grad + lax.dot_general(
            window, conv_weight[a + 1, b + 1], (((1,), (1,)), ((), ())), preferred_element_type=jnp.float32
        )
    pre_grad = (back_grad * silu_slope(pre_float)).astype(jnp.bfloat16)

    grid = (height + 2, breadth + 2)
    grad_flat = grad_pad.reshape(-1, channels)
    input_flat = input_pad.reshape(-1, channels)
    q_taps = q_prev.reshape(taps, channels, 2, rank).transpose(2, 1, 0, 3).reshape(2, channels, taps * rank)

    first_terms = exact_dot(input_flat, q_taps[0], ((1,), (0,))).reshape(grid + (taps, rank))
    first_sum = sum(
        first_terms[1 + a : 1 + a + height, 1 + b : 1 + b + breadth, k] for k, (a, b) in enumerate(TAPS)
    ).reshape(pixels, rank)
    first_raw = exact_dot(pre_grad, first_sum, ((0,), (0,)))
    second_terms = exact_dot(hidden, q_taps[1], ((1,), (0,))).reshape(height, breadth, taps, rank)
    second_sum = sum(
        jnp.pad(second_terms[:, :, k], ((1 - a, 1 + a), (1 - b, 1 + b), (0, 0))) for k, (a, b) in enumerate(TAPS)
    ).reshape(-1, rank)
    second_raw = exact_dot(grad_flat, second_sum, ((0,), (0,)))

    power_raw = all_sum_small(jnp.stack([first_raw, second_raw], axis=1), sizes)

    first_image = exact_dot(pre_grad, power_raw[:, 0], ((1,), (0,))).reshape(height, breadth, rank)
    first_spread = jnp.concatenate(
        [
            jnp.pad(first_image, ((1 + a, 1 - a), (1 + b, 1 - b), (0, 0))).reshape(-1, rank)
            for a, b in TAPS
        ],
        axis=1,
    )
    first_rows = exact_dot(input_flat, first_spread, ((0,), (0,)))
    second_image = exact_dot(grad_flat, power_raw[:, 1], ((1,), (0,))).reshape(grid + (rank,))
    second_spread = jnp.concatenate(
        [
            second_image[1 - a : 1 - a + height, 1 - b : 1 - b + breadth].reshape(pixels, rank)
            for a, b in TAPS
        ],
        axis=1,
    )
    second_rows = exact_dot(hidden, second_spread, ((0,), (0,)))
    rows = jnp.stack([first_rows, second_rows]).reshape(2, channels, taps, rank)
    rows = rows.transpose(2, 1, 0, 3).reshape(taps * channels, 2, rank)
    row_block = block_sum(rows, sizes)

    gram = jnp.einsum(
        "mqn,mqg->qng", power_raw, power_raw, precision=lax.Precision.HIGHEST, preferred_element_type=jnp.float32
    )
    lower = jnp.linalg.cholesky(gram)
    basis_count = channels // sizes["dp"]
    raw_part = lax.dynamic_slice_in_dim(power_raw, lax.axis_index("dp") * basis_count, basis_count, 0)
    basis_out = lax.linalg.triangular_solve(
        lower, raw_part.transpose(1, 0, 2), left_side=False, lower=True, transpose_a=True
    ).transpose(1, 0, 2)
    factor_out = lax.linalg.triangular_solve(
        lower, row_block.transpose(1, 0, 2), left_side=False, lower=True, transpose_a=True
    ).transpose(1, 0, 2)
    return (basis_out, factor_out)


def allsum_kernel(p_ref, o_ref, *scratch, sizes):
    recv1, send_y, recv_y, send_z, recv_z, piece, recv_z2, zrows, recv_y2, chunk = scratch[:10]
    sems = scratch[10:]
    groups = (("row", "col"), ("dp_y",), ("dp_z",))
    count = {g: math.prod(axis_length(a, sizes) for a in g) for g in groups}
    me = {}
    for g in groups:
        index = 0
        for axis in g:
            index = index * axis_length(axis, sizes) + member_index(axis, sizes)
        me[g] = index
    barrier = pltpu.get_barrier_semaphore()
    for g in groups:
        for s in range(1, count[g]):
            peer = member_coords(lax.rem(me[g] + s, count[g]), g, sizes)
            pl.semaphore_signal(barrier, inc=1, device_id=peer, device_id_type=pl.DeviceIdType.MESH)
    pl.semaphore_wait(barrier, sum(count[g] - 1 for g in groups))

    def phase(k, source, target, g, gather):
        send_sem, recv_sem, local_sem = sems[3 * k : 3 * k + 3]
        n, mine = count[g], me[g]
        copies = []
        for s in range(1, n):
            dst = lax.rem(mine + s, n)
            copy = pltpu.make_async_remote_copy(
                src_ref=source if gather else source.at[dst],
                dst_ref=target.at[mine],
                send_sem=send_sem.at[s - 1],
                recv_sem=recv_sem.at[s - 1],
                device_id=member_coords(dst, g, sizes),
                device_id_type=pl.DeviceIdType.MESH,
            )
            copy.start()
            copies.append(copy)
        local = pltpu.make_async_copy(source if gather else source.at[mine], target.at[mine], local_sem)
        local.start()
        for copy in copies:
            copy.wait_send()
            copy.wait_recv()
        local.wait()

    def summed(ref):
        total = ref[0]
        for j in range(1, ref.shape[0]):
            total = total + ref[j]
        return total

    group, along_y, along_z = groups
    ny, nz = count[along_y], count[along_z]
    phase(0, p_ref, recv1, group, False)
    total = summed(recv1)
    for j in range(ny):
        send_y[j] = total[j * nz : (j + 1) * nz]
    phase(1, send_y, recv_y, along_y, False)
    part = summed(recv_y)
    for j in range(nz):
        send_z[j] = part[j : j + 1]
    phase(2, send_z, recv_z, along_z, False)
    piece[...] = summed(recv_z)
    phase(3, piece, recv_z2, along_z, True)
    for j in range(nz):
        zrows[j : j + 1] = recv_z2[j]
    phase(4, zrows, recv_y2, along_y, True)
    for j in range(ny):
        chunk[j * nz : (j + 1) * nz] = recv_y2[j]
    phase(5, chunk, o_ref, group, True)


def all_sum_small(value, sizes):
    shape = value.shape
    n_group = sizes["row"] * sizes["col"]
    ny = split_of(sizes)
    nz = sizes["dp"] // ny
    width = value.size // (n_group * ny * nz)
    parts = value.reshape(n_group, ny * nz, width)
    vmem = pl.BlockSpec(memory_space=pltpu.VMEM)
    f32 = jnp.float32
    sems = []
    for n in (n_group, ny, nz, nz, ny, n_group):
        sems += [pltpu.SemaphoreType.DMA((max(n - 1, 1),)), pltpu.SemaphoreType.DMA((max(n - 1, 1),)), pltpu.SemaphoreType.DMA]
    out = pl.pallas_call(
        functools.partial(allsum_kernel, sizes=sizes),
        out_shape=jax.ShapeDtypeStruct(parts.shape, parts.dtype),
        in_specs=[vmem],
        out_specs=vmem,
        scratch_shapes=[
            pltpu.VMEM((n_group, ny * nz, width), f32),
            pltpu.VMEM((ny, nz, width), f32),
            pltpu.VMEM((ny, nz, width), f32),
            pltpu.VMEM((nz, 1, width), f32),
            pltpu.VMEM((nz, 1, width), f32),
            pltpu.VMEM((1, width), f32),
            pltpu.VMEM((nz, 1, width), f32),
            pltpu.VMEM((nz, width), f32),
            pltpu.VMEM((ny, nz, width), f32),
            pltpu.VMEM((ny * nz, width), f32),
        ]
        + sems,
        compiler_params=pltpu.CompilerParams(collective_id=0, has_side_effects=True),
    )(parts)
    return out.reshape(shape)


def block_sum(value, sizes):
    shape = value.shape
    blocks, rows_n, cols_n = sizes["dp"], sizes["row"], sizes["col"]
    group = rows_n * cols_n
    block_rows = shape[0] // blocks
    piece_rows = -(-block_rows // (group * 8)) * 8
    lanes = math.prod(shape[1:])
    padded = jnp.pad(value.reshape(blocks, block_rows, lanes), ((0, 0), (0, piece_rows * group - block_rows), (0, 0)))
    pieces = padded.reshape(blocks, rows_n, cols_n, piece_rows, lanes)
    half = blocks // 2
    first = pieces[:half].transpose(1, 2, 0, 3, 4)
    second = pieces[half:].transpose(2, 1, 0, 3, 4)
    first, second = exchange_many([(first, ("row",), False), (second, ("col",), False)], sizes, 4)
    first, second = exchange_many(
        [(first.sum(0), ("col",), False), (second.sum(0), ("row",), False)], sizes, 5
    )
    pieces = jnp.concatenate([first.sum(0), second.sum(0)])
    piece = exchange(pieces, ("dp",), sizes, 6).sum(0)
    block = exchange(piece, ("row", "col"), sizes, 7, gather=True)
    return block.reshape(group * piece_rows, lanes)[:block_rows].reshape((block_rows,) + shape[1:])


def solution(mesh):
    placed = (
        P("dp", "row", "col", None),
        P("dp", "row", "col", None),
        P("dp", "row", "col", None),
        P(),
        P(),
    )
    sizes = dict(mesh.shape)
    return jax.shard_map(
        functools.partial(on_device, sizes=sizes),
        mesh=mesh,
        in_specs=placed,
        out_specs=(P("dp", None, None), P("dp", None, None)),
        check_vma=False,
    )
```

```python
import functools
import math

import jax
import jax.numpy as jnp
from jax import lax
from jax.experimental import pallas as pl
from jax.experimental.pallas import tpu as pltpu
from jax.sharding import PartitionSpec as P


def split_of(sizes):
    return 4 if sizes["dp"] % 4 == 0 else 1


def member_index(axis, sizes):
    if axis == "dp_y":
        return lax.rem(lax.axis_index("dp"), split_of(sizes))
    if axis == "dp_z":
        return lax.axis_index("dp") // split_of(sizes)
    return lax.axis_index(axis)


def axis_length(axis, sizes):
    if axis == "dp_y":
        return split_of(sizes)
    if axis == "dp_z":
        return sizes["dp"] // split_of(sizes)
    return sizes[axis]


def member_coords(j, axes, sizes):
    coords = {}
    for axis in reversed(axes):
        index = lax.rem(j, axis_length(axis, sizes))
        j = j // axis_length(axis, sizes)
        if axis == "dp_y":
            coords["dp"] = lax.axis_index("dp") // split_of(sizes) * split_of(sizes) + index
        elif axis == "dp_z":
            coords["dp"] = index * split_of(sizes) + lax.rem(lax.axis_index("dp"), split_of(sizes))
        else:
            coords[axis] = index
    return coords


def exchange_kernel(*refs, jobs, sizes):
    count = len(jobs)
    x_refs, o_refs = refs[:count], refs[count : 2 * count]
    sems = refs[2 * count :]
    barrier = pltpu.get_barrier_semaphore()
    plans = []
    total = 0
    for axes, gather in jobs:
        n = math.prod(sizes[a] for a in axes)
        me = 0
        for axis in axes:
            me = me * sizes[axis] + lax.axis_index(axis)
        for s in range(1, n):
            peer = member_coords(lax.rem(me + s, n), axes, sizes)
            pl.semaphore_signal(barrier, inc=1, device_id=peer, device_id_type=pl.DeviceIdType.MESH)
        total += n - 1
        plans.append((n, me))
    pl.semaphore_wait(barrier, total)
    copies, locals_ = [], []
    for job, ((axes, gather), (n, me)) in enumerate(zip(jobs, plans)):
        x_ref, o_ref = x_refs[job], o_refs[job]
        send_sem, recv_sem, local_sem = sems[3 * job : 3 * job + 3]
        for s in range(1, n):
            dst = lax.rem(me + s, n)
            copy = pltpu.make_async_remote_copy(
                src_ref=x_ref if gather else x_ref.at[dst],
                dst_ref=o_ref.at[me],
                send_sem=send_sem.at[s - 1],
                recv_sem=recv_sem.at[s - 1],
                device_id=member_coords(dst, axes, sizes),
                device_id_type=pl.DeviceIdType.MESH,
            )
            copy.start()
            copies.append(copy)
        local = pltpu.make_async_copy(x_ref if gather else x_ref.at[me], o_ref.at[me], local_sem)
        local.start()
        locals_.append(local)
    for copy in copies:
        copy.wait_send()
        copy.wait_recv()
    for local in locals_:
        local.wait()


def exchange_many(items, sizes, cid):
    jobs, shapes, scratch = [], [], []
    for x, axes, gather in items:
        n = math.prod(sizes[a] for a in axes)
        slab = x.shape if gather else x.shape[1:]
        jobs.append((axes, gather))
        shapes.append(jax.ShapeDtypeStruct((n,) + slab, x.dtype))
        scratch += [
            pltpu.SemaphoreType.DMA((max(n - 1, 1),)),
            pltpu.SemaphoreType.DMA((max(n - 1, 1),)),
            pltpu.SemaphoreType.DMA,
        ]
    return pl.pallas_call(
        functools.partial(exchange_kernel, jobs=tuple(jobs), sizes=sizes),
        out_shape=tuple(shapes),
        in_specs=[pl.BlockSpec(memory_space=pltpu.VMEM)] * len(items),
        out_specs=tuple(pl.BlockSpec(memory_space=pltpu.VMEM) for _ in items),
        scratch_shapes=scratch,
        compiler_params=pltpu.CompilerParams(
            collective_id=cid, has_side_effects=True, vmem_limit_bytes=48 * 1024 * 1024
        ),
    )(*[x for x, _, _ in items])


def exchange(x, axes, sizes, cid, gather=False):
    return exchange_many([(x, axes, gather)], sizes, cid)[0]


HALO_MOVES = ((1, 0), (-1, 0), (0, 1), (0, -1), (1, 1), (1, -1), (-1, 1), (-1, -1))


def halo_kernel(*refs, sizes):
    sends, recvs = refs[:3], refs[3:6]
    send_sem, recv_sem = refs[6:8]
    row, col = lax.axis_index("row"), lax.axis_index("col")

    def target(dr, dc):
        return {"row": lax.rem(row + dr + sizes["row"], sizes["row"]), "col": lax.rem(col + dc + sizes["col"], sizes["col"])}

    barrier = pltpu.get_barrier_semaphore()
    for dr, dc in HALO_MOVES:
        pl.semaphore_signal(barrier, inc=1, device_id=target(dr, dc), device_id_type=pl.DeviceIdType.MESH)
    pl.semaphore_wait(barrier, len(HALO_MOVES))
    copies = []
    for k, (dr, dc) in enumerate(HALO_MOVES):
        kind, slot = (0, k) if k < 2 else ((1, k - 2) if k < 4 else (2, k - 4))
        copy = pltpu.make_async_remote_copy(
            src_ref=sends[kind].at[slot],
            dst_ref=recvs[kind].at[slot],
            send_sem=send_sem.at[k],
            recv_sem=recv_sem.at[k],
            device_id=target(dr, dc),
            device_id_type=pl.DeviceIdType.MESH,
        )
        copy.start()
        copies.append(copy)
    for copy in copies:
        copy.wait_send()
        copy.wait_recv()


def padded_pair(tiles, sizes):
    rows_out = jnp.stack([tiles[:, -1], tiles[:, 0]])
    cols_out = jnp.stack([tiles[:, :, -1], tiles[:, :, 0]])
    corners_out = jnp.stack([tiles[:, -1, -1], tiles[:, -1, 0], tiles[:, 0, -1], tiles[:, 0, 0]])
    sends = (rows_out, cols_out, corners_out)
    recvs = pl.pallas_call(
        functools.partial(halo_kernel, sizes=sizes),
        out_shape=tuple(jax.ShapeDtypeStruct(x.shape, x.dtype) for x in sends),
        in_specs=[pl.BlockSpec(memory_space=pltpu.VMEM)] * 3,
        out_specs=tuple(pl.BlockSpec(memory_space=pltpu.VMEM) for _ in sends),
        scratch_shapes=[pltpu.SemaphoreType.DMA((len(HALO_MOVES),)), pltpu.SemaphoreType.DMA((len(HALO_MOVES),))],
        compiler_params=pltpu.CompilerParams(collective_id=8, has_side_effects=True),
    )(*sends)
    rows_in, cols_in, corners_in = recvs
    row, col = lax.axis_index("row"), lax.axis_index("col")
    up, down = row > 0, row < sizes["row"] - 1
    left, right = col > 0, col < sizes["col"] - 1
    zero = jnp.zeros((), tiles.dtype)
    top = jnp.where(up, rows_in[0], zero)
    bottom = jnp.where(down, rows_in[1], zero)
    west = jnp.where(left, cols_in[0], zero)
    east = jnp.where(right, cols_in[1], zero)
    top_left = jnp.where(up & left, corners_in[0], zero)
    top_right = jnp.where(up & right, corners_in[1], zero)
    bottom_left = jnp.where(down & left, corners_in[2], zero)
    bottom_right = jnp.where(down & right, corners_in[3], zero)
    first = jnp.concatenate([top_left[:, None], top, top_right[:, None]], axis=1)
    middle = jnp.concatenate([west[:, :, None], tiles, east[:, :, None]], axis=2)
    last = jnp.concatenate([bottom_left[:, None], bottom, bottom_right[:, None]], axis=1)
    return jnp.concatenate([first[:, None], middle, last[:, None]], axis=1)


def silu_slope(pre_float):
    sigma = jax.nn.sigmoid(pre_float)
    return sigma * (1.0 + pre_float * (1.0 - sigma))


def exact_dot(left, right, contract):
    return lax.dot_general(
        left.astype(jnp.float32),
        right.astype(jnp.float32),
        (contract, ((), ())),
        precision=lax.Precision.HIGHEST,
        preferred_element_type=jnp.float32,
    )


TAPS = [(a, b) for a in (-1, 0, 1) for b in (-1, 0, 1)]


def on_device(x_input, pre_act, out_grad, conv_weight, q_prev, sizes):
    height, breadth, channels = (x_input.shape[1], x_input.shape[2], x_input.shape[3])
    pixels = height * breadth
    rank = q_prev.shape[2]
    taps = len(TAPS)
    pre_float = pre_act.reshape(pixels, channels).astype(jnp.float32)
    hidden = jax.nn.silu(pre_float).astype(jnp.bfloat16)
    both_pad = padded_pair(
        jnp.stack([out_grad.reshape(height, breadth, channels), x_input.reshape(height, breadth, channels)]), sizes
    )
    grad_pad, input_pad = both_pad[0], both_pad[1]
    back_grad = jnp.zeros((pixels, channels), jnp.float32)
    for a, b in TAPS:
        window = grad_pad[1 - a : 1 - a + height, 1 - b : 1 - b + breadth].reshape(pixels, channels)
        back_grad = back_grad + lax.dot_general(
            window, conv_weight[a + 1, b + 1], (((1,), (1,)), ((), ())), preferred_element_type=jnp.float32
        )
    pre_grad = (back_grad * silu_slope(pre_float)).astype(jnp.bfloat16)

    grid = (height + 2, breadth + 2)
    grad_flat = grad_pad.reshape(-1, channels)
    input_flat = input_pad.reshape(-1, channels)
    q_taps = q_prev.reshape(taps, channels, 2, rank).transpose(2, 1, 0, 3).reshape(2, channels, taps * rank)

    first_terms = exact_dot(input_flat, q_taps[0], ((1,), (0,))).reshape(grid + (taps, rank))
    first_sum = sum(
        first_terms[1 + a : 1 + a + height, 1 + b : 1 + b + breadth, k] for k, (a, b) in enumerate(TAPS)
    ).reshape(pixels, rank)
    first_raw = exact_dot(pre_grad, first_sum, ((0,), (0,)))
    second_terms = exact_dot(hidden, q_taps[1], ((1,), (0,))).reshape(height, breadth, taps, rank)
    second_sum = sum(
        jnp.pad(second_terms[:, :, k], ((1 - a, 1 + a), (1 - b, 1 + b), (0, 0))) for k, (a, b) in enumerate(TAPS)
    ).reshape(-1, rank)
    second_raw = exact_dot(grad_flat, second_sum, ((0,), (0,)))

    power_raw = all_sum_small(jnp.stack([first_raw, second_raw], axis=1), sizes)

    first_image = exact_dot(pre_grad, power_raw[:, 0], ((1,), (0,))).reshape(height, breadth, rank)
    first_spread = jnp.concatenate(
        [
            jnp.pad(first_image, ((1 + a, 1 - a), (1 + b, 1 - b), (0, 0))).reshape(-1, rank)
            for a, b in TAPS
        ],
        axis=1,
    )
    first_rows = exact_dot(input_flat, first_spread, ((0,), (0,)))
    second_image = exact_dot(grad_flat, power_raw[:, 1], ((1,), (0,))).reshape(grid + (rank,))
    second_spread = jnp.concatenate(
        [
            second_image[1 - a : 1 - a + height, 1 - b : 1 - b + breadth].reshape(pixels, rank)
            for a, b in TAPS
        ],
        axis=1,
    )
    second_rows = exact_dot(hidden, second_spread, ((0,), (0,)))
    rows = jnp.stack([first_rows, second_rows]).reshape(2, channels, taps, rank)
    rows = rows.transpose(2, 1, 0, 3).reshape(taps * channels, 2, rank)
    row_block = block_sum(rows, sizes)

    gram = jnp.einsum(
        "mqn,mqg->qng", power_raw, power_raw, precision=lax.Precision.HIGHEST, preferred_element_type=jnp.float32
    )
    lower = jnp.linalg.cholesky(gram)
    basis_count = channels // sizes["dp"]
    raw_part = lax.dynamic_slice_in_dim(power_raw, lax.axis_index("dp") * basis_count, basis_count, 0)
    basis_out = lax.linalg.triangular_solve(
        lower, raw_part.transpose(1, 0, 2), left_side=False, lower=True, transpose_a=True
    ).transpose(1, 0, 2)
    factor_out = lax.linalg.triangular_solve(
        lower, row_block.transpose(1, 0, 2), left_side=False, lower=True, transpose_a=True
    ).transpose(1, 0, 2)
    return (basis_out, factor_out)


def allsum_kernel(p_ref, o_ref, *scratch, sizes):
    recv1, send_y, recv_y, send_z, recv_z, piece, recv_z2, zrows, recv_y2, chunk = scratch[:10]
    sems = scratch[10:]
    groups = (("row", "col"), ("dp_y",), ("dp_z",))
    count = {g: math.prod(axis_length(a, sizes) for a in g) for g in groups}
    me = {}
    for g in groups:
        index = 0
        for axis in g:
            index = index * axis_length(axis, sizes) + member_index(axis, sizes)
        me[g] = index
    barrier = pltpu.get_barrier_semaphore()
    for g in groups:
        for s in range(1, count[g]):
            peer = member_coords(lax.rem(me[g] + s, count[g]), g, sizes)
            pl.semaphore_signal(barrier, inc=1, device_id=peer, device_id_type=pl.DeviceIdType.MESH)
    pl.semaphore_wait(barrier, sum(count[g] - 1 for g in groups))

    def phase(k, source, target, g, gather):
        send_sem, recv_sem, local_sem = sems[3 * k : 3 * k + 3]
        n, mine = count[g], me[g]
        copies = []
        for s in range(1, n):
            dst = lax.rem(mine + s, n)
            copy = pltpu.make_async_remote_copy(
                src_ref=source if gather else source.at[dst],
                dst_ref=target.at[mine],
                send_sem=send_sem.at[s - 1],
                recv_sem=recv_sem.at[s - 1],
                device_id=member_coords(dst, g, sizes),
                device_id_type=pl.DeviceIdType.MESH,
            )
            copy.start()
            copies.append(copy)
        local = pltpu.make_async_copy(source if gather else source.at[mine], target.at[mine], local_sem)
        local.start()
        for copy in copies:
            copy.wait_send()
            copy.wait_recv()
        local.wait()

    def summed(ref):
        total = ref[0]
        for j in range(1, ref.shape[0]):
            total = total + ref[j]
        return total

    group, along_y, along_z = groups
    ny, nz = count[along_y], count[along_z]
    phase(0, p_ref, recv1, group, False)
    total = summed(recv1)
    for j in range(ny):
        send_y[j] = total[j * nz : (j + 1) * nz]
    phase(1, send_y, recv_y, along_y, False)
    part = summed(recv_y)
    for j in range(nz):
        send_z[j] = part[j : j + 1]
    phase(2, send_z, recv_z, along_z, False)
    piece[...] = summed(recv_z)
    phase(3, piece, recv_z2, along_z, True)
    for j in range(nz):
        zrows[j : j + 1] = recv_z2[j]
    phase(4, zrows, recv_y2, along_y, True)
    for j in range(ny):
        chunk[j * nz : (j + 1) * nz] = recv_y2[j]
    phase(5, chunk, o_ref, group, True)


def all_sum_small(value, sizes):
    shape = value.shape
    n_group = sizes["row"] * sizes["col"]
    ny = split_of(sizes)
    nz = sizes["dp"] // ny
    width = value.size // (n_group * ny * nz)
    parts = value.reshape(n_group, ny * nz, width)
    vmem = pl.BlockSpec(memory_space=pltpu.VMEM)
    f32 = jnp.float32
    sems = []
    for n in (n_group, ny, nz, nz, ny, n_group):
        sems += [pltpu.SemaphoreType.DMA((max(n - 1, 1),)), pltpu.SemaphoreType.DMA((max(n - 1, 1),)), pltpu.SemaphoreType.DMA]
    out = pl.pallas_call(
        functools.partial(allsum_kernel, sizes=sizes),
        out_shape=jax.ShapeDtypeStruct(parts.shape, parts.dtype),
        in_specs=[vmem],
        out_specs=vmem,
        scratch_shapes=[
            pltpu.VMEM((n_group, ny * nz, width), f32),
            pltpu.VMEM((ny, nz, width), f32),
            pltpu.VMEM((ny, nz, width), f32),
            pltpu.VMEM((nz, 1, width), f32),
            pltpu.VMEM((nz, 1, width), f32),
            pltpu.VMEM((1, width), f32),
            pltpu.VMEM((nz, 1, width), f32),
            pltpu.VMEM((nz, width), f32),
            pltpu.VMEM((ny, nz, width), f32),
            pltpu.VMEM((ny * nz, width), f32),
        ]
        + sems,
        compiler_params=pltpu.CompilerParams(collective_id=0, has_side_effects=True),
    )(parts)
    return out.reshape(shape)


def tail_kernel(first_ref, second_ref, o_ref, send, recv, piece, *sems, sizes):
    ring, group = ("dp",), ("row", "col")
    n_ring, n_group = sizes["dp"], sizes["row"] * sizes["col"]
    me_ring = lax.axis_index("dp")
    me_group = lax.axis_index("row") * sizes["col"] + lax.axis_index("col")
    barrier = pltpu.get_barrier_semaphore()
    for g, n, mine in ((ring, n_ring, me_ring), (group, n_group, me_group)):
        for s in range(1, n):
            peer = member_coords(lax.rem(mine + s, n), g, sizes)
            pl.semaphore_signal(barrier, inc=1, device_id=peer, device_id_type=pl.DeviceIdType.MESH)
    pl.semaphore_wait(barrier, n_ring - 1 + n_group - 1)

    def phase(k, source, target, g, n, mine, gather):
        send_sem, recv_sem, local_sem = sems[3 * k : 3 * k + 3]
        copies = []
        for s in range(1, n):
            dst = lax.rem(mine + s, n)
            copy = pltpu.make_async_remote_copy(
                src_ref=source if gather else source.at[dst],
                dst_ref=target.at[mine],
                send_sem=send_sem.at[s - 1],
                recv_sem=recv_sem.at[s - 1],
                device_id=member_coords(dst, g, sizes),
                device_id_type=pl.DeviceIdType.MESH,
            )
            copy.start()
            copies.append(copy)
        local = pltpu.make_async_copy(source if gather else source.at[mine], target.at[mine], local_sem)
        local.start()
        for copy in copies:
            copy.wait_send()
            copy.wait_recv()
        local.wait()

    half = first_ref.shape[1]
    for b in range(half):
        total = first_ref[0, b]
        for j in range(1, first_ref.shape[0]):
            total = total + first_ref[j, b]
        send[b] = total
        total = second_ref[0, b]
        for j in range(1, second_ref.shape[0]):
            total = total + second_ref[j, b]
        send[half + b] = total
    phase(0, send, recv, ring, n_ring, me_ring, False)
    total = recv[0]
    for j in range(1, n_ring):
        total = total + recv[j]
    piece[...] = total
    phase(1, piece, o_ref, group, n_group, me_group, True)


def block_sum(value, sizes):
    shape = value.shape
    blocks, rows_n, cols_n = sizes["dp"], sizes["row"], sizes["col"]
    group = rows_n * cols_n
    block_rows = shape[0] // blocks
    piece_rows = -(-block_rows // (group * 8)) * 8
    lanes = math.prod(shape[1:])
    padded = jnp.pad(value.reshape(blocks, block_rows, lanes), ((0, 0), (0, piece_rows * group - block_rows), (0, 0)))
    pieces = padded.reshape(blocks, rows_n, cols_n, piece_rows, lanes)
    half = blocks // 2
    first = pieces[:half].transpose(1, 2, 0, 3, 4)
    second = pieces[half:].transpose(2, 1, 0, 3, 4)
    first, second = exchange_many([(first, ("row",), False), (second, ("col",), False)], sizes, 4)
    first, second = exchange_many(
        [(first.sum(0), ("col",), False), (second.sum(0), ("row",), False)], sizes, 5
    )
    vmem = pl.BlockSpec(memory_space=pltpu.VMEM)
    sems = []
    for n in (blocks, group):
        sems += [pltpu.SemaphoreType.DMA((n - 1,)), pltpu.SemaphoreType.DMA((n - 1,)), pltpu.SemaphoreType.DMA]
    block = pl.pallas_call(
        functools.partial(tail_kernel, sizes=sizes),
        out_shape=jax.ShapeDtypeStruct((group, piece_rows, lanes), value.dtype),
        in_specs=[vmem, vmem],
        out_specs=vmem,
        scratch_shapes=[
            pltpu.VMEM((blocks, piece_rows, lanes), jnp.float32),
            pltpu.VMEM((blocks, piece_rows, lanes), jnp.float32),
            pltpu.VMEM((piece_rows, lanes), jnp.float32),
        ]
        + sems,
        compiler_params=pltpu.CompilerParams(collective_id=6, has_side_effects=True),
    )(first, second)
    return block.reshape(group * piece_rows, lanes)[:block_rows].reshape((block_rows,) + shape[1:])


def solution(mesh):
    placed = (
        P("dp", "row", "col", None),
        P("dp", "row", "col", None),
        P("dp", "row", "col", None),
        P(),
        P(),
    )
    sizes = dict(mesh.shape)
    return jax.shard_map(
        functools.partial(on_device, sizes=sizes),
        mesh=mesh,
        in_specs=placed,
        out_specs=(P("dp", None, None), P("dp", None, None)),
        check_vma=False,
    )
```

```python
import functools
import math

import jax
import jax.numpy as jnp
from jax import lax
from jax.experimental import pallas as pl
from jax.experimental.pallas import tpu as pltpu
from jax.sharding import PartitionSpec as P


def member_coords(j, axes, sizes):
    coords = {}
    for axis in reversed(axes):
        coords[axis] = lax.rem(j, sizes[axis])
        j = j // sizes[axis]
    return coords


def exchange_kernel(*refs, jobs, sizes):
    count = len(jobs)
    x_refs, o_refs = refs[:count], refs[count : 2 * count]
    sems = refs[2 * count :]
    barrier = pltpu.get_barrier_semaphore()
    plans = []
    total = 0
    for axes, gather in jobs:
        n = math.prod(sizes[a] for a in axes)
        me = 0
        for axis in axes:
            me = me * sizes[axis] + lax.axis_index(axis)
        for s in range(1, n):
            peer = member_coords(lax.rem(me + s, n), axes, sizes)
            pl.semaphore_signal(barrier, inc=1, device_id=peer, device_id_type=pl.DeviceIdType.MESH)
        total += n - 1
        plans.append((n, me))
    pl.semaphore_wait(barrier, total)
    copies, locals_ = [], []
    for job, ((axes, gather), (n, me)) in enumerate(zip(jobs, plans)):
        x_ref, o_ref = x_refs[job], o_refs[job]
        send_sem, recv_sem, local_sem = sems[3 * job : 3 * job + 3]
        for s in range(1, n):
            dst = lax.rem(me + s, n)
            copy = pltpu.make_async_remote_copy(
                src_ref=x_ref if gather else x_ref.at[dst],
                dst_ref=o_ref.at[me],
                send_sem=send_sem.at[s - 1],
                recv_sem=recv_sem.at[s - 1],
                device_id=member_coords(dst, axes, sizes),
                device_id_type=pl.DeviceIdType.MESH,
            )
            copy.start()
            copies.append(copy)
        local = pltpu.make_async_copy(x_ref if gather else x_ref.at[me], o_ref.at[me], local_sem)
        local.start()
        locals_.append(local)
    for copy in copies:
        copy.wait_send()
        copy.wait_recv()
    for local in locals_:
        local.wait()


def exchange_many(items, sizes, cid):
    jobs, shapes, scratch = [], [], []
    for x, axes, gather in items:
        n = math.prod(sizes[a] for a in axes)
        slab = x.shape if gather else x.shape[1:]
        jobs.append((axes, gather))
        shapes.append(jax.ShapeDtypeStruct((n,) + slab, x.dtype))
        scratch += [
            pltpu.SemaphoreType.DMA((max(n - 1, 1),)),
            pltpu.SemaphoreType.DMA((max(n - 1, 1),)),
            pltpu.SemaphoreType.DMA,
        ]
    return pl.pallas_call(
        functools.partial(exchange_kernel, jobs=tuple(jobs), sizes=sizes),
        out_shape=tuple(shapes),
        in_specs=[pl.BlockSpec(memory_space=pltpu.VMEM)] * len(items),
        out_specs=tuple(pl.BlockSpec(memory_space=pltpu.VMEM) for _ in items),
        scratch_shapes=scratch,
        compiler_params=pltpu.CompilerParams(
            collective_id=cid, has_side_effects=True, vmem_limit_bytes=48 * 1024 * 1024
        ),
    )(*[x for x, _, _ in items])


def exchange(x, axes, sizes, cid, gather=False):
    return exchange_many([(x, axes, gather)], sizes, cid)[0]


HALO_MOVES = ((1, 0), (-1, 0), (0, 1), (0, -1), (1, 1), (1, -1), (-1, 1), (-1, -1))


def halo_kernel(*refs, sizes):
    sends, recvs = refs[:3], refs[3:6]
    send_sem, recv_sem = refs[6:8]
    row, col = lax.axis_index("row"), lax.axis_index("col")

    def target(dr, dc):
        return {"row": lax.rem(row + dr + sizes["row"], sizes["row"]), "col": lax.rem(col + dc + sizes["col"], sizes["col"])}

    barrier = pltpu.get_barrier_semaphore()
    for dr, dc in HALO_MOVES:
        pl.semaphore_signal(barrier, inc=1, device_id=target(dr, dc), device_id_type=pl.DeviceIdType.MESH)
    pl.semaphore_wait(barrier, len(HALO_MOVES))
    copies = []
    for k, (dr, dc) in enumerate(HALO_MOVES):
        kind, slot = (0, k) if k < 2 else ((1, k - 2) if k < 4 else (2, k - 4))
        copy = pltpu.make_async_remote_copy(
            src_ref=sends[kind].at[slot],
            dst_ref=recvs[kind].at[slot],
            send_sem=send_sem.at[k],
            recv_sem=recv_sem.at[k],
            device_id=target(dr, dc),
            device_id_type=pl.DeviceIdType.MESH,
        )
        copy.start()
        copies.append(copy)
    for copy in copies:
        copy.wait_send()
        copy.wait_recv()


def padded_pair(tiles, sizes):
    rows_out = jnp.stack([tiles[:, -1], tiles[:, 0]])
    cols_out = jnp.stack([tiles[:, :, -1], tiles[:, :, 0]])
    corners_out = jnp.stack([tiles[:, -1, -1], tiles[:, -1, 0], tiles[:, 0, -1], tiles[:, 0, 0]])
    sends = (rows_out, cols_out, corners_out)
    recvs = pl.pallas_call(
        functools.partial(halo_kernel, sizes=sizes),
        out_shape=tuple(jax.ShapeDtypeStruct(x.shape, x.dtype) for x in sends),
        in_specs=[pl.BlockSpec(memory_space=pltpu.VMEM)] * 3,
        out_specs=tuple(pl.BlockSpec(memory_space=pltpu.VMEM) for _ in sends),
        scratch_shapes=[pltpu.SemaphoreType.DMA((len(HALO_MOVES),)), pltpu.SemaphoreType.DMA((len(HALO_MOVES),))],
        compiler_params=pltpu.CompilerParams(collective_id=8, has_side_effects=True),
    )(*sends)
    rows_in, cols_in, corners_in = recvs
    row, col = lax.axis_index("row"), lax.axis_index("col")
    up, down = row > 0, row < sizes["row"] - 1
    left, right = col > 0, col < sizes["col"] - 1
    zero = jnp.zeros((), tiles.dtype)
    top = jnp.where(up, rows_in[0], zero)
    bottom = jnp.where(down, rows_in[1], zero)
    west = jnp.where(left, cols_in[0], zero)
    east = jnp.where(right, cols_in[1], zero)
    top_left = jnp.where(up & left, corners_in[0], zero)
    top_right = jnp.where(up & right, corners_in[1], zero)
    bottom_left = jnp.where(down & left, corners_in[2], zero)
    bottom_right = jnp.where(down & right, corners_in[3], zero)
    first = jnp.concatenate([top_left[:, None], top, top_right[:, None]], axis=1)
    middle = jnp.concatenate([west[:, :, None], tiles, east[:, :, None]], axis=2)
    last = jnp.concatenate([bottom_left[:, None], bottom, bottom_right[:, None]], axis=1)
    return jnp.concatenate([first[:, None], middle, last[:, None]], axis=1)


def silu_slope(pre_float):
    sigma = jax.nn.sigmoid(pre_float)
    return sigma * (1.0 + pre_float * (1.0 - sigma))


def exact_dot(left, right, contract):
    return lax.dot_general(
        left.astype(jnp.float32),
        right.astype(jnp.float32),
        (contract, ((), ())),
        precision=lax.Precision.HIGHEST,
        preferred_element_type=jnp.float32,
    )


TAPS = [(a, b) for a in (-1, 0, 1) for b in (-1, 0, 1)]


def on_device(x_input, pre_act, out_grad, conv_weight, q_prev, sizes):
    height, breadth, channels = (x_input.shape[1], x_input.shape[2], x_input.shape[3])
    pixels = height * breadth
    rank = q_prev.shape[2]
    taps = len(TAPS)
    pre_float = pre_act.reshape(pixels, channels).astype(jnp.float32)
    hidden = jax.nn.silu(pre_float).astype(jnp.bfloat16)
    both_pad = padded_pair(
        jnp.stack([out_grad.reshape(height, breadth, channels), x_input.reshape(height, breadth, channels)]), sizes
    )
    grad_pad, input_pad = both_pad[0], both_pad[1]
    back_grad = jnp.zeros((pixels, channels), jnp.float32)
    for a, b in TAPS:
        window = grad_pad[1 - a : 1 - a + height, 1 - b : 1 - b + breadth].reshape(pixels, channels)
        back_grad = back_grad + lax.dot_general(
            window, conv_weight[a + 1, b + 1], (((1,), (1,)), ((), ())), preferred_element_type=jnp.float32
        )
    pre_grad = (back_grad * silu_slope(pre_float)).astype(jnp.bfloat16)

    grid = (height + 2, breadth + 2)
    grad_flat = grad_pad.reshape(-1, channels)
    input_flat = input_pad.reshape(-1, channels)
    q_taps = q_prev.reshape(taps, channels, 2, rank).transpose(2, 1, 0, 3).reshape(2, channels, taps * rank)

    first_terms = exact_dot(input_flat, q_taps[0], ((1,), (0,))).reshape(grid + (taps, rank))
    first_sum = sum(
        first_terms[1 + a : 1 + a + height, 1 + b : 1 + b + breadth, k] for k, (a, b) in enumerate(TAPS)
    ).reshape(pixels, rank)
    first_raw = exact_dot(pre_grad, first_sum, ((0,), (0,)))
    second_terms = exact_dot(hidden, q_taps[1], ((1,), (0,))).reshape(height, breadth, taps, rank)
    second_sum = sum(
        jnp.pad(second_terms[:, :, k], ((1 - a, 1 + a), (1 - b, 1 + b), (0, 0))) for k, (a, b) in enumerate(TAPS)
    ).reshape(-1, rank)
    second_raw = exact_dot(grad_flat, second_sum, ((0,), (0,)))

    power_raw = all_sum_small(jnp.stack([first_raw, second_raw], axis=1), sizes)

    first_image = exact_dot(pre_grad, power_raw[:, 0], ((1,), (0,))).reshape(height, breadth, rank)
    first_spread = jnp.concatenate(
        [
            jnp.pad(first_image, ((1 + a, 1 - a), (1 + b, 1 - b), (0, 0))).reshape(-1, rank)
            for a, b in TAPS
        ],
        axis=1,
    )
    first_rows = exact_dot(input_flat, first_spread, ((0,), (0,)))
    second_image = exact_dot(grad_flat, power_raw[:, 1], ((1,), (0,))).reshape(grid + (rank,))
    second_spread = jnp.concatenate(
        [
            second_image[1 - a : 1 - a + height, 1 - b : 1 - b + breadth].reshape(pixels, rank)
            for a, b in TAPS
        ],
        axis=1,
    )
    second_rows = exact_dot(hidden, second_spread, ((0,), (0,)))
    rows = jnp.stack([first_rows, second_rows]).reshape(2, channels, taps, rank)
    rows = rows.transpose(2, 1, 0, 3).reshape(taps * channels, 2, rank)
    row_block = block_sum(rows, sizes)

    gram = jnp.einsum(
        "mqn,mqg->qng", power_raw, power_raw, precision=lax.Precision.HIGHEST, preferred_element_type=jnp.float32
    )
    lower = jnp.linalg.cholesky(gram)
    basis_count = channels // sizes["dp"]
    raw_part = lax.dynamic_slice_in_dim(power_raw, lax.axis_index("dp") * basis_count, basis_count, 0)
    basis_out = lax.linalg.triangular_solve(
        lower, raw_part.transpose(1, 0, 2), left_side=False, lower=True, transpose_a=True
    ).transpose(1, 0, 2)
    factor_out = lax.linalg.triangular_solve(
        lower, row_block.transpose(1, 0, 2), left_side=False, lower=True, transpose_a=True
    ).transpose(1, 0, 2)
    return (basis_out, factor_out)


def allsum_kernel(p_ref, o_ref, recv1, send2, recv2, piece, recv3, chunk, *sems, sizes):
    group_axes, ring_axes = ("row", "col"), ("dp",)
    n_group = sizes["row"] * sizes["col"]
    n_ring = sizes["dp"]
    me_group = lax.axis_index("row") * sizes["col"] + lax.axis_index("col")
    me_ring = lax.axis_index("dp")
    barrier = pltpu.get_barrier_semaphore()
    for s in range(1, n_group):
        peer = member_coords(lax.rem(me_group + s, n_group), group_axes, sizes)
        pl.semaphore_signal(barrier, inc=1, device_id=peer, device_id_type=pl.DeviceIdType.MESH)
    for s in range(1, n_ring):
        peer = member_coords(lax.rem(me_ring + s, n_ring), ring_axes, sizes)
        pl.semaphore_signal(barrier, inc=1, device_id=peer, device_id_type=pl.DeviceIdType.MESH)
    pl.semaphore_wait(barrier, n_group - 1 + n_ring - 1)

    def phase(source, target, me, n, axes, send_sem, recv_sem, local_sem, gather):
        copies = []
        for s in range(1, n):
            dst = lax.rem(me + s, n)
            copy = pltpu.make_async_remote_copy(
                src_ref=source if gather else source.at[dst],
                dst_ref=target.at[me],
                send_sem=send_sem.at[s - 1],
                recv_sem=recv_sem.at[s - 1],
                device_id=member_coords(dst, axes, sizes),
                device_id_type=pl.DeviceIdType.MESH,
            )
            copy.start()
            copies.append(copy)
        local = pltpu.make_async_copy(source if gather else source.at[me], target.at[me], local_sem)
        local.start()
        for copy in copies:
            copy.wait_send()
            copy.wait_recv()
        local.wait()

    phase(p_ref, recv1, me_group, n_group, group_axes, sems[0], sems[1], sems[8], False)
    total = recv1[0]
    for j in range(1, n_group):
        total = total + recv1[j]
    for j in range(n_ring):
        send2[j] = total[j : j + 1]
    phase(send2, recv2, me_ring, n_ring, ring_axes, sems[2], sems[3], sems[9], False)
    reduced = recv2[0]
    for j in range(1, n_ring):
        reduced = reduced + recv2[j]
    piece[...] = reduced
    phase(piece, recv3, me_ring, n_ring, ring_axes, sems[4], sems[5], sems[10], True)
    for j in range(n_ring):
        chunk[j : j + 1] = recv3[j]
    phase(chunk, o_ref, me_group, n_group, group_axes, sems[6], sems[7], sems[11], True)


def all_sum_small(value, sizes):
    shape = value.shape
    n_group = sizes["row"] * sizes["col"]
    n_ring = sizes["dp"]
    width = value.size // (n_group * n_ring)
    parts = value.reshape(n_group, n_ring, width)
    vmem = pl.BlockSpec(memory_space=pltpu.VMEM)
    out = pl.pallas_call(
        functools.partial(allsum_kernel, sizes=sizes),
        out_shape=jax.ShapeDtypeStruct(parts.shape, parts.dtype),
        in_specs=[vmem],
        out_specs=vmem,
        scratch_shapes=[
            pltpu.VMEM((n_group, n_ring, width), jnp.float32),
            pltpu.VMEM((n_ring, 1, width), jnp.float32),
            pltpu.VMEM((n_ring, 1, width), jnp.float32),
            pltpu.VMEM((1, width), jnp.float32),
            pltpu.VMEM((n_ring, 1, width), jnp.float32),
            pltpu.VMEM((n_ring, width), jnp.float32),
        ]
        + [pltpu.SemaphoreType.DMA((n - 1,)) for n in (n_group, n_group, n_ring, n_ring, n_ring, n_ring, n_group, n_group)]
        + [pltpu.SemaphoreType.DMA] * 4,
        compiler_params=pltpu.CompilerParams(collective_id=0, has_side_effects=True),
    )(parts)
    return out.reshape(shape)


def permute_sum(value, axis, sizes):
    n = sizes[axis]
    me = lax.axis_index(axis)
    total = lax.dynamic_index_in_dim(value, me, 0, keepdims=False)
    for shift in range(1, n):
        slab = lax.dynamic_index_in_dim(value, lax.rem(me + shift, n), 0, keepdims=False)
        total = total + lax.ppermute(slab, axis, [(i, (i + shift) % n) for i in range(n)])
    return total


def block_sum(value, sizes):
    shape = value.shape
    blocks, rows_n, cols_n = sizes["dp"], sizes["row"], sizes["col"]
    group = rows_n * cols_n
    block_rows = shape[0] // blocks
    piece_rows = -(-block_rows // (group * 8)) * 8
    lanes = math.prod(shape[1:])
    padded = jnp.pad(value.reshape(blocks, block_rows, lanes), ((0, 0), (0, piece_rows * group - block_rows), (0, 0)))
    pieces = padded.reshape(blocks, rows_n, cols_n, piece_rows, lanes)
    half = blocks // 2
    first = pieces[:half].transpose(1, 2, 0, 3, 4)
    second = pieces[half:].transpose(2, 1, 0, 3, 4)
    first, second = permute_sum(first, "row", sizes), permute_sum(second, "col", sizes)
    first, second = exchange_many([(first, ("col",), False), (second, ("row",), False)], sizes, 5)
    pieces = jnp.concatenate([first.sum(0), second.sum(0)])
    piece = exchange(pieces, ("dp",), sizes, 6).sum(0)
    block = exchange(piece, ("row", "col"), sizes, 7, gather=True)
    return block.reshape(group * piece_rows, lanes)[:block_rows].reshape((block_rows,) + shape[1:])


def solution(mesh):
    placed = (
        P("dp", "row", "col", None),
        P("dp", "row", "col", None),
        P("dp", "row", "col", None),
        P(),
        P(),
    )
    sizes = dict(mesh.shape)
    return jax.shard_map(
        functools.partial(on_device, sizes=sizes),
        mesh=mesh,
        in_specs=placed,
        out_specs=(P("dp", None, None), P("dp", None, None)),
        check_vma=False,
    )
```

```python
import functools
import math

import jax
import jax.numpy as jnp
from jax import lax
from jax.experimental import pallas as pl
from jax.experimental.pallas import tpu as pltpu
from jax.sharding import PartitionSpec as P


def member_coords(j, axes, sizes):
    coords = {}
    for axis in reversed(axes):
        coords[axis] = lax.rem(j, sizes[axis])
        j = j // sizes[axis]
    return coords


def exchange_kernel(*refs, jobs, sizes):
    count = len(jobs)
    x_refs, o_refs = refs[:count], refs[count : 2 * count]
    sems = refs[2 * count :]
    barrier = pltpu.get_barrier_semaphore()
    plans = []
    total = 0
    for axes, gather in jobs:
        n = math.prod(sizes[a] for a in axes)
        me = 0
        for axis in axes:
            me = me * sizes[axis] + lax.axis_index(axis)
        for s in range(1, n):
            peer = member_coords(lax.rem(me + s, n), axes, sizes)
            pl.semaphore_signal(barrier, inc=1, device_id=peer, device_id_type=pl.DeviceIdType.MESH)
        total += n - 1
        plans.append((n, me))
    pl.semaphore_wait(barrier, total)
    copies, locals_ = [], []
    for job, ((axes, gather), (n, me)) in enumerate(zip(jobs, plans)):
        x_ref, o_ref = x_refs[job], o_refs[job]
        send_sem, recv_sem, local_sem = sems[3 * job : 3 * job + 3]
        for s in range(1, n):
            dst = lax.rem(me + s, n)
            copy = pltpu.make_async_remote_copy(
                src_ref=x_ref if gather else x_ref.at[dst],
                dst_ref=o_ref.at[me],
                send_sem=send_sem.at[s - 1],
                recv_sem=recv_sem.at[s - 1],
                device_id=member_coords(dst, axes, sizes),
                device_id_type=pl.DeviceIdType.MESH,
            )
            copy.start()
            copies.append(copy)
        local = pltpu.make_async_copy(x_ref if gather else x_ref.at[me], o_ref.at[me], local_sem)
        local.start()
        locals_.append(local)
    for copy in copies:
        copy.wait_send()
        copy.wait_recv()
    for local in locals_:
        local.wait()


def exchange_many(items, sizes, cid):
    jobs, shapes, scratch = [], [], []
    for x, axes, gather in items:
        n = math.prod(sizes[a] for a in axes)
        slab = x.shape if gather else x.shape[1:]
        jobs.append((axes, gather))
        shapes.append(jax.ShapeDtypeStruct((n,) + slab, x.dtype))
        scratch += [
            pltpu.SemaphoreType.DMA((max(n - 1, 1),)),
            pltpu.SemaphoreType.DMA((max(n - 1, 1),)),
            pltpu.SemaphoreType.DMA,
        ]
    return pl.pallas_call(
        functools.partial(exchange_kernel, jobs=tuple(jobs), sizes=sizes),
        out_shape=tuple(shapes),
        in_specs=[pl.BlockSpec(memory_space=pltpu.VMEM)] * len(items),
        out_specs=tuple(pl.BlockSpec(memory_space=pltpu.VMEM) for _ in items),
        scratch_shapes=scratch,
        compiler_params=pltpu.CompilerParams(
            collective_id=cid, has_side_effects=True, vmem_limit_bytes=48 * 1024 * 1024
        ),
    )(*[x for x, _, _ in items])


def exchange(x, axes, sizes, cid, gather=False):
    return exchange_many([(x, axes, gather)], sizes, cid)[0]


HALO_MOVES = ((1, 0), (-1, 0), (0, 1), (0, -1), (1, 1), (1, -1), (-1, 1), (-1, -1))


def halo_kernel(*refs, sizes):
    sends, recvs = refs[:3], refs[3:6]
    send_sem, recv_sem = refs[6:8]
    row, col = lax.axis_index("row"), lax.axis_index("col")

    def target(dr, dc):
        return {"row": lax.rem(row + dr + sizes["row"], sizes["row"]), "col": lax.rem(col + dc + sizes["col"], sizes["col"])}

    barrier = pltpu.get_barrier_semaphore()
    for dr, dc in HALO_MOVES:
        pl.semaphore_signal(barrier, inc=1, device_id=target(dr, dc), device_id_type=pl.DeviceIdType.MESH)
    pl.semaphore_wait(barrier, len(HALO_MOVES))
    copies = []
    for k, (dr, dc) in enumerate(HALO_MOVES):
        kind, slot = (0, k) if k < 2 else ((1, k - 2) if k < 4 else (2, k - 4))
        copy = pltpu.make_async_remote_copy(
            src_ref=sends[kind].at[slot],
            dst_ref=recvs[kind].at[slot],
            send_sem=send_sem.at[k],
            recv_sem=recv_sem.at[k],
            device_id=target(dr, dc),
            device_id_type=pl.DeviceIdType.MESH,
        )
        copy.start()
        copies.append(copy)
    for copy in copies:
        copy.wait_send()
        copy.wait_recv()


def padded_pair(tiles, sizes):
    rows_out = jnp.stack([tiles[:, -1], tiles[:, 0]])
    cols_out = jnp.stack([tiles[:, :, -1], tiles[:, :, 0]])
    corners_out = jnp.stack([tiles[:, -1, -1], tiles[:, -1, 0], tiles[:, 0, -1], tiles[:, 0, 0]])
    sends = (rows_out, cols_out, corners_out)
    recvs = pl.pallas_call(
        functools.partial(halo_kernel, sizes=sizes),
        out_shape=tuple(jax.ShapeDtypeStruct(x.shape, x.dtype) for x in sends),
        in_specs=[pl.BlockSpec(memory_space=pltpu.VMEM)] * 3,
        out_specs=tuple(pl.BlockSpec(memory_space=pltpu.VMEM) for _ in sends),
        scratch_shapes=[pltpu.SemaphoreType.DMA((len(HALO_MOVES),)), pltpu.SemaphoreType.DMA((len(HALO_MOVES),))],
        compiler_params=pltpu.CompilerParams(collective_id=8, has_side_effects=True),
    )(*sends)
    rows_in, cols_in, corners_in = recvs
    row, col = lax.axis_index("row"), lax.axis_index("col")
    up, down = row > 0, row < sizes["row"] - 1
    left, right = col > 0, col < sizes["col"] - 1
    zero = jnp.zeros((), tiles.dtype)
    top = jnp.where(up, rows_in[0], zero)
    bottom = jnp.where(down, rows_in[1], zero)
    west = jnp.where(left, cols_in[0], zero)
    east = jnp.where(right, cols_in[1], zero)
    top_left = jnp.where(up & left, corners_in[0], zero)
    top_right = jnp.where(up & right, corners_in[1], zero)
    bottom_left = jnp.where(down & left, corners_in[2], zero)
    bottom_right = jnp.where(down & right, corners_in[3], zero)
    first = jnp.concatenate([top_left[:, None], top, top_right[:, None]], axis=1)
    middle = jnp.concatenate([west[:, :, None], tiles, east[:, :, None]], axis=2)
    last = jnp.concatenate([bottom_left[:, None], bottom, bottom_right[:, None]], axis=1)
    return jnp.concatenate([first[:, None], middle, last[:, None]], axis=1)


def silu_slope(pre_float):
    sigma = jax.nn.sigmoid(pre_float)
    return sigma * (1.0 + pre_float * (1.0 - sigma))


def exact_dot(left, right, contract):
    return lax.dot_general(
        left.astype(jnp.float32),
        right.astype(jnp.float32),
        (contract, ((), ())),
        precision=lax.Precision.HIGHEST,
        preferred_element_type=jnp.float32,
    )


TAPS = [(a, b) for a in (-1, 0, 1) for b in (-1, 0, 1)]


def on_device(x_input, pre_act, out_grad, conv_weight, q_prev, sizes):
    height, breadth, channels = (x_input.shape[1], x_input.shape[2], x_input.shape[3])
    pixels = height * breadth
    rank = q_prev.shape[2]
    taps = len(TAPS)
    pre_float = pre_act.reshape(pixels, channels).astype(jnp.float32)
    hidden = jax.nn.silu(pre_float).astype(jnp.bfloat16)
    both_pad = padded_pair(
        jnp.stack([out_grad.reshape(height, breadth, channels), x_input.reshape(height, breadth, channels)]), sizes
    )
    grad_pad, input_pad = both_pad[0], both_pad[1]
    back_grad = jnp.zeros((pixels, channels), jnp.float32)
    for a, b in TAPS:
        window = grad_pad[1 - a : 1 - a + height, 1 - b : 1 - b + breadth].reshape(pixels, channels)
        back_grad = back_grad + lax.dot_general(
            window, conv_weight[a + 1, b + 1], (((1,), (1,)), ((), ())), preferred_element_type=jnp.float32
        )
    pre_grad = (back_grad * silu_slope(pre_float)).astype(jnp.bfloat16)

    grid = (height + 2, breadth + 2)
    grad_flat = grad_pad.reshape(-1, channels)
    input_flat = input_pad.reshape(-1, channels)
    q_taps = q_prev.reshape(taps, channels, 2, rank).transpose(2, 1, 0, 3).reshape(2, channels, taps * rank)

    first_terms = exact_dot(input_flat, q_taps[0], ((1,), (0,))).reshape(grid + (taps, rank))
    first_sum = sum(
        first_terms[1 + a : 1 + a + height, 1 + b : 1 + b + breadth, k] for k, (a, b) in enumerate(TAPS)
    ).reshape(pixels, rank)
    first_raw = exact_dot(pre_grad, first_sum, ((0,), (0,)))
    second_terms = exact_dot(hidden, q_taps[1], ((1,), (0,))).reshape(height, breadth, taps, rank)
    second_sum = sum(
        jnp.pad(second_terms[:, :, k], ((1 - a, 1 + a), (1 - b, 1 + b), (0, 0))) for k, (a, b) in enumerate(TAPS)
    ).reshape(-1, rank)
    second_raw = exact_dot(grad_flat, second_sum, ((0,), (0,)))

    power_raw = all_sum_small(jnp.stack([first_raw, second_raw], axis=1), sizes)

    first_image = exact_dot(pre_grad, power_raw[:, 0], ((1,), (0,))).reshape(height, breadth, rank)
    first_spread = jnp.concatenate(
        [
            jnp.pad(first_image, ((1 + a, 1 - a), (1 + b, 1 - b), (0, 0))).reshape(-1, rank)
            for a, b in TAPS
        ],
        axis=1,
    )
    first_rows = exact_dot(input_flat, first_spread, ((0,), (0,)))
    second_image = exact_dot(grad_flat, power_raw[:, 1], ((1,), (0,))).reshape(grid + (rank,))
    second_spread = jnp.concatenate(
        [
            second_image[1 - a : 1 - a + height, 1 - b : 1 - b + breadth].reshape(pixels, rank)
            for a, b in TAPS
        ],
        axis=1,
    )
    second_rows = exact_dot(hidden, second_spread, ((0,), (0,)))
    rows = jnp.stack([first_rows, second_rows]).reshape(2, channels, taps, rank)
    rows = rows.transpose(2, 1, 0, 3).reshape(taps * channels, 2, rank)
    row_block = block_sum(rows, sizes)

    gram = jnp.einsum(
        "mqn,mqg->qng", power_raw, power_raw, precision=lax.Precision.HIGHEST, preferred_element_type=jnp.float32
    )
    lower = jnp.linalg.cholesky(gram)
    basis_count = channels // sizes["dp"]
    raw_part = lax.dynamic_slice_in_dim(power_raw, lax.axis_index("dp") * basis_count, basis_count, 0)
    basis_out = lax.linalg.triangular_solve(
        lower, raw_part.transpose(1, 0, 2), left_side=False, lower=True, transpose_a=True
    ).transpose(1, 0, 2)
    factor_out = lax.linalg.triangular_solve(
        lower, row_block.transpose(1, 0, 2), left_side=False, lower=True, transpose_a=True
    ).transpose(1, 0, 2)
    return (basis_out, factor_out)


def allsum_kernel(p_ref, o_ref, recv1, send2, recv2, piece, recv3, chunk, *sems, sizes):
    group_axes, ring_axes = ("row", "col"), ("dp",)
    n_group = sizes["row"] * sizes["col"]
    n_ring = sizes["dp"]
    me_group = lax.axis_index("row") * sizes["col"] + lax.axis_index("col")
    me_ring = lax.axis_index("dp")
    barrier = pltpu.get_barrier_semaphore()
    for s in range(1, n_group):
        peer = member_coords(lax.rem(me_group + s, n_group), group_axes, sizes)
        pl.semaphore_signal(barrier, inc=1, device_id=peer, device_id_type=pl.DeviceIdType.MESH)
    for s in range(1, n_ring):
        peer = member_coords(lax.rem(me_ring + s, n_ring), ring_axes, sizes)
        pl.semaphore_signal(barrier, inc=1, device_id=peer, device_id_type=pl.DeviceIdType.MESH)
    pl.semaphore_wait(barrier, n_group - 1 + n_ring - 1)

    def phase(source, target, me, n, axes, send_sem, recv_sem, local_sem, gather):
        copies = []
        for s in range(1, n):
            dst = lax.rem(me + s, n)
            copy = pltpu.make_async_remote_copy(
                src_ref=source if gather else source.at[dst],
                dst_ref=target.at[me],
                send_sem=send_sem.at[s - 1],
                recv_sem=recv_sem.at[s - 1],
                device_id=member_coords(dst, axes, sizes),
                device_id_type=pl.DeviceIdType.MESH,
            )
            copy.start()
            copies.append(copy)
        local = pltpu.make_async_copy(source if gather else source.at[me], target.at[me], local_sem)
        local.start()
        for copy in copies:
            copy.wait_send()
            copy.wait_recv()
        local.wait()

    phase(p_ref, recv1, me_group, n_group, group_axes, sems[0], sems[1], sems[8], False)
    total = recv1[0]
    for j in range(1, n_group):
        total = total + recv1[j]
    for j in range(n_ring):
        send2[j] = total[j : j + 1]
    phase(send2, recv2, me_ring, n_ring, ring_axes, sems[2], sems[3], sems[9], False)
    reduced = recv2[0]
    for j in range(1, n_ring):
        reduced = reduced + recv2[j]
    piece[...] = reduced
    phase(piece, recv3, me_ring, n_ring, ring_axes, sems[4], sems[5], sems[10], True)
    for j in range(n_ring):
        chunk[j : j + 1] = recv3[j]
    phase(chunk, o_ref, me_group, n_group, group_axes, sems[6], sems[7], sems[11], True)


def all_sum_small(value, sizes):
    shape = value.shape
    n_group = sizes["row"] * sizes["col"]
    n_ring = sizes["dp"]
    width = value.size // (n_group * n_ring)
    parts = value.reshape(n_group, n_ring, width)
    vmem = pl.BlockSpec(memory_space=pltpu.VMEM)
    out = pl.pallas_call(
        functools.partial(allsum_kernel, sizes=sizes),
        out_shape=jax.ShapeDtypeStruct(parts.shape, parts.dtype),
        in_specs=[vmem],
        out_specs=vmem,
        scratch_shapes=[
            pltpu.VMEM((n_group, n_ring, width), jnp.float32),
            pltpu.VMEM((n_ring, 1, width), jnp.float32),
            pltpu.VMEM((n_ring, 1, width), jnp.float32),
            pltpu.VMEM((1, width), jnp.float32),
            pltpu.VMEM((n_ring, 1, width), jnp.float32),
            pltpu.VMEM((n_ring, width), jnp.float32),
        ]
        + [pltpu.SemaphoreType.DMA((n - 1,)) for n in (n_group, n_group, n_ring, n_ring, n_ring, n_ring, n_group, n_group)]
        + [pltpu.SemaphoreType.DMA] * 4,
        compiler_params=pltpu.CompilerParams(collective_id=0, has_side_effects=True),
    )(parts)
    return out.reshape(shape)


def permute_sum(value, axis, sizes, dim):
    n = sizes[axis]
    me = lax.axis_index(axis)
    total = lax.dynamic_index_in_dim(value, me, dim, keepdims=False)
    for shift in range(1, n):
        slab = lax.dynamic_index_in_dim(value, lax.rem(me + shift, n), dim, keepdims=False)
        total = total + lax.ppermute(slab, axis, [(i, (i + shift) % n) for i in range(n)])
    return total


def block_sum(value, sizes):
    shape = value.shape
    blocks, rows_n, cols_n = sizes["dp"], sizes["row"], sizes["col"]
    group = rows_n * cols_n
    block_rows = shape[0] // blocks
    piece_rows = -(-block_rows // (group * 8)) * 8
    lanes = math.prod(shape[1:])
    padded = jnp.pad(value.reshape(blocks, block_rows, lanes), ((0, 0), (0, piece_rows * group - block_rows), (0, 0)))
    pieces = padded.reshape(blocks, rows_n, cols_n, piece_rows, lanes)
    half = blocks // 2
    first = permute_sum(pieces[:half], "row", sizes, 1).transpose(1, 0, 2, 3)
    second = permute_sum(pieces[half:], "col", sizes, 2).transpose(1, 0, 2, 3)
    first, second = exchange_many([(first, ("col",), False), (second, ("row",), False)], sizes, 5)
    pieces = jnp.concatenate([first.sum(0), second.sum(0)])
    piece = exchange(pieces, ("dp",), sizes, 6).sum(0)
    block = exchange(piece, ("row", "col"), sizes, 7, gather=True)
    return block.reshape(group * piece_rows, lanes)[:block_rows].reshape((block_rows,) + shape[1:])


def solution(mesh):
    placed = (
        P("dp", "row", "col", None),
        P("dp", "row", "col", None),
        P("dp", "row", "col", None),
        P(),
        P(),
    )
    sizes = dict(mesh.shape)
    return jax.shard_map(
        functools.partial(on_device, sizes=sizes),
        mesh=mesh,
        in_specs=placed,
        out_specs=(P("dp", None, None), P("dp", None, None)),
        check_vma=False,
    )
```

```python
import functools
import math

import jax
import jax.numpy as jnp
from jax import lax
from jax.experimental import pallas as pl
from jax.experimental.pallas import tpu as pltpu
from jax.sharding import PartitionSpec as P


def member_coords(j, axes, sizes):
    coords = {}
    for axis in reversed(axes):
        coords[axis] = lax.rem(j, sizes[axis])
        j = j // sizes[axis]
    return coords


def exchange_kernel(*refs, jobs, sizes):
    count = len(jobs)
    x_refs, o_refs = refs[:count], refs[count : 2 * count]
    sems = refs[2 * count :]
    barrier = pltpu.get_barrier_semaphore()
    plans = []
    total = 0
    for axes, gather in jobs:
        n = math.prod(sizes[a] for a in axes)
        me = 0
        for axis in axes:
            me = me * sizes[axis] + lax.axis_index(axis)
        for s in range(1, n):
            peer = member_coords(lax.rem(me + s, n), axes, sizes)
            pl.semaphore_signal(barrier, inc=1, device_id=peer, device_id_type=pl.DeviceIdType.MESH)
        total += n - 1
        plans.append((n, me))
    pl.semaphore_wait(barrier, total)
    copies, locals_ = [], []
    for job, ((axes, gather), (n, me)) in enumerate(zip(jobs, plans)):
        x_ref, o_ref = x_refs[job], o_refs[job]
        send_sem, recv_sem, local_sem = sems[3 * job : 3 * job + 3]
        for s in range(1, n):
            dst = lax.rem(me + s, n)
            copy = pltpu.make_async_remote_copy(
                src_ref=x_ref if gather else x_ref.at[dst],
                dst_ref=o_ref.at[me],
                send_sem=send_sem.at[s - 1],
                recv_sem=recv_sem.at[s - 1],
                device_id=member_coords(dst, axes, sizes),
                device_id_type=pl.DeviceIdType.MESH,
            )
            copy.start()
            copies.append(copy)
        local = pltpu.make_async_copy(x_ref if gather else x_ref.at[me], o_ref.at[me], local_sem)
        local.start()
        locals_.append(local)
    for copy in copies:
        copy.wait_send()
        copy.wait_recv()
    for local in locals_:
        local.wait()


def exchange_many(items, sizes, cid):
    jobs, shapes, scratch = [], [], []
    for x, axes, gather in items:
        n = math.prod(sizes[a] for a in axes)
        slab = x.shape if gather else x.shape[1:]
        jobs.append((axes, gather))
        shapes.append(jax.ShapeDtypeStruct((n,) + slab, x.dtype))
        scratch += [
            pltpu.SemaphoreType.DMA((max(n - 1, 1),)),
            pltpu.SemaphoreType.DMA((max(n - 1, 1),)),
            pltpu.SemaphoreType.DMA,
        ]
    return pl.pallas_call(
        functools.partial(exchange_kernel, jobs=tuple(jobs), sizes=sizes),
        out_shape=tuple(shapes),
        in_specs=[pl.BlockSpec(memory_space=pltpu.VMEM)] * len(items),
        out_specs=tuple(pl.BlockSpec(memory_space=pltpu.VMEM) for _ in items),
        scratch_shapes=scratch,
        compiler_params=pltpu.CompilerParams(
            collective_id=cid, has_side_effects=True, vmem_limit_bytes=48 * 1024 * 1024
        ),
    )(*[x for x, _, _ in items])


def exchange(x, axes, sizes, cid, gather=False):
    return exchange_many([(x, axes, gather)], sizes, cid)[0]


HALO_MOVES = ((1, 0), (-1, 0), (0, 1), (0, -1), (1, 1), (1, -1), (-1, 1), (-1, -1))


def halo_kernel(*refs, sizes):
    sends, recvs = refs[:3], refs[3:6]
    send_sem, recv_sem = refs[6:8]
    row, col = lax.axis_index("row"), lax.axis_index("col")

    def target(dr, dc):
        return {"row": lax.rem(row + dr + sizes["row"], sizes["row"]), "col": lax.rem(col + dc + sizes["col"], sizes["col"])}

    barrier = pltpu.get_barrier_semaphore()
    for dr, dc in HALO_MOVES:
        pl.semaphore_signal(barrier, inc=1, device_id=target(dr, dc), device_id_type=pl.DeviceIdType.MESH)
    pl.semaphore_wait(barrier, len(HALO_MOVES))
    copies = []
    for k, (dr, dc) in enumerate(HALO_MOVES):
        kind, slot = (0, k) if k < 2 else ((1, k - 2) if k < 4 else (2, k - 4))
        copy = pltpu.make_async_remote_copy(
            src_ref=sends[kind].at[slot],
            dst_ref=recvs[kind].at[slot],
            send_sem=send_sem.at[k],
            recv_sem=recv_sem.at[k],
            device_id=target(dr, dc),
            device_id_type=pl.DeviceIdType.MESH,
        )
        copy.start()
        copies.append(copy)
    for copy in copies:
        copy.wait_send()
        copy.wait_recv()


def padded_pair(tiles, sizes):
    rows_out = jnp.stack([tiles[:, -1], tiles[:, 0]])
    cols_out = jnp.stack([tiles[:, :, -1], tiles[:, :, 0]])
    corners_out = jnp.stack([tiles[:, -1, -1], tiles[:, -1, 0], tiles[:, 0, -1], tiles[:, 0, 0]])
    sends = (rows_out, cols_out, corners_out)
    recvs = pl.pallas_call(
        functools.partial(halo_kernel, sizes=sizes),
        out_shape=tuple(jax.ShapeDtypeStruct(x.shape, x.dtype) for x in sends),
        in_specs=[pl.BlockSpec(memory_space=pltpu.VMEM)] * 3,
        out_specs=tuple(pl.BlockSpec(memory_space=pltpu.VMEM) for _ in sends),
        scratch_shapes=[pltpu.SemaphoreType.DMA((len(HALO_MOVES),)), pltpu.SemaphoreType.DMA((len(HALO_MOVES),))],
        compiler_params=pltpu.CompilerParams(collective_id=8, has_side_effects=True),
    )(*sends)
    rows_in, cols_in, corners_in = recvs
    row, col = lax.axis_index("row"), lax.axis_index("col")
    up, down = row > 0, row < sizes["row"] - 1
    left, right = col > 0, col < sizes["col"] - 1
    zero = jnp.zeros((), tiles.dtype)
    top = jnp.where(up, rows_in[0], zero)
    bottom = jnp.where(down, rows_in[1], zero)
    west = jnp.where(left, cols_in[0], zero)
    east = jnp.where(right, cols_in[1], zero)
    top_left = jnp.where(up & left, corners_in[0], zero)
    top_right = jnp.where(up & right, corners_in[1], zero)
    bottom_left = jnp.where(down & left, corners_in[2], zero)
    bottom_right = jnp.where(down & right, corners_in[3], zero)
    first = jnp.concatenate([top_left[:, None], top, top_right[:, None]], axis=1)
    middle = jnp.concatenate([west[:, :, None], tiles, east[:, :, None]], axis=2)
    last = jnp.concatenate([bottom_left[:, None], bottom, bottom_right[:, None]], axis=1)
    return jnp.concatenate([first[:, None], middle, last[:, None]], axis=1)


def silu_slope(pre_float):
    sigma = jax.nn.sigmoid(pre_float)
    return sigma * (1.0 + pre_float * (1.0 - sigma))


def exact_dot(left, right, contract):
    return lax.dot_general(
        left.astype(jnp.float32),
        right.astype(jnp.float32),
        (contract, ((), ())),
        precision=lax.Precision.HIGHEST,
        preferred_element_type=jnp.float32,
    )


TAPS = [(a, b) for a in (-1, 0, 1) for b in (-1, 0, 1)]


def on_device(x_input, pre_act, out_grad, conv_weight, q_prev, sizes):
    height, breadth, channels = (x_input.shape[1], x_input.shape[2], x_input.shape[3])
    pixels = height * breadth
    rank = q_prev.shape[2]
    taps = len(TAPS)
    pre_float = pre_act.reshape(pixels, channels).astype(jnp.float32)
    hidden = jax.nn.silu(pre_float).astype(jnp.bfloat16)
    both_pad = padded_pair(
        jnp.stack([out_grad.reshape(height, breadth, channels), x_input.reshape(height, breadth, channels)]), sizes
    )
    grad_pad, input_pad = both_pad[0], both_pad[1]
    back_grad = jnp.zeros((pixels, channels), jnp.float32)
    for a, b in TAPS:
        window = grad_pad[1 - a : 1 - a + height, 1 - b : 1 - b + breadth].reshape(pixels, channels)
        back_grad = back_grad + lax.dot_general(
            window, conv_weight[a + 1, b + 1], (((1,), (1,)), ((), ())), preferred_element_type=jnp.float32
        )
    pre_grad = (back_grad * silu_slope(pre_float)).astype(jnp.bfloat16)

    grid = (height + 2, breadth + 2)
    grad_flat = grad_pad.reshape(-1, channels)
    input_flat = input_pad.reshape(-1, channels)
    q_taps = q_prev.reshape(taps, channels, 2, rank).transpose(2, 1, 0, 3).reshape(2, channels, taps * rank)

    first_terms = exact_dot(input_flat, q_taps[0], ((1,), (0,))).reshape(grid + (taps, rank))
    first_sum = sum(
        first_terms[1 + a : 1 + a + height, 1 + b : 1 + b + breadth, k] for k, (a, b) in enumerate(TAPS)
    ).reshape(pixels, rank)
    first_raw = exact_dot(pre_grad, first_sum, ((0,), (0,)))
    second_terms = exact_dot(hidden, q_taps[1], ((1,), (0,))).reshape(height, breadth, taps, rank)
    second_sum = sum(
        jnp.pad(second_terms[:, :, k], ((1 - a, 1 + a), (1 - b, 1 + b), (0, 0))) for k, (a, b) in enumerate(TAPS)
    ).reshape(-1, rank)
    second_raw = exact_dot(grad_flat, second_sum, ((0,), (0,)))

    power_raw = all_sum_small(jnp.stack([first_raw, second_raw], axis=1), sizes)

    first_image = exact_dot(pre_grad, power_raw[:, 0], ((1,), (0,))).reshape(height, breadth, rank)
    first_spread = jnp.concatenate(
        [
            jnp.pad(first_image, ((1 + a, 1 - a), (1 + b, 1 - b), (0, 0))).reshape(-1, rank)
            for a, b in TAPS
        ],
        axis=1,
    )
    first_rows = exact_dot(input_flat, first_spread, ((0,), (0,)))
    second_image = exact_dot(grad_flat, power_raw[:, 1], ((1,), (0,))).reshape(grid + (rank,))
    second_spread = jnp.concatenate(
        [
            second_image[1 - a : 1 - a + height, 1 - b : 1 - b + breadth].reshape(pixels, rank)
            for a, b in TAPS
        ],
        axis=1,
    )
    second_rows = exact_dot(hidden, second_spread, ((0,), (0,)))
    rows = jnp.concatenate(
        [
            first_rows.reshape(channels, taps, rank).transpose(1, 0, 2),
            second_rows.reshape(channels, taps, rank).transpose(1, 0, 2),
        ],
        axis=-1,
    ).reshape(taps * channels, 2, rank)
    row_block = block_sum(rows, sizes)

    gram = jnp.einsum(
        "mqn,mqg->qng", power_raw, power_raw, precision=lax.Precision.HIGHEST, preferred_element_type=jnp.float32
    )
    lower = jnp.linalg.cholesky(gram)
    basis_count = channels // sizes["dp"]
    raw_part = lax.dynamic_slice_in_dim(power_raw, lax.axis_index("dp") * basis_count, basis_count, 0)
    basis_out = lax.linalg.triangular_solve(
        lower, raw_part.transpose(1, 0, 2), left_side=False, lower=True, transpose_a=True
    ).transpose(1, 0, 2)
    factor_out = lax.linalg.triangular_solve(
        lower, row_block.transpose(1, 0, 2), left_side=False, lower=True, transpose_a=True
    ).transpose(1, 0, 2)
    return (basis_out, factor_out)


def allsum_kernel(p_ref, o_ref, recv1, send2, recv2, piece, recv3, chunk, *sems, sizes):
    group_axes, ring_axes = ("row", "col"), ("dp",)
    n_group = sizes["row"] * sizes["col"]
    n_ring = sizes["dp"]
    me_group = lax.axis_index("row") * sizes["col"] + lax.axis_index("col")
    me_ring = lax.axis_index("dp")
    barrier = pltpu.get_barrier_semaphore()
    for s in range(1, n_group):
        peer = member_coords(lax.rem(me_group + s, n_group), group_axes, sizes)
        pl.semaphore_signal(barrier, inc=1, device_id=peer, device_id_type=pl.DeviceIdType.MESH)
    for s in range(1, n_ring):
        peer = member_coords(lax.rem(me_ring + s, n_ring), ring_axes, sizes)
        pl.semaphore_signal(barrier, inc=1, device_id=peer, device_id_type=pl.DeviceIdType.MESH)
    pl.semaphore_wait(barrier, n_group - 1 + n_ring - 1)

    def phase(source, target, me, n, axes, send_sem, recv_sem, local_sem, gather):
        copies = []
        for s in range(1, n):
            dst = lax.rem(me + s, n)
            copy = pltpu.make_async_remote_copy(
                src_ref=source if gather else source.at[dst],
                dst_ref=target.at[me],
                send_sem=send_sem.at[s - 1],
                recv_sem=recv_sem.at[s - 1],
                device_id=member_coords(dst, axes, sizes),
                device_id_type=pl.DeviceIdType.MESH,
            )
            copy.start()
            copies.append(copy)
        local = pltpu.make_async_copy(source if gather else source.at[me], target.at[me], local_sem)
        local.start()
        for copy in copies:
            copy.wait_send()
            copy.wait_recv()
        local.wait()

    phase(p_ref, recv1, me_group, n_group, group_axes, sems[0], sems[1], sems[8], False)
    total = recv1[0]
    for j in range(1, n_group):
        total = total + recv1[j]
    for j in range(n_ring):
        send2[j] = total[j : j + 1]
    phase(send2, recv2, me_ring, n_ring, ring_axes, sems[2], sems[3], sems[9], False)
    reduced = recv2[0]
    for j in range(1, n_ring):
        reduced = reduced + recv2[j]
    piece[...] = reduced
    phase(piece, recv3, me_ring, n_ring, ring_axes, sems[4], sems[5], sems[10], True)
    for j in range(n_ring):
        chunk[j : j + 1] = recv3[j]
    phase(chunk, o_ref, me_group, n_group, group_axes, sems[6], sems[7], sems[11], True)


def all_sum_small(value, sizes):
    shape = value.shape
    n_group = sizes["row"] * sizes["col"]
    n_ring = sizes["dp"]
    width = value.size // (n_group * n_ring)
    parts = value.reshape(n_group, n_ring, width)
    vmem = pl.BlockSpec(memory_space=pltpu.VMEM)
    out = pl.pallas_call(
        functools.partial(allsum_kernel, sizes=sizes),
        out_shape=jax.ShapeDtypeStruct(parts.shape, parts.dtype),
        in_specs=[vmem],
        out_specs=vmem,
        scratch_shapes=[
            pltpu.VMEM((n_group, n_ring, width), jnp.float32),
            pltpu.VMEM((n_ring, 1, width), jnp.float32),
            pltpu.VMEM((n_ring, 1, width), jnp.float32),
            pltpu.VMEM((1, width), jnp.float32),
            pltpu.VMEM((n_ring, 1, width), jnp.float32),
            pltpu.VMEM((n_ring, width), jnp.float32),
        ]
        + [pltpu.SemaphoreType.DMA((n - 1,)) for n in (n_group, n_group, n_ring, n_ring, n_ring, n_ring, n_group, n_group)]
        + [pltpu.SemaphoreType.DMA] * 4,
        compiler_params=pltpu.CompilerParams(collective_id=0, has_side_effects=True),
    )(parts)
    return out.reshape(shape)


def permute_sum(value, axis, sizes):
    n = sizes[axis]
    me = lax.axis_index(axis)
    total = lax.dynamic_index_in_dim(value, me, 0, keepdims=False)
    for shift in range(1, n):
        slab = lax.dynamic_index_in_dim(value, lax.rem(me + shift, n), 0, keepdims=False)
        total = total + lax.ppermute(slab, axis, [(i, (i + shift) % n) for i in range(n)])
    return total


def block_sum(value, sizes):
    shape = value.shape
    blocks, rows_n, cols_n = sizes["dp"], sizes["row"], sizes["col"]
    group = rows_n * cols_n
    block_rows = shape[0] // blocks
    piece_rows = -(-block_rows // (group * 8)) * 8
    lanes = math.prod(shape[1:])
    padded = jnp.pad(value.reshape(blocks, block_rows, lanes), ((0, 0), (0, piece_rows * group - block_rows), (0, 0)))
    pieces = padded.reshape(blocks, rows_n, cols_n, piece_rows, lanes)
    half = blocks // 2
    first = pieces[:half].transpose(1, 2, 0, 3, 4)
    second = pieces[half:].transpose(2, 1, 0, 3, 4)
    first, second = permute_sum(first, "row", sizes), permute_sum(second, "col", sizes)
    first, second = exchange_many([(first, ("col",), False), (second, ("row",), False)], sizes, 5)
    pieces = jnp.concatenate([first.sum(0), second.sum(0)])
    piece = exchange(pieces, ("dp",), sizes, 6).sum(0)
    block = exchange(piece, ("row", "col"), sizes, 7, gather=True)
    return block.reshape(group * piece_rows, lanes)[:block_rows].reshape((block_rows,) + shape[1:])


def solution(mesh):
    placed = (
        P("dp", "row", "col", None),
        P("dp", "row", "col", None),
        P("dp", "row", "col", None),
        P(),
        P(),
    )
    sizes = dict(mesh.shape)
    return jax.shard_map(
        functools.partial(on_device, sizes=sizes),
        mesh=mesh,
        in_specs=placed,
        out_specs=(P("dp", None, None), P("dp", None, None)),
        check_vma=False,
    )
```

```python
import functools
import math

import jax
import jax.numpy as jnp
from jax import lax
from jax.experimental import pallas as pl
from jax.experimental.pallas import tpu as pltpu
from jax.sharding import PartitionSpec as P


def member_coords(j, axes, sizes):
    coords = {}
    for axis in reversed(axes):
        coords[axis] = lax.rem(j, sizes[axis])
        j = j // sizes[axis]
    return coords


def exchange_kernel(*refs, jobs, sizes):
    count = len(jobs)
    x_refs, o_refs = refs[:count], refs[count : 2 * count]
    sems = refs[2 * count :]
    barrier = pltpu.get_barrier_semaphore()
    plans = []
    total = 0
    for axes, gather in jobs:
        n = math.prod(sizes[a] for a in axes)
        me = 0
        for axis in axes:
            me = me * sizes[axis] + lax.axis_index(axis)
        for s in range(1, n):
            peer = member_coords(lax.rem(me + s, n), axes, sizes)
            pl.semaphore_signal(barrier, inc=1, device_id=peer, device_id_type=pl.DeviceIdType.MESH)
        total += n - 1
        plans.append((n, me))
    pl.semaphore_wait(barrier, total)
    copies, locals_ = [], []
    for job, ((axes, gather), (n, me)) in enumerate(zip(jobs, plans)):
        x_ref, o_ref = x_refs[job], o_refs[job]
        send_sem, recv_sem, local_sem = sems[3 * job : 3 * job + 3]
        for s in range(1, n):
            dst = lax.rem(me + s, n)
            copy = pltpu.make_async_remote_copy(
                src_ref=x_ref if gather else x_ref.at[dst],
                dst_ref=o_ref.at[me],
                send_sem=send_sem.at[s - 1],
                recv_sem=recv_sem.at[s - 1],
                device_id=member_coords(dst, axes, sizes),
                device_id_type=pl.DeviceIdType.MESH,
            )
            copy.start()
            copies.append(copy)
        local = pltpu.make_async_copy(x_ref if gather else x_ref.at[me], o_ref.at[me], local_sem)
        local.start()
        locals_.append(local)
    for copy in copies:
        copy.wait_send()
        copy.wait_recv()
    for local in locals_:
        local.wait()


def exchange_many(items, sizes, cid):
    jobs, shapes, scratch = [], [], []
    for x, axes, gather in items:
        n = math.prod(sizes[a] for a in axes)
        slab = x.shape if gather else x.shape[1:]
        jobs.append((axes, gather))
        shapes.append(jax.ShapeDtypeStruct((n,) + slab, x.dtype))
        scratch += [
            pltpu.SemaphoreType.DMA((max(n - 1, 1),)),
            pltpu.SemaphoreType.DMA((max(n - 1, 1),)),
            pltpu.SemaphoreType.DMA,
        ]
    return pl.pallas_call(
        functools.partial(exchange_kernel, jobs=tuple(jobs), sizes=sizes),
        out_shape=tuple(shapes),
        in_specs=[pl.BlockSpec(memory_space=pltpu.VMEM)] * len(items),
        out_specs=tuple(pl.BlockSpec(memory_space=pltpu.VMEM) for _ in items),
        scratch_shapes=scratch,
        compiler_params=pltpu.CompilerParams(
            collective_id=cid, has_side_effects=True, vmem_limit_bytes=48 * 1024 * 1024
        ),
    )(*[x for x, _, _ in items])


def exchange(x, axes, sizes, cid, gather=False):
    return exchange_many([(x, axes, gather)], sizes, cid)[0]


HALO_MOVES = ((1, 0), (-1, 0), (0, 1), (0, -1), (1, 1), (1, -1), (-1, 1), (-1, -1))


def halo_kernel(*refs, sizes):
    sends, recvs = refs[:3], refs[3:6]
    send_sem, recv_sem = refs[6:8]
    row, col = lax.axis_index("row"), lax.axis_index("col")

    def target(dr, dc):
        return {"row": lax.rem(row + dr + sizes["row"], sizes["row"]), "col": lax.rem(col + dc + sizes["col"], sizes["col"])}

    barrier = pltpu.get_barrier_semaphore()
    for dr, dc in HALO_MOVES:
        pl.semaphore_signal(barrier, inc=1, device_id=target(dr, dc), device_id_type=pl.DeviceIdType.MESH)
    pl.semaphore_wait(barrier, len(HALO_MOVES))
    copies = []
    for k, (dr, dc) in enumerate(HALO_MOVES):
        kind, slot = (0, k) if k < 2 else ((1, k - 2) if k < 4 else (2, k - 4))
        copy = pltpu.make_async_remote_copy(
            src_ref=sends[kind].at[slot],
            dst_ref=recvs[kind].at[slot],
            send_sem=send_sem.at[k],
            recv_sem=recv_sem.at[k],
            device_id=target(dr, dc),
            device_id_type=pl.DeviceIdType.MESH,
        )
        copy.start()
        copies.append(copy)
    for copy in copies:
        copy.wait_send()
        copy.wait_recv()


def padded_pair(tiles, sizes):
    rows_out = jnp.stack([tiles[:, -1], tiles[:, 0]])
    cols_out = jnp.stack([tiles[:, :, -1], tiles[:, :, 0]])
    corners_out = jnp.stack([tiles[:, -1, -1], tiles[:, -1, 0], tiles[:, 0, -1], tiles[:, 0, 0]])
    sends = (rows_out, cols_out, corners_out)
    recvs = pl.pallas_call(
        functools.partial(halo_kernel, sizes=sizes),
        out_shape=tuple(jax.ShapeDtypeStruct(x.shape, x.dtype) for x in sends),
        in_specs=[pl.BlockSpec(memory_space=pltpu.VMEM)] * 3,
        out_specs=tuple(pl.BlockSpec(memory_space=pltpu.VMEM) for _ in sends),
        scratch_shapes=[pltpu.SemaphoreType.DMA((len(HALO_MOVES),)), pltpu.SemaphoreType.DMA((len(HALO_MOVES),))],
        compiler_params=pltpu.CompilerParams(collective_id=8, has_side_effects=True),
    )(*sends)
    rows_in, cols_in, corners_in = recvs
    row, col = lax.axis_index("row"), lax.axis_index("col")
    up, down = row > 0, row < sizes["row"] - 1
    left, right = col > 0, col < sizes["col"] - 1
    zero = jnp.zeros((), tiles.dtype)
    top = jnp.where(up, rows_in[0], zero)
    bottom = jnp.where(down, rows_in[1], zero)
    west = jnp.where(left, cols_in[0], zero)
    east = jnp.where(right, cols_in[1], zero)
    top_left = jnp.where(up & left, corners_in[0], zero)
    top_right = jnp.where(up & right, corners_in[1], zero)
    bottom_left = jnp.where(down & left, corners_in[2], zero)
    bottom_right = jnp.where(down & right, corners_in[3], zero)
    first = jnp.concatenate([top_left[:, None], top, top_right[:, None]], axis=1)
    middle = jnp.concatenate([west[:, :, None], tiles, east[:, :, None]], axis=2)
    last = jnp.concatenate([bottom_left[:, None], bottom, bottom_right[:, None]], axis=1)
    return jnp.concatenate([first[:, None], middle, last[:, None]], axis=1)


def silu_slope(pre_float):
    sigma = jax.nn.sigmoid(pre_float)
    return sigma * (1.0 + pre_float * (1.0 - sigma))


def exact_dot(left, right, contract):
    return lax.dot_general(
        left.astype(jnp.float32),
        right.astype(jnp.float32),
        (contract, ((), ())),
        precision=lax.Precision.HIGHEST,
        preferred_element_type=jnp.float32,
    )


TAPS = [(a, b) for a in (-1, 0, 1) for b in (-1, 0, 1)]


def on_device(x_input, pre_act, out_grad, conv_weight, q_prev, sizes):
    height, breadth, channels = (x_input.shape[1], x_input.shape[2], x_input.shape[3])
    pixels = height * breadth
    rank = q_prev.shape[2]
    taps = len(TAPS)
    pre_float = pre_act.reshape(pixels, channels).astype(jnp.float32)
    hidden = jax.nn.silu(pre_float).astype(jnp.bfloat16)
    both_pad = padded_pair(
        jnp.stack([out_grad.reshape(height, breadth, channels), x_input.reshape(height, breadth, channels)]), sizes
    )
    grad_pad, input_pad = both_pad[0], both_pad[1]
    back_grad = jnp.zeros((pixels, channels), jnp.float32)
    for a, b in TAPS:
        window = grad_pad[1 - a : 1 - a + height, 1 - b : 1 - b + breadth].reshape(pixels, channels)
        back_grad = back_grad + lax.dot_general(
            window, conv_weight[a + 1, b + 1], (((1,), (1,)), ((), ())), preferred_element_type=jnp.float32
        )
    pre_grad = (back_grad * silu_slope(pre_float)).astype(jnp.bfloat16)

    grid = (height + 2, breadth + 2)
    grad_flat = grad_pad.reshape(-1, channels)
    input_flat = input_pad.reshape(-1, channels)
    q_taps = q_prev.reshape(taps, channels, 2, rank).transpose(2, 1, 0, 3).reshape(2, channels, taps * rank)

    first_terms = exact_dot(input_flat, q_taps[0], ((1,), (0,))).reshape(grid + (taps * rank,))
    first_sum = sum(
        first_terms[1 + a : 1 + a + height, 1 + b : 1 + b + breadth, k * rank : (k + 1) * rank]
        for k, (a, b) in enumerate(TAPS)
    ).reshape(pixels, rank)
    first_raw = exact_dot(pre_grad, first_sum, ((0,), (0,)))
    second_terms = exact_dot(hidden, q_taps[1], ((1,), (0,))).reshape(height, breadth, taps * rank)
    second_sum = sum(
        jnp.pad(second_terms[:, :, k * rank : (k + 1) * rank], ((1 - a, 1 + a), (1 - b, 1 + b), (0, 0)))
        for k, (a, b) in enumerate(TAPS)
    ).reshape(-1, rank)
    second_raw = exact_dot(grad_flat, second_sum, ((0,), (0,)))

    power_raw = all_sum_small(jnp.stack([first_raw, second_raw], axis=1), sizes)

    first_image = exact_dot(pre_grad, power_raw[:, 0], ((1,), (0,))).reshape(height, breadth, rank)
    first_spread = jnp.concatenate(
        [
            jnp.pad(first_image, ((1 + a, 1 - a), (1 + b, 1 - b), (0, 0))).reshape(-1, rank)
            for a, b in TAPS
        ],
        axis=1,
    )
    first_rows = exact_dot(input_flat, first_spread, ((0,), (0,)))
    second_image = exact_dot(grad_flat, power_raw[:, 1], ((1,), (0,))).reshape(grid + (rank,))
    second_spread = jnp.concatenate(
        [
            second_image[1 - a : 1 - a + height, 1 - b : 1 - b + breadth].reshape(pixels, rank)
            for a, b in TAPS
        ],
        axis=1,
    )
    second_rows = exact_dot(hidden, second_spread, ((0,), (0,)))
    rows = jnp.concatenate(
        [
            first_rows.reshape(channels, taps, rank).transpose(1, 0, 2),
            second_rows.reshape(channels, taps, rank).transpose(1, 0, 2),
        ],
        axis=-1,
    ).reshape(taps * channels, 2, rank)
    row_block = block_sum(rows, sizes)

    gram = jnp.einsum(
        "mqn,mqg->qng", power_raw, power_raw, precision=lax.Precision.HIGHEST, preferred_element_type=jnp.float32
    )
    lower = jnp.linalg.cholesky(gram)
    basis_count = channels // sizes["dp"]
    raw_part = lax.dynamic_slice_in_dim(power_raw, lax.axis_index("dp") * basis_count, basis_count, 0)
    basis_out = lax.linalg.triangular_solve(
        lower, raw_part.transpose(1, 0, 2), left_side=False, lower=True, transpose_a=True
    ).transpose(1, 0, 2)
    factor_out = lax.linalg.triangular_solve(
        lower, row_block.transpose(1, 0, 2), left_side=False, lower=True, transpose_a=True
    ).transpose(1, 0, 2)
    return (basis_out, factor_out)


def allsum_kernel(p_ref, o_ref, recv1, send2, recv2, piece, recv3, chunk, *sems, sizes):
    group_axes, ring_axes = ("row", "col"), ("dp",)
    n_group = sizes["row"] * sizes["col"]
    n_ring = sizes["dp"]
    me_group = lax.axis_index("row") * sizes["col"] + lax.axis_index("col")
    me_ring = lax.axis_index("dp")
    barrier = pltpu.get_barrier_semaphore()
    for s in range(1, n_group):
        peer = member_coords(lax.rem(me_group + s, n_group), group_axes, sizes)
        pl.semaphore_signal(barrier, inc=1, device_id=peer, device_id_type=pl.DeviceIdType.MESH)
    for s in range(1, n_ring):
        peer = member_coords(lax.rem(me_ring + s, n_ring), ring_axes, sizes)
        pl.semaphore_signal(barrier, inc=1, device_id=peer, device_id_type=pl.DeviceIdType.MESH)
    pl.semaphore_wait(barrier, n_group - 1 + n_ring - 1)

    def phase(source, target, me, n, axes, send_sem, recv_sem, local_sem, gather):
        copies = []
        for s in range(1, n):
            dst = lax.rem(me + s, n)
            copy = pltpu.make_async_remote_copy(
                src_ref=source if gather else source.at[dst],
                dst_ref=target.at[me],
                send_sem=send_sem.at[s - 1],
                recv_sem=recv_sem.at[s - 1],
                device_id=member_coords(dst, axes, sizes),
                device_id_type=pl.DeviceIdType.MESH,
            )
            copy.start()
            copies.append(copy)
        local = pltpu.make_async_copy(source if gather else source.at[me], target.at[me], local_sem)
        local.start()
        for copy in copies:
            copy.wait_send()
            copy.wait_recv()
        local.wait()

    phase(p_ref, recv1, me_group, n_group, group_axes, sems[0], sems[1], sems[8], False)
    total = recv1[0]
    for j in range(1, n_group):
        total = total + recv1[j]
    for j in range(n_ring):
        send2[j] = total[j : j + 1]
    phase(send2, recv2, me_ring, n_ring, ring_axes, sems[2], sems[3], sems[9], False)
    reduced = recv2[0]
    for j in range(1, n_ring):
        reduced = reduced + recv2[j]
    piece[...] = reduced
    phase(piece, recv3, me_ring, n_ring, ring_axes, sems[4], sems[5], sems[10], True)
    for j in range(n_ring):
        chunk[j : j + 1] = recv3[j]
    phase(chunk, o_ref, me_group, n_group, group_axes, sems[6], sems[7], sems[11], True)


def all_sum_small(value, sizes):
    shape = value.shape
    n_group = sizes["row"] * sizes["col"]
    n_ring = sizes["dp"]
    width = value.size // (n_group * n_ring)
    parts = value.reshape(n_group, n_ring, width)
    vmem = pl.BlockSpec(memory_space=pltpu.VMEM)
    out = pl.pallas_call(
        functools.partial(allsum_kernel, sizes=sizes),
        out_shape=jax.ShapeDtypeStruct(parts.shape, parts.dtype),
        in_specs=[vmem],
        out_specs=vmem,
        scratch_shapes=[
            pltpu.VMEM((n_group, n_ring, width), jnp.float32),
            pltpu.VMEM((n_ring, 1, width), jnp.float32),
            pltpu.VMEM((n_ring, 1, width), jnp.float32),
            pltpu.VMEM((1, width), jnp.float32),
            pltpu.VMEM((n_ring, 1, width), jnp.float32),
            pltpu.VMEM((n_ring, width), jnp.float32),
        ]
        + [pltpu.SemaphoreType.DMA((n - 1,)) for n in (n_group, n_group, n_ring, n_ring, n_ring, n_ring, n_group, n_group)]
        + [pltpu.SemaphoreType.DMA] * 4,
        compiler_params=pltpu.CompilerParams(collective_id=0, has_side_effects=True),
    )(parts)
    return out.reshape(shape)


def permute_sum(value, axis, sizes):
    n = sizes[axis]
    me = lax.axis_index(axis)
    total = lax.dynamic_index_in_dim(value, me, 0, keepdims=False)
    for shift in range(1, n):
        slab = lax.dynamic_index_in_dim(value, lax.rem(me + shift, n), 0, keepdims=False)
        total = total + lax.ppermute(slab, axis, [(i, (i + shift) % n) for i in range(n)])
    return total


def block_sum(value, sizes):
    shape = value.shape
    blocks, rows_n, cols_n = sizes["dp"], sizes["row"], sizes["col"]
    group = rows_n * cols_n
    block_rows = shape[0] // blocks
    piece_rows = -(-block_rows // (group * 8)) * 8
    lanes = math.prod(shape[1:])
    padded = jnp.pad(value.reshape(blocks, block_rows, lanes), ((0, 0), (0, piece_rows * group - block_rows), (0, 0)))
    pieces = padded.reshape(blocks, rows_n, cols_n, piece_rows, lanes)
    half = blocks // 2
    first = pieces[:half].transpose(1, 2, 0, 3, 4)
    second = pieces[half:].transpose(2, 1, 0, 3, 4)
    first, second = permute_sum(first, "row", sizes), permute_sum(second, "col", sizes)
    first, second = exchange_many([(first, ("col",), False), (second, ("row",), False)], sizes, 5)
    pieces = jnp.concatenate([first.sum(0), second.sum(0)])
    piece = exchange(pieces, ("dp",), sizes, 6).sum(0)
    block = exchange(piece, ("row", "col"), sizes, 7, gather=True)
    return block.reshape(group * piece_rows, lanes)[:block_rows].reshape((block_rows,) + shape[1:])


def solution(mesh):
    placed = (
        P("dp", "row", "col", None),
        P("dp", "row", "col", None),
        P("dp", "row", "col", None),
        P(),
        P(),
    )
    sizes = dict(mesh.shape)
    return jax.shard_map(
        functools.partial(on_device, sizes=sizes),
        mesh=mesh,
        in_specs=placed,
        out_specs=(P("dp", None, None), P("dp", None, None)),
        check_vma=False,
    )
```

```python
import functools
import math

import jax
import jax.numpy as jnp
from jax import lax
from jax.experimental import pallas as pl
from jax.experimental.pallas import tpu as pltpu
from jax.sharding import PartitionSpec as P


def member_coords(j, axes, sizes):
    coords = {}
    for axis in reversed(axes):
        coords[axis] = lax.rem(j, sizes[axis])
        j = j // sizes[axis]
    return coords


def exchange_kernel(*refs, jobs, sizes):
    count = len(jobs)
    x_refs, o_refs = refs[:count], refs[count : 2 * count]
    sems = refs[2 * count :]
    barrier = pltpu.get_barrier_semaphore()
    plans = []
    total = 0
    for axes, gather in jobs:
        n = math.prod(sizes[a] for a in axes)
        me = 0
        for axis in axes:
            me = me * sizes[axis] + lax.axis_index(axis)
        for s in range(1, n):
            peer = member_coords(lax.rem(me + s, n), axes, sizes)
            pl.semaphore_signal(barrier, inc=1, device_id=peer, device_id_type=pl.DeviceIdType.MESH)
        total += n - 1
        plans.append((n, me))
    pl.semaphore_wait(barrier, total)
    copies, locals_ = [], []
    for job, ((axes, gather), (n, me)) in enumerate(zip(jobs, plans)):
        x_ref, o_ref = x_refs[job], o_refs[job]
        send_sem, recv_sem, local_sem = sems[3 * job : 3 * job + 3]
        for s in range(1, n):
            dst = lax.rem(me + s, n)
            copy = pltpu.make_async_remote_copy(
                src_ref=x_ref if gather else x_ref.at[dst],
                dst_ref=o_ref.at[me],
                send_sem=send_sem.at[s - 1],
                recv_sem=recv_sem.at[s - 1],
                device_id=member_coords(dst, axes, sizes),
                device_id_type=pl.DeviceIdType.MESH,
            )
            copy.start()
            copies.append(copy)
        local = pltpu.make_async_copy(x_ref if gather else x_ref.at[me], o_ref.at[me], local_sem)
        local.start()
        locals_.append(local)
    for copy in copies:
        copy.wait_send()
        copy.wait_recv()
    for local in locals_:
        local.wait()


def exchange_many(items, sizes, cid):
    jobs, shapes, scratch = [], [], []
    for x, axes, gather in items:
        n = math.prod(sizes[a] for a in axes)
        slab = x.shape if gather else x.shape[1:]
        jobs.append((axes, gather))
        shapes.append(jax.ShapeDtypeStruct((n,) + slab, x.dtype))
        scratch += [
            pltpu.SemaphoreType.DMA((max(n - 1, 1),)),
            pltpu.SemaphoreType.DMA((max(n - 1, 1),)),
            pltpu.SemaphoreType.DMA,
        ]
    return pl.pallas_call(
        functools.partial(exchange_kernel, jobs=tuple(jobs), sizes=sizes),
        out_shape=tuple(shapes),
        in_specs=[pl.BlockSpec(memory_space=pltpu.VMEM)] * len(items),
        out_specs=tuple(pl.BlockSpec(memory_space=pltpu.VMEM) for _ in items),
        scratch_shapes=scratch,
        compiler_params=pltpu.CompilerParams(
            collective_id=cid, has_side_effects=True, vmem_limit_bytes=48 * 1024 * 1024
        ),
    )(*[x for x, _, _ in items])


def exchange(x, axes, sizes, cid, gather=False):
    return exchange_many([(x, axes, gather)], sizes, cid)[0]


HALO_MOVES = ((1, 0), (-1, 0), (0, 1), (0, -1), (1, 1), (1, -1), (-1, 1), (-1, -1))


def halo_kernel(*refs, sizes):
    sends, recvs = refs[:3], refs[3:6]
    send_sem, recv_sem = refs[6:8]
    row, col = lax.axis_index("row"), lax.axis_index("col")

    def target(dr, dc):
        return {"row": lax.rem(row + dr + sizes["row"], sizes["row"]), "col": lax.rem(col + dc + sizes["col"], sizes["col"])}

    barrier = pltpu.get_barrier_semaphore()
    for dr, dc in HALO_MOVES:
        pl.semaphore_signal(barrier, inc=1, device_id=target(dr, dc), device_id_type=pl.DeviceIdType.MESH)
    pl.semaphore_wait(barrier, len(HALO_MOVES))
    copies = []
    for k, (dr, dc) in enumerate(HALO_MOVES):
        kind, slot = (0, k) if k < 2 else ((1, k - 2) if k < 4 else (2, k - 4))
        copy = pltpu.make_async_remote_copy(
            src_ref=sends[kind].at[slot],
            dst_ref=recvs[kind].at[slot],
            send_sem=send_sem.at[k],
            recv_sem=recv_sem.at[k],
            device_id=target(dr, dc),
            device_id_type=pl.DeviceIdType.MESH,
        )
        copy.start()
        copies.append(copy)
    for copy in copies:
        copy.wait_send()
        copy.wait_recv()


def padded_pair(tiles, sizes):
    rows_out = jnp.stack([tiles[:, -1], tiles[:, 0]])
    cols_out = jnp.stack([tiles[:, :, -1], tiles[:, :, 0]])
    corners_out = jnp.stack([tiles[:, -1, -1], tiles[:, -1, 0], tiles[:, 0, -1], tiles[:, 0, 0]])
    sends = (rows_out, cols_out, corners_out)
    recvs = pl.pallas_call(
        functools.partial(halo_kernel, sizes=sizes),
        out_shape=tuple(jax.ShapeDtypeStruct(x.shape, x.dtype) for x in sends),
        in_specs=[pl.BlockSpec(memory_space=pltpu.VMEM)] * 3,
        out_specs=tuple(pl.BlockSpec(memory_space=pltpu.VMEM) for _ in sends),
        scratch_shapes=[pltpu.SemaphoreType.DMA((len(HALO_MOVES),)), pltpu.SemaphoreType.DMA((len(HALO_MOVES),))],
        compiler_params=pltpu.CompilerParams(collective_id=8, has_side_effects=True),
    )(*sends)
    rows_in, cols_in, corners_in = recvs
    row, col = lax.axis_index("row"), lax.axis_index("col")
    up, down = row > 0, row < sizes["row"] - 1
    left, right = col > 0, col < sizes["col"] - 1
    zero = jnp.zeros((), tiles.dtype)
    top = jnp.where(up, rows_in[0], zero)
    bottom = jnp.where(down, rows_in[1], zero)
    west = jnp.where(left, cols_in[0], zero)
    east = jnp.where(right, cols_in[1], zero)
    top_left = jnp.where(up & left, corners_in[0], zero)
    top_right = jnp.where(up & right, corners_in[1], zero)
    bottom_left = jnp.where(down & left, corners_in[2], zero)
    bottom_right = jnp.where(down & right, corners_in[3], zero)
    padded = []
    for k in range(tiles.shape[0]):
        first = jnp.concatenate([top_left[k, None], top[k], top_right[k, None]], axis=0)
        middle = jnp.concatenate([west[k, :, None], tiles[k], east[k, :, None]], axis=1)
        last = jnp.concatenate([bottom_left[k, None], bottom[k], bottom_right[k, None]], axis=0)
        padded.append(jnp.concatenate([first[None], middle, last[None]], axis=0))
    return padded


def silu_slope(pre_float):
    sigma = jax.nn.sigmoid(pre_float)
    return sigma * (1.0 + pre_float * (1.0 - sigma))


def exact_dot(left, right, contract):
    return lax.dot_general(
        left.astype(jnp.float32),
        right.astype(jnp.float32),
        (contract, ((), ())),
        precision=lax.Precision.HIGHEST,
        preferred_element_type=jnp.float32,
    )


TAPS = [(a, b) for a in (-1, 0, 1) for b in (-1, 0, 1)]


def on_device(x_input, pre_act, out_grad, conv_weight, q_prev, sizes):
    height, breadth, channels = (x_input.shape[1], x_input.shape[2], x_input.shape[3])
    pixels = height * breadth
    rank = q_prev.shape[2]
    taps = len(TAPS)
    pre_float = pre_act.reshape(pixels, channels).astype(jnp.float32)
    hidden = jax.nn.silu(pre_float).astype(jnp.bfloat16)
    both_pad = padded_pair(
        jnp.stack([out_grad.reshape(height, breadth, channels), x_input.reshape(height, breadth, channels)]), sizes
    )
    grad_pad, input_pad = both_pad
    back_grad = jnp.zeros((pixels, channels), jnp.float32)
    for a, b in TAPS:
        window = grad_pad[1 - a : 1 - a + height, 1 - b : 1 - b + breadth].reshape(pixels, channels)
        back_grad = back_grad + lax.dot_general(
            window, conv_weight[a + 1, b + 1], (((1,), (1,)), ((), ())), preferred_element_type=jnp.float32
        )
    pre_grad = (back_grad * silu_slope(pre_float)).astype(jnp.bfloat16)

    grid = (height + 2, breadth + 2)
    grad_flat = grad_pad.reshape(-1, channels)
    input_flat = input_pad.reshape(-1, channels)
    q_taps = q_prev.reshape(taps, channels, 2, rank).transpose(2, 1, 0, 3).reshape(2, channels, taps * rank)

    first_terms = exact_dot(input_flat, q_taps[0], ((1,), (0,))).reshape(grid + (taps * rank,))
    first_sum = sum(
        first_terms[1 + a : 1 + a + height, 1 + b : 1 + b + breadth, k * rank : (k + 1) * rank]
        for k, (a, b) in enumerate(TAPS)
    ).reshape(pixels, rank)
    first_raw = exact_dot(pre_grad, first_sum, ((0,), (0,)))
    second_terms = exact_dot(hidden, q_taps[1], ((1,), (0,))).reshape(height, breadth, taps * rank)
    second_sum = sum(
        jnp.pad(second_terms[:, :, k * rank : (k + 1) * rank], ((1 - a, 1 + a), (1 - b, 1 + b), (0, 0)))
        for k, (a, b) in enumerate(TAPS)
    ).reshape(-1, rank)
    second_raw = exact_dot(grad_flat, second_sum, ((0,), (0,)))

    power_raw = all_sum_small(jnp.stack([first_raw, second_raw], axis=1), sizes)

    first_image = exact_dot(pre_grad, power_raw[:, 0], ((1,), (0,))).reshape(height, breadth, rank)
    first_spread = jnp.concatenate(
        [
            jnp.pad(first_image, ((1 + a, 1 - a), (1 + b, 1 - b), (0, 0))).reshape(-1, rank)
            for a, b in TAPS
        ],
        axis=1,
    )
    first_rows = exact_dot(input_flat, first_spread, ((0,), (0,)))
    second_image = exact_dot(grad_flat, power_raw[:, 1], ((1,), (0,))).reshape(grid + (rank,))
    second_spread = jnp.concatenate(
        [
            second_image[1 - a : 1 - a + height, 1 - b : 1 - b + breadth].reshape(pixels, rank)
            for a, b in TAPS
        ],
        axis=1,
    )
    second_rows = exact_dot(hidden, second_spread, ((0,), (0,)))
    rows = jnp.concatenate(
        [
            first_rows.reshape(channels, taps, rank).transpose(1, 0, 2),
            second_rows.reshape(channels, taps, rank).transpose(1, 0, 2),
        ],
        axis=-1,
    ).reshape(taps * channels, 2, rank)
    row_block = block_sum(rows, sizes)

    gram = jnp.einsum(
        "mqn,mqg->qng", power_raw, power_raw, precision=lax.Precision.HIGHEST, preferred_element_type=jnp.float32
    )
    lower = jnp.linalg.cholesky(gram)
    basis_count = channels // sizes["dp"]
    raw_part = lax.dynamic_slice_in_dim(power_raw, lax.axis_index("dp") * basis_count, basis_count, 0)
    basis_out = lax.linalg.triangular_solve(
        lower, raw_part.transpose(1, 0, 2), left_side=False, lower=True, transpose_a=True
    ).transpose(1, 0, 2)
    factor_out = lax.linalg.triangular_solve(
        lower, row_block.transpose(1, 0, 2), left_side=False, lower=True, transpose_a=True
    ).transpose(1, 0, 2)
    return (basis_out, factor_out)


def allsum_kernel(p_ref, o_ref, recv1, send2, recv2, piece, recv3, chunk, *sems, sizes):
    group_axes, ring_axes = ("row", "col"), ("dp",)
    n_group = sizes["row"] * sizes["col"]
    n_ring = sizes["dp"]
    me_group = lax.axis_index("row") * sizes["col"] + lax.axis_index("col")
    me_ring = lax.axis_index("dp")
    barrier = pltpu.get_barrier_semaphore()
    for s in range(1, n_group):
        peer = member_coords(lax.rem(me_group + s, n_group), group_axes, sizes)
        pl.semaphore_signal(barrier, inc=1, device_id=peer, device_id_type=pl.DeviceIdType.MESH)
    for s in range(1, n_ring):
        peer = member_coords(lax.rem(me_ring + s, n_ring), ring_axes, sizes)
        pl.semaphore_signal(barrier, inc=1, device_id=peer, device_id_type=pl.DeviceIdType.MESH)
    pl.semaphore_wait(barrier, n_group - 1 + n_ring - 1)

    def phase(source, target, me, n, axes, send_sem, recv_sem, local_sem, gather):
        copies = []
        for s in range(1, n):
            dst = lax.rem(me + s, n)
            copy = pltpu.make_async_remote_copy(
                src_ref=source if gather else source.at[dst],
                dst_ref=target.at[me],
                send_sem=send_sem.at[s - 1],
                recv_sem=recv_sem.at[s - 1],
                device_id=member_coords(dst, axes, sizes),
                device_id_type=pl.DeviceIdType.MESH,
            )
            copy.start()
            copies.append(copy)
        local = pltpu.make_async_copy(source if gather else source.at[me], target.at[me], local_sem)
        local.start()
        for copy in copies:
            copy.wait_send()
            copy.wait_recv()
        local.wait()

    phase(p_ref, recv1, me_group, n_group, group_axes, sems[0], sems[1], sems[8], False)
    total = recv1[0]
    for j in range(1, n_group):
        total = total + recv1[j]
    for j in range(n_ring):
        send2[j] = total[j : j + 1]
    phase(send2, recv2, me_ring, n_ring, ring_axes, sems[2], sems[3], sems[9], False)
    reduced = recv2[0]
    for j in range(1, n_ring):
        reduced = reduced + recv2[j]
    piece[...] = reduced
    phase(piece, recv3, me_ring, n_ring, ring_axes, sems[4], sems[5], sems[10], True)
    for j in range(n_ring):
        chunk[j : j + 1] = recv3[j]
    phase(chunk, o_ref, me_group, n_group, group_axes, sems[6], sems[7], sems[11], True)


def all_sum_small(value, sizes):
    shape = value.shape
    n_group = sizes["row"] * sizes["col"]
    n_ring = sizes["dp"]
    width = value.size // (n_group * n_ring)
    parts = value.reshape(n_group, n_ring, width)
    vmem = pl.BlockSpec(memory_space=pltpu.VMEM)
    out = pl.pallas_call(
        functools.partial(allsum_kernel, sizes=sizes),
        out_shape=jax.ShapeDtypeStruct(parts.shape, parts.dtype),
        in_specs=[vmem],
        out_specs=vmem,
        scratch_shapes=[
            pltpu.VMEM((n_group, n_ring, width), jnp.float32),
            pltpu.VMEM((n_ring, 1, width), jnp.float32),
            pltpu.VMEM((n_ring, 1, width), jnp.float32),
            pltpu.VMEM((1, width), jnp.float32),
            pltpu.VMEM((n_ring, 1, width), jnp.float32),
            pltpu.VMEM((n_ring, width), jnp.float32),
        ]
        + [pltpu.SemaphoreType.DMA((n - 1,)) for n in (n_group, n_group, n_ring, n_ring, n_ring, n_ring, n_group, n_group)]
        + [pltpu.SemaphoreType.DMA] * 4,
        compiler_params=pltpu.CompilerParams(collective_id=0, has_side_effects=True),
    )(parts)
    return out.reshape(shape)


def permute_sum(value, axis, sizes):
    n = sizes[axis]
    me = lax.axis_index(axis)
    total = lax.dynamic_index_in_dim(value, me, 0, keepdims=False)
    for shift in range(1, n):
        slab = lax.dynamic_index_in_dim(value, lax.rem(me + shift, n), 0, keepdims=False)
        total = total + lax.ppermute(slab, axis, [(i, (i + shift) % n) for i in range(n)])
    return total


def block_sum(value, sizes):
    shape = value.shape
    blocks, rows_n, cols_n = sizes["dp"], sizes["row"], sizes["col"]
    group = rows_n * cols_n
    block_rows = shape[0] // blocks
    piece_rows = -(-block_rows // (group * 8)) * 8
    lanes = math.prod(shape[1:])
    padded = jnp.pad(value.reshape(blocks, block_rows, lanes), ((0, 0), (0, piece_rows * group - block_rows), (0, 0)))
    pieces = padded.reshape(blocks, rows_n, cols_n, piece_rows, lanes)
    half = blocks // 2
    first = pieces[:half].transpose(1, 2, 0, 3, 4)
    second = pieces[half:].transpose(2, 1, 0, 3, 4)
    first, second = permute_sum(first, "row", sizes), permute_sum(second, "col", sizes)
    first, second = exchange_many([(first, ("col",), False), (second, ("row",), False)], sizes, 5)
    pieces = jnp.concatenate([first.sum(0), second.sum(0)])
    piece = exchange(pieces, ("dp",), sizes, 6).sum(0)
    block = exchange(piece, ("row", "col"), sizes, 7, gather=True)
    return block.reshape(group * piece_rows, lanes)[:block_rows].reshape((block_rows,) + shape[1:])


def solution(mesh):
    placed = (
        P("dp", "row", "col", None),
        P("dp", "row", "col", None),
        P("dp", "row", "col", None),
        P(),
        P(),
    )
    sizes = dict(mesh.shape)
    return jax.shard_map(
        functools.partial(on_device, sizes=sizes),
        mesh=mesh,
        in_specs=placed,
        out_specs=(P("dp", None, None), P("dp", None, None)),
        check_vma=False,
    )
```

```python
import functools
import math

import jax
import jax.numpy as jnp
from jax import lax
from jax.experimental import pallas as pl
from jax.experimental.pallas import tpu as pltpu
from jax.sharding import PartitionSpec as P


def member_coords(j, axes, sizes):
    coords = {}
    for axis in reversed(axes):
        coords[axis] = lax.rem(j, sizes[axis])
        j = j // sizes[axis]
    return coords


def exchange_kernel(*refs, jobs, sizes):
    count = len(jobs)
    x_refs, o_refs = refs[:count], refs[count : 2 * count]
    sems = refs[2 * count :]
    barrier = pltpu.get_barrier_semaphore()
    plans = []
    total = 0
    for axes, gather in jobs:
        n = math.prod(sizes[a] for a in axes)
        me = 0
        for axis in axes:
            me = me * sizes[axis] + lax.axis_index(axis)
        for s in range(1, n):
            peer = member_coords(lax.rem(me + s, n), axes, sizes)
            pl.semaphore_signal(barrier, inc=1, device_id=peer, device_id_type=pl.DeviceIdType.MESH)
        total += n - 1
        plans.append((n, me))
    pl.semaphore_wait(barrier, total)
    copies, locals_ = [], []
    for job, ((axes, gather), (n, me)) in enumerate(zip(jobs, plans)):
        x_ref, o_ref = x_refs[job], o_refs[job]
        send_sem, recv_sem, local_sem = sems[3 * job : 3 * job + 3]
        for s in range(1, n):
            dst = lax.rem(me + s, n)
            copy = pltpu.make_async_remote_copy(
                src_ref=x_ref if gather else x_ref.at[dst],
                dst_ref=o_ref.at[me],
                send_sem=send_sem.at[s - 1],
                recv_sem=recv_sem.at[s - 1],
                device_id=member_coords(dst, axes, sizes),
                device_id_type=pl.DeviceIdType.MESH,
            )
            copy.start()
            copies.append(copy)
        local = pltpu.make_async_copy(x_ref if gather else x_ref.at[me], o_ref.at[me], local_sem)
        local.start()
        locals_.append(local)
    for copy in copies:
        copy.wait_send()
        copy.wait_recv()
    for local in locals_:
        local.wait()


def exchange_many(items, sizes, cid):
    jobs, shapes, scratch = [], [], []
    for x, axes, gather in items:
        n = math.prod(sizes[a] for a in axes)
        slab = x.shape if gather else x.shape[1:]
        jobs.append((axes, gather))
        shapes.append(jax.ShapeDtypeStruct((n,) + slab, x.dtype))
        scratch += [
            pltpu.SemaphoreType.DMA((max(n - 1, 1),)),
            pltpu.SemaphoreType.DMA((max(n - 1, 1),)),
            pltpu.SemaphoreType.DMA,
        ]
    return pl.pallas_call(
        functools.partial(exchange_kernel, jobs=tuple(jobs), sizes=sizes),
        out_shape=tuple(shapes),
        in_specs=[pl.BlockSpec(memory_space=pltpu.VMEM)] * len(items),
        out_specs=tuple(pl.BlockSpec(memory_space=pltpu.VMEM) for _ in items),
        scratch_shapes=scratch,
        compiler_params=pltpu.CompilerParams(
            collective_id=cid, has_side_effects=True, vmem_limit_bytes=48 * 1024 * 1024
        ),
    )(*[x for x, _, _ in items])


def exchange(x, axes, sizes, cid, gather=False):
    return exchange_many([(x, axes, gather)], sizes, cid)[0]


HALO_MOVES = ((1, 0), (-1, 0), (0, 1), (0, -1), (1, 1), (1, -1), (-1, 1), (-1, -1))


def halo_kernel(*refs, sizes):
    sends, recvs = refs[:3], refs[3:6]
    send_sem, recv_sem = refs[6:8]
    row, col = lax.axis_index("row"), lax.axis_index("col")

    def target(dr, dc):
        return {"row": lax.rem(row + dr + sizes["row"], sizes["row"]), "col": lax.rem(col + dc + sizes["col"], sizes["col"])}

    barrier = pltpu.get_barrier_semaphore()
    for dr, dc in HALO_MOVES:
        pl.semaphore_signal(barrier, inc=1, device_id=target(dr, dc), device_id_type=pl.DeviceIdType.MESH)
    pl.semaphore_wait(barrier, len(HALO_MOVES))
    copies = []
    for k, (dr, dc) in enumerate(HALO_MOVES):
        kind, slot = (0, k) if k < 2 else ((1, k - 2) if k < 4 else (2, k - 4))
        copy = pltpu.make_async_remote_copy(
            src_ref=sends[kind].at[slot],
            dst_ref=recvs[kind].at[slot],
            send_sem=send_sem.at[k],
            recv_sem=recv_sem.at[k],
            device_id=target(dr, dc),
            device_id_type=pl.DeviceIdType.MESH,
        )
        copy.start()
        copies.append(copy)
    for copy in copies:
        copy.wait_send()
        copy.wait_recv()


def padded_pair(tiles, sizes):
    rows_out = jnp.stack([tiles[:, -1], tiles[:, 0]])
    cols_out = jnp.stack([tiles[:, :, -1], tiles[:, :, 0]])
    corners_out = jnp.stack([tiles[:, -1, -1], tiles[:, -1, 0], tiles[:, 0, -1], tiles[:, 0, 0]])
    sends = (rows_out, cols_out, corners_out)
    recvs = pl.pallas_call(
        functools.partial(halo_kernel, sizes=sizes),
        out_shape=tuple(jax.ShapeDtypeStruct(x.shape, x.dtype) for x in sends),
        in_specs=[pl.BlockSpec(memory_space=pltpu.VMEM)] * 3,
        out_specs=tuple(pl.BlockSpec(memory_space=pltpu.VMEM) for _ in sends),
        scratch_shapes=[pltpu.SemaphoreType.DMA((len(HALO_MOVES),)), pltpu.SemaphoreType.DMA((len(HALO_MOVES),))],
        compiler_params=pltpu.CompilerParams(collective_id=8, has_side_effects=True),
    )(*sends)
    rows_in, cols_in, corners_in = recvs
    row, col = lax.axis_index("row"), lax.axis_index("col")
    up, down = row > 0, row < sizes["row"] - 1
    left, right = col > 0, col < sizes["col"] - 1
    zero = jnp.zeros((), tiles.dtype)
    top = jnp.where(up, rows_in[0], zero)
    bottom = jnp.where(down, rows_in[1], zero)
    west = jnp.where(left, cols_in[0], zero)
    east = jnp.where(right, cols_in[1], zero)
    top_left = jnp.where(up & left, corners_in[0], zero)
    top_right = jnp.where(up & right, corners_in[1], zero)
    bottom_left = jnp.where(down & left, corners_in[2], zero)
    bottom_right = jnp.where(down & right, corners_in[3], zero)
    padded = []
    for k in range(tiles.shape[0]):
        first = jnp.concatenate([top_left[k, None], top[k], top_right[k, None]], axis=0)
        middle = jnp.concatenate([west[k, :, None], tiles[k], east[k, :, None]], axis=1)
        last = jnp.concatenate([bottom_left[k, None], bottom[k], bottom_right[k, None]], axis=0)
        padded.append(jnp.concatenate([first[None], middle, last[None]], axis=0))
    return padded


def silu_slope(pre_float):
    sigma = jax.nn.sigmoid(pre_float)
    return sigma * (1.0 + pre_float * (1.0 - sigma))


def exact_dot(left, right, contract):
    return lax.dot_general(
        left.astype(jnp.float32),
        right.astype(jnp.float32),
        (contract, ((), ())),
        precision=lax.Precision.HIGHEST,
        preferred_element_type=jnp.float32,
    )


TAPS = [(a, b) for a in (-1, 0, 1) for b in (-1, 0, 1)]


def on_device(x_input, pre_act, out_grad, conv_weight, q_prev, sizes):
    height, breadth, channels = (x_input.shape[1], x_input.shape[2], x_input.shape[3])
    pixels = height * breadth
    rank = q_prev.shape[2]
    taps = len(TAPS)
    pre_float = pre_act.reshape(pixels, channels).astype(jnp.float32)
    hidden = jax.nn.silu(pre_float).astype(jnp.bfloat16)
    both_pad = padded_pair(
        jnp.stack([out_grad.reshape(height, breadth, channels), x_input.reshape(height, breadth, channels)]), sizes
    )
    grad_pad, input_pad = both_pad
    back_grad = jnp.zeros((pixels, channels), jnp.float32)
    for a, b in TAPS:
        window = grad_pad[1 - a : 1 - a + height, 1 - b : 1 - b + breadth].reshape(pixels, channels)
        back_grad = back_grad + lax.dot_general(
            window, conv_weight[a + 1, b + 1], (((1,), (1,)), ((), ())), preferred_element_type=jnp.float32
        )
    pre_grad = (back_grad * silu_slope(pre_float)).astype(jnp.bfloat16)

    grid = (height + 2, breadth + 2)
    grad_flat = grad_pad.reshape(-1, channels)
    input_flat = input_pad.reshape(-1, channels)
    q_taps = q_prev.reshape(taps, channels, 2, rank).transpose(2, 1, 0, 3).reshape(2, channels, taps * rank)

    first_terms = exact_dot(input_flat, q_taps[0], ((1,), (0,))).reshape(grid + (taps * rank,))
    first_sum = sum(
        first_terms[1 + a : 1 + a + height, 1 + b : 1 + b + breadth, k * rank : (k + 1) * rank]
        for k, (a, b) in enumerate(TAPS)
    ).reshape(pixels, rank)
    first_raw = exact_dot(pre_grad, first_sum, ((0,), (0,)))
    second_terms = exact_dot(hidden, q_taps[1], ((1,), (0,))).reshape(height, breadth, taps * rank)
    second_sum = sum(
        jnp.pad(second_terms[:, :, k * rank : (k + 1) * rank], ((1 - a, 1 + a), (1 - b, 1 + b), (0, 0)))
        for k, (a, b) in enumerate(TAPS)
    ).reshape(-1, rank)
    second_raw = exact_dot(grad_flat, second_sum, ((0,), (0,)))

    power_raw = all_sum_small(jnp.stack([first_raw, second_raw], axis=1), sizes)

    first_image = exact_dot(pre_grad, power_raw[:, 0], ((1,), (0,))).reshape(height, breadth, rank)
    first_spread = jnp.concatenate(
        [
            jnp.pad(first_image, ((1 + a, 1 - a), (1 + b, 1 - b), (0, 0))).reshape(-1, rank)
            for a, b in TAPS
        ],
        axis=1,
    )
    first_rows = exact_dot(input_flat, first_spread, ((0,), (0,)))
    second_image = exact_dot(grad_flat, power_raw[:, 1], ((1,), (0,))).reshape(grid + (rank,))
    second_spread = jnp.concatenate(
        [
            second_image[1 - a : 1 - a + height, 1 - b : 1 - b + breadth].reshape(pixels, rank)
            for a, b in TAPS
        ],
        axis=1,
    )
    second_rows = exact_dot(hidden, second_spread, ((0,), (0,)))
    rows = jnp.concatenate(
        [
            first_rows.reshape(channels, taps, rank).transpose(1, 0, 2),
            second_rows.reshape(channels, taps, rank).transpose(1, 0, 2),
        ],
        axis=-1,
    ).reshape(taps * channels, 2, rank)
    row_block = block_sum(rows, sizes)

    gram = jnp.einsum(
        "mqn,mqg->qng", power_raw, power_raw, precision=lax.Precision.HIGHEST, preferred_element_type=jnp.float32
    )
    lower = jnp.linalg.cholesky(gram)
    basis_count = channels // sizes["dp"]
    raw_part = lax.dynamic_slice_in_dim(power_raw, lax.axis_index("dp") * basis_count, basis_count, 0)
    basis_out = lax.linalg.triangular_solve(
        lower, raw_part.transpose(1, 0, 2), left_side=False, lower=True, transpose_a=True
    ).transpose(1, 0, 2)
    factor_out = lax.linalg.triangular_solve(
        lower, row_block.transpose(1, 0, 2), left_side=False, lower=True, transpose_a=True
    ).transpose(1, 0, 2)
    return (basis_out, factor_out)


def allsum_kernel(p_ref, o_ref, recv1, send2, recv2, piece, recv3, chunk, *sems, sizes):
    group_axes, ring_axes = ("row", "col"), ("dp",)
    n_group = sizes["row"] * sizes["col"]
    n_ring = sizes["dp"]
    me_group = lax.axis_index("row") * sizes["col"] + lax.axis_index("col")
    me_ring = lax.axis_index("dp")
    barrier = pltpu.get_barrier_semaphore()
    for s in range(1, n_group):
        peer = member_coords(lax.rem(me_group + s, n_group), group_axes, sizes)
        pl.semaphore_signal(barrier, inc=1, device_id=peer, device_id_type=pl.DeviceIdType.MESH)
    for s in range(1, n_ring):
        peer = member_coords(lax.rem(me_ring + s, n_ring), ring_axes, sizes)
        pl.semaphore_signal(barrier, inc=1, device_id=peer, device_id_type=pl.DeviceIdType.MESH)
    pl.semaphore_wait(barrier, n_group - 1 + n_ring - 1)

    def phase(source, target, me, n, axes, send_sem, recv_sem, local_sem, gather):
        copies = []
        for s in range(1, n):
            dst = lax.rem(me + s, n)
            copy = pltpu.make_async_remote_copy(
                src_ref=source if gather else source.at[dst],
                dst_ref=target.at[me],
                send_sem=send_sem.at[s - 1],
                recv_sem=recv_sem.at[s - 1],
                device_id=member_coords(dst, axes, sizes),
                device_id_type=pl.DeviceIdType.MESH,
            )
            copy.start()
            copies.append(copy)
        local = pltpu.make_async_copy(source if gather else source.at[me], target.at[me], local_sem)
        local.start()
        for copy in copies:
            copy.wait_send()
            copy.wait_recv()
        local.wait()

    phase(p_ref, recv1, me_group, n_group, group_axes, sems[0], sems[1], sems[8], False)
    total = recv1[0]
    for j in range(1, n_group):
        total = total + recv1[j]
    for j in range(n_ring):
        send2[j] = total[j : j + 1]
    phase(send2, recv2, me_ring, n_ring, ring_axes, sems[2], sems[3], sems[9], False)
    reduced = recv2[0]
    for j in range(1, n_ring):
        reduced = reduced + recv2[j]
    piece[...] = reduced
    phase(piece, recv3, me_ring, n_ring, ring_axes, sems[4], sems[5], sems[10], True)
    for j in range(n_ring):
        chunk[j : j + 1] = recv3[j]
    phase(chunk, o_ref, me_group, n_group, group_axes, sems[6], sems[7], sems[11], True)


def all_sum_small(value, sizes):
    shape = value.shape
    n_group = sizes["row"] * sizes["col"]
    n_ring = sizes["dp"]
    width = value.size // (n_group * n_ring)
    parts = value.reshape(n_group, n_ring, width)
    vmem = pl.BlockSpec(memory_space=pltpu.VMEM)
    out = pl.pallas_call(
        functools.partial(allsum_kernel, sizes=sizes),
        out_shape=jax.ShapeDtypeStruct(parts.shape, parts.dtype),
        in_specs=[vmem],
        out_specs=vmem,
        scratch_shapes=[
            pltpu.VMEM((n_group, n_ring, width), jnp.float32),
            pltpu.VMEM((n_ring, 1, width), jnp.float32),
            pltpu.VMEM((n_ring, 1, width), jnp.float32),
            pltpu.VMEM((1, width), jnp.float32),
            pltpu.VMEM((n_ring, 1, width), jnp.float32),
            pltpu.VMEM((n_ring, width), jnp.float32),
        ]
        + [pltpu.SemaphoreType.DMA((n - 1,)) for n in (n_group, n_group, n_ring, n_ring, n_ring, n_ring, n_group, n_group)]
        + [pltpu.SemaphoreType.DMA] * 4,
        compiler_params=pltpu.CompilerParams(collective_id=0, has_side_effects=True),
    )(parts)
    return out.reshape(shape)


def permute_sum(value, axis, sizes):
    n = sizes[axis]
    me = lax.axis_index(axis)
    total = lax.dynamic_index_in_dim(value, me, 0, keepdims=False)
    for shift in range(1, n):
        slab = lax.dynamic_index_in_dim(value, lax.rem(me + shift, n), 0, keepdims=False)
        total = total + lax.ppermute(slab, axis, [(i, (i + shift) % n) for i in range(n)])
    return total


def block_sum(value, sizes):
    shape = value.shape
    blocks, rows_n, cols_n = sizes["dp"], sizes["row"], sizes["col"]
    group = rows_n * cols_n
    block_rows = shape[0] // blocks
    piece_rows = -(-block_rows // (group * 8)) * 8
    lanes = math.prod(shape[1:])
    padded = jnp.pad(value.reshape(blocks, block_rows, lanes), ((0, 0), (0, piece_rows * group - block_rows), (0, 0)))
    pieces = padded.reshape(blocks, rows_n, cols_n, piece_rows, lanes)
    half = blocks * 3 // 8
    first = pieces[:half].transpose(1, 2, 0, 3, 4)
    second = pieces[half:].transpose(2, 1, 0, 3, 4)
    first, second = permute_sum(first, "row", sizes), permute_sum(second, "col", sizes)
    first, second = exchange_many([(first, ("col",), False), (second, ("row",), False)], sizes, 5)
    pieces = jnp.concatenate([first.sum(0), second.sum(0)])
    piece = exchange(pieces, ("dp",), sizes, 6).sum(0)
    block = exchange(piece, ("row", "col"), sizes, 7, gather=True)
    return block.reshape(group * piece_rows, lanes)[:block_rows].reshape((block_rows,) + shape[1:])


def solution(mesh):
    placed = (
        P("dp", "row", "col", None),
        P("dp", "row", "col", None),
        P("dp", "row", "col", None),
        P(),
        P(),
    )
    sizes = dict(mesh.shape)
    return jax.shard_map(
        functools.partial(on_device, sizes=sizes),
        mesh=mesh,
        in_specs=placed,
        out_specs=(P("dp", None, None), P("dp", None, None)),
        check_vma=False,
    )
```

```python
import functools
import math

import jax
import jax.numpy as jnp
from jax import lax
from jax.experimental import pallas as pl
from jax.experimental.pallas import tpu as pltpu
from jax.sharding import PartitionSpec as P


def member_coords(j, axes, sizes):
    coords = {}
    for axis in reversed(axes):
        coords[axis] = lax.rem(j, sizes[axis])
        j = j // sizes[axis]
    return coords


def exchange_kernel(*refs, jobs, sizes):
    count = len(jobs)
    x_refs, o_refs = refs[:count], refs[count : 2 * count]
    sems = refs[2 * count :]
    barrier = pltpu.get_barrier_semaphore()
    plans = []
    total = 0
    for axes, gather in jobs:
        n = math.prod(sizes[a] for a in axes)
        me = 0
        for axis in axes:
            me = me * sizes[axis] + lax.axis_index(axis)
        for s in range(1, n):
            peer = member_coords(lax.rem(me + s, n), axes, sizes)
            pl.semaphore_signal(barrier, inc=1, device_id=peer, device_id_type=pl.DeviceIdType.MESH)
        total += n - 1
        plans.append((n, me))
    pl.semaphore_wait(barrier, total)
    copies, locals_ = [], []
    for job, ((axes, gather), (n, me)) in enumerate(zip(jobs, plans)):
        x_ref, o_ref = x_refs[job], o_refs[job]
        send_sem, recv_sem, local_sem = sems[3 * job : 3 * job + 3]
        for s in range(1, n):
            dst = lax.rem(me + s, n)
            copy = pltpu.make_async_remote_copy(
                src_ref=x_ref if gather else x_ref.at[dst],
                dst_ref=o_ref.at[me],
                send_sem=send_sem.at[s - 1],
                recv_sem=recv_sem.at[s - 1],
                device_id=member_coords(dst, axes, sizes),
                device_id_type=pl.DeviceIdType.MESH,
            )
            copy.start()
            copies.append(copy)
        local = pltpu.make_async_copy(x_ref if gather else x_ref.at[me], o_ref.at[me], local_sem)
        local.start()
        locals_.append(local)
    for copy in copies:
        copy.wait_send()
        copy.wait_recv()
    for local in locals_:
        local.wait()


def exchange_many(items, sizes, cid):
    jobs, shapes, scratch = [], [], []
    for x, axes, gather in items:
        n = math.prod(sizes[a] for a in axes)
        slab = x.shape if gather else x.shape[1:]
        jobs.append((axes, gather))
        shapes.append(jax.ShapeDtypeStruct((n,) + slab, x.dtype))
        scratch += [
            pltpu.SemaphoreType.DMA((max(n - 1, 1),)),
            pltpu.SemaphoreType.DMA((max(n - 1, 1),)),
            pltpu.SemaphoreType.DMA,
        ]
    return pl.pallas_call(
        functools.partial(exchange_kernel, jobs=tuple(jobs), sizes=sizes),
        out_shape=tuple(shapes),
        in_specs=[pl.BlockSpec(memory_space=pltpu.VMEM)] * len(items),
        out_specs=tuple(pl.BlockSpec(memory_space=pltpu.VMEM) for _ in items),
        scratch_shapes=scratch,
        compiler_params=pltpu.CompilerParams(
            collective_id=cid, has_side_effects=True, vmem_limit_bytes=48 * 1024 * 1024
        ),
    )(*[x for x, _, _ in items])


def exchange(x, axes, sizes, cid, gather=False):
    return exchange_many([(x, axes, gather)], sizes, cid)[0]


HALO_MOVES = ((1, 0), (-1, 0), (0, 1), (0, -1), (1, 1), (1, -1), (-1, 1), (-1, -1))


def halo_kernel(*refs, sizes):
    sends, recvs = refs[:3], refs[3:6]
    send_sem, recv_sem = refs[6:8]
    row, col = lax.axis_index("row"), lax.axis_index("col")

    def target(dr, dc):
        return {"row": lax.rem(row + dr + sizes["row"], sizes["row"]), "col": lax.rem(col + dc + sizes["col"], sizes["col"])}

    barrier = pltpu.get_barrier_semaphore()
    for dr, dc in HALO_MOVES:
        pl.semaphore_signal(barrier, inc=1, device_id=target(dr, dc), device_id_type=pl.DeviceIdType.MESH)
    pl.semaphore_wait(barrier, len(HALO_MOVES))
    copies = []
    for k, (dr, dc) in enumerate(HALO_MOVES):
        kind, slot = (0, k) if k < 2 else ((1, k - 2) if k < 4 else (2, k - 4))
        copy = pltpu.make_async_remote_copy(
            src_ref=sends[kind].at[slot],
            dst_ref=recvs[kind].at[slot],
            send_sem=send_sem.at[k],
            recv_sem=recv_sem.at[k],
            device_id=target(dr, dc),
            device_id_type=pl.DeviceIdType.MESH,
        )
        copy.start()
        copies.append(copy)
    for copy in copies:
        copy.wait_send()
        copy.wait_recv()


def padded_pair(tiles, sizes):
    rows_out = jnp.stack([tiles[:, -1], tiles[:, 0]])
    cols_out = jnp.stack([tiles[:, :, -1], tiles[:, :, 0]])
    corners_out = jnp.stack([tiles[:, -1, -1], tiles[:, -1, 0], tiles[:, 0, -1], tiles[:, 0, 0]])
    sends = (rows_out, cols_out, corners_out)
    recvs = pl.pallas_call(
        functools.partial(halo_kernel, sizes=sizes),
        out_shape=tuple(jax.ShapeDtypeStruct(x.shape, x.dtype) for x in sends),
        in_specs=[pl.BlockSpec(memory_space=pltpu.VMEM)] * 3,
        out_specs=tuple(pl.BlockSpec(memory_space=pltpu.VMEM) for _ in sends),
        scratch_shapes=[pltpu.SemaphoreType.DMA((len(HALO_MOVES),)), pltpu.SemaphoreType.DMA((len(HALO_MOVES),))],
        compiler_params=pltpu.CompilerParams(collective_id=8, has_side_effects=True),
    )(*sends)
    rows_in, cols_in, corners_in = recvs
    row, col = lax.axis_index("row"), lax.axis_index("col")
    up, down = row > 0, row < sizes["row"] - 1
    left, right = col > 0, col < sizes["col"] - 1
    zero = jnp.zeros((), tiles.dtype)
    top = jnp.where(up, rows_in[0], zero)
    bottom = jnp.where(down, rows_in[1], zero)
    west = jnp.where(left, cols_in[0], zero)
    east = jnp.where(right, cols_in[1], zero)
    top_left = jnp.where(up & left, corners_in[0], zero)
    top_right = jnp.where(up & right, corners_in[1], zero)
    bottom_left = jnp.where(down & left, corners_in[2], zero)
    bottom_right = jnp.where(down & right, corners_in[3], zero)
    padded = []
    for k in range(tiles.shape[0]):
        first = jnp.concatenate([top_left[k, None], top[k], top_right[k, None]], axis=0)
        middle = jnp.concatenate([west[k, :, None], tiles[k], east[k, :, None]], axis=1)
        last = jnp.concatenate([bottom_left[k, None], bottom[k], bottom_right[k, None]], axis=0)
        padded.append(jnp.concatenate([first[None], middle, last[None]], axis=0))
    return padded


def silu_slope(pre_float):
    sigma = jax.nn.sigmoid(pre_float)
    return sigma * (1.0 + pre_float * (1.0 - sigma))


def exact_dot(left, right, contract):
    return lax.dot_general(
        left.astype(jnp.float32),
        right.astype(jnp.float32),
        (contract, ((), ())),
        precision=lax.Precision.HIGHEST,
        preferred_element_type=jnp.float32,
    )


TAPS = [(a, b) for a in (-1, 0, 1) for b in (-1, 0, 1)]


def on_device(x_input, pre_act, out_grad, conv_weight, q_prev, sizes):
    height, breadth, channels = (x_input.shape[1], x_input.shape[2], x_input.shape[3])
    pixels = height * breadth
    rank = q_prev.shape[2]
    taps = len(TAPS)
    pre_float = pre_act.reshape(pixels, channels).astype(jnp.float32)
    hidden = jax.nn.silu(pre_float).astype(jnp.bfloat16)
    both_pad = padded_pair(
        jnp.stack([out_grad.reshape(height, breadth, channels), x_input.reshape(height, breadth, channels)]), sizes
    )
    grad_pad, input_pad = both_pad
    back_grad = jnp.zeros((pixels, channels), jnp.float32)
    for a, b in TAPS:
        window = grad_pad[1 - a : 1 - a + height, 1 - b : 1 - b + breadth].reshape(pixels, channels)
        back_grad = back_grad + lax.dot_general(
            window, conv_weight[a + 1, b + 1], (((1,), (1,)), ((), ())), preferred_element_type=jnp.float32
        )
    pre_grad = (back_grad * silu_slope(pre_float)).astype(jnp.bfloat16)

    grid = (height + 2, breadth + 2)
    grad_flat = grad_pad.reshape(-1, channels)
    input_flat = input_pad.reshape(-1, channels)
    q_taps = q_prev.reshape(taps, channels, 2, rank).transpose(2, 1, 0, 3).reshape(2, channels, taps * rank)

    first_terms = exact_dot(input_flat, q_taps[0], ((1,), (0,))).reshape(grid + (taps * rank,))
    first_sum = sum(
        first_terms[1 + a : 1 + a + height, 1 + b : 1 + b + breadth, k * rank : (k + 1) * rank]
        for k, (a, b) in enumerate(TAPS)
    ).reshape(pixels, rank)
    first_raw = exact_dot(pre_grad, first_sum, ((0,), (0,)))
    second_terms = exact_dot(hidden, q_taps[1], ((1,), (0,))).reshape(height, breadth, taps * rank)
    second_sum = sum(
        jnp.pad(second_terms[:, :, k * rank : (k + 1) * rank], ((1 - a, 1 + a), (1 - b, 1 + b), (0, 0)))
        for k, (a, b) in enumerate(TAPS)
    ).reshape(-1, rank)
    second_raw = exact_dot(grad_flat, second_sum, ((0,), (0,)))

    power_raw = all_sum_small(jnp.stack([first_raw, second_raw], axis=1), sizes)

    first_image = exact_dot(pre_grad, power_raw[:, 0], ((1,), (0,))).reshape(height, breadth, rank)
    first_spread = jnp.concatenate(
        [
            jnp.pad(first_image, ((1 + a, 1 - a), (1 + b, 1 - b), (0, 0))).reshape(-1, rank)
            for a, b in TAPS
        ],
        axis=1,
    )
    first_rows = exact_dot(input_flat, first_spread, ((0,), (0,)))
    second_image = exact_dot(grad_flat, power_raw[:, 1], ((1,), (0,))).reshape(grid + (rank,))
    second_spread = jnp.concatenate(
        [
            second_image[1 - a : 1 - a + height, 1 - b : 1 - b + breadth].reshape(pixels, rank)
            for a, b in TAPS
        ],
        axis=1,
    )
    second_rows = exact_dot(hidden, second_spread, ((0,), (0,)))
    rows = jnp.concatenate(
        [
            first_rows.reshape(channels, taps, rank).transpose(1, 0, 2),
            second_rows.reshape(channels, taps, rank).transpose(1, 0, 2),
        ],
        axis=-1,
    ).reshape(taps * channels, 2, rank)
    row_block = block_sum(rows, sizes)

    gram = jnp.einsum(
        "mqn,mqg->qng", power_raw, power_raw, precision=lax.Precision.HIGHEST, preferred_element_type=jnp.float32
    )
    lower = jnp.linalg.cholesky(gram)
    basis_count = channels // sizes["dp"]
    raw_part = lax.dynamic_slice_in_dim(power_raw, lax.axis_index("dp") * basis_count, basis_count, 0)
    basis_out = lax.linalg.triangular_solve(
        lower, raw_part.transpose(1, 0, 2), left_side=False, lower=True, transpose_a=True
    ).transpose(1, 0, 2)
    factor_out = lax.linalg.triangular_solve(
        lower, row_block.transpose(1, 0, 2), left_side=False, lower=True, transpose_a=True
    ).transpose(1, 0, 2)
    return (basis_out, factor_out)


def allsum_kernel(p_ref, o_ref, recv1, send2, recv2, piece, recv3, chunk, *sems, sizes):
    group_axes, ring_axes = ("row", "col"), ("dp",)
    n_group = sizes["row"] * sizes["col"]
    n_ring = sizes["dp"]
    me_group = lax.axis_index("row") * sizes["col"] + lax.axis_index("col")
    me_ring = lax.axis_index("dp")
    barrier = pltpu.get_barrier_semaphore()
    for s in range(1, n_group):
        peer = member_coords(lax.rem(me_group + s, n_group), group_axes, sizes)
        pl.semaphore_signal(barrier, inc=1, device_id=peer, device_id_type=pl.DeviceIdType.MESH)
    for s in range(1, n_ring):
        peer = member_coords(lax.rem(me_ring + s, n_ring), ring_axes, sizes)
        pl.semaphore_signal(barrier, inc=1, device_id=peer, device_id_type=pl.DeviceIdType.MESH)
    pl.semaphore_wait(barrier, n_group - 1 + n_ring - 1)

    def phase(source, target, me, n, axes, send_sem, recv_sem, local_sem, gather):
        copies = []
        for s in range(1, n):
            dst = lax.rem(me + s, n)
            copy = pltpu.make_async_remote_copy(
                src_ref=source if gather else source.at[dst],
                dst_ref=target.at[me],
                send_sem=send_sem.at[s - 1],
                recv_sem=recv_sem.at[s - 1],
                device_id=member_coords(dst, axes, sizes),
                device_id_type=pl.DeviceIdType.MESH,
            )
            copy.start()
            copies.append(copy)
        local = pltpu.make_async_copy(source if gather else source.at[me], target.at[me], local_sem)
        local.start()
        for copy in copies:
            copy.wait_send()
            copy.wait_recv()
        local.wait()

    phase(p_ref, recv1, me_group, n_group, group_axes, sems[0], sems[1], sems[8], False)
    total = recv1[0]
    for j in range(1, n_group):
        total = total + recv1[j]
    for j in range(n_ring):
        send2[j] = total[j : j + 1]
    phase(send2, recv2, me_ring, n_ring, ring_axes, sems[2], sems[3], sems[9], False)
    reduced = recv2[0]
    for j in range(1, n_ring):
        reduced = reduced + recv2[j]
    piece[...] = reduced
    phase(piece, recv3, me_ring, n_ring, ring_axes, sems[4], sems[5], sems[10], True)
    for j in range(n_ring):
        chunk[j : j + 1] = recv3[j]
    phase(chunk, o_ref, me_group, n_group, group_axes, sems[6], sems[7], sems[11], True)


def all_sum_small(value, sizes):
    shape = value.shape
    n_group = sizes["row"] * sizes["col"]
    n_ring = sizes["dp"]
    width = value.size // (n_group * n_ring)
    parts = value.reshape(n_group, n_ring, width)
    vmem = pl.BlockSpec(memory_space=pltpu.VMEM)
    out = pl.pallas_call(
        functools.partial(allsum_kernel, sizes=sizes),
        out_shape=jax.ShapeDtypeStruct(parts.shape, parts.dtype),
        in_specs=[vmem],
        out_specs=vmem,
        scratch_shapes=[
            pltpu.VMEM((n_group, n_ring, width), jnp.float32),
            pltpu.VMEM((n_ring, 1, width), jnp.float32),
            pltpu.VMEM((n_ring, 1, width), jnp.float32),
            pltpu.VMEM((1, width), jnp.float32),
            pltpu.VMEM((n_ring, 1, width), jnp.float32),
            pltpu.VMEM((n_ring, width), jnp.float32),
        ]
        + [pltpu.SemaphoreType.DMA((n - 1,)) for n in (n_group, n_group, n_ring, n_ring, n_ring, n_ring, n_group, n_group)]
        + [pltpu.SemaphoreType.DMA] * 4,
        compiler_params=pltpu.CompilerParams(collective_id=0, has_side_effects=True),
    )(parts)
    return out.reshape(shape)


def permute_sum(value, axis, sizes):
    n = sizes[axis]
    me = lax.axis_index(axis)
    total = lax.dynamic_index_in_dim(value, me, 0, keepdims=False)
    for shift in range(1, n):
        slab = lax.dynamic_index_in_dim(value, lax.rem(me + shift, n), 0, keepdims=False)
        total = total + lax.ppermute(slab, axis, [(i, (i + shift) % n) for i in range(n)])
    return total


def block_sum(value, sizes):
    shape = value.shape
    blocks, rows_n, cols_n = sizes["dp"], sizes["row"], sizes["col"]
    group = rows_n * cols_n
    block_rows = shape[0] // blocks
    piece_rows = -(-block_rows // (group * 8)) * 8
    lanes = math.prod(shape[1:])
    padded = jnp.pad(value.reshape(blocks, block_rows, lanes), ((0, 0), (0, piece_rows * group - block_rows), (0, 0)))
    pieces = padded.reshape(blocks, rows_n, cols_n, piece_rows, lanes)
    half = blocks // 4
    first = pieces[:half].transpose(1, 2, 0, 3, 4)
    second = pieces[half:].transpose(2, 1, 0, 3, 4)
    first, second = permute_sum(first, "row", sizes), permute_sum(second, "col", sizes)
    first, second = exchange_many([(first, ("col",), False), (second, ("row",), False)], sizes, 5)
    pieces = jnp.concatenate([first.sum(0), second.sum(0)])
    piece = exchange(pieces, ("dp",), sizes, 6).sum(0)
    block = exchange(piece, ("row", "col"), sizes, 7, gather=True)
    return block.reshape(group * piece_rows, lanes)[:block_rows].reshape((block_rows,) + shape[1:])


def solution(mesh):
    placed = (
        P("dp", "row", "col", None),
        P("dp", "row", "col", None),
        P("dp", "row", "col", None),
        P(),
        P(),
    )
    sizes = dict(mesh.shape)
    return jax.shard_map(
        functools.partial(on_device, sizes=sizes),
        mesh=mesh,
        in_specs=placed,
        out_specs=(P("dp", None, None), P("dp", None, None)),
        check_vma=False,
    )
```

```python
import functools
import math

import jax
import jax.numpy as jnp
from jax import lax
from jax.experimental import pallas as pl
from jax.experimental.pallas import tpu as pltpu
from jax.sharding import PartitionSpec as P


def member_coords(j, axes, sizes):
    coords = {}
    for axis in reversed(axes):
        coords[axis] = lax.rem(j, sizes[axis])
        j = j // sizes[axis]
    return coords


def exchange_kernel(*refs, jobs, sizes):
    count = len(jobs)
    x_refs, o_refs = refs[:count], refs[count : 2 * count]
    sems = refs[2 * count :]
    barrier = pltpu.get_barrier_semaphore()
    plans = []
    total = 0
    for axes, gather in jobs:
        n = math.prod(sizes[a] for a in axes)
        me = 0
        for axis in axes:
            me = me * sizes[axis] + lax.axis_index(axis)
        for s in range(1, n):
            peer = member_coords(lax.rem(me + s, n), axes, sizes)
            pl.semaphore_signal(barrier, inc=1, device_id=peer, device_id_type=pl.DeviceIdType.MESH)
        total += n - 1
        plans.append((n, me))
    pl.semaphore_wait(barrier, total)
    copies, locals_ = [], []
    for job, ((axes, gather), (n, me)) in enumerate(zip(jobs, plans)):
        x_ref, o_ref = x_refs[job], o_refs[job]
        send_sem, recv_sem, local_sem = sems[3 * job : 3 * job + 3]
        for s in range(1, n):
            dst = lax.rem(me + s, n)
            copy = pltpu.make_async_remote_copy(
                src_ref=x_ref if gather else x_ref.at[dst],
                dst_ref=o_ref.at[me],
                send_sem=send_sem.at[s - 1],
                recv_sem=recv_sem.at[s - 1],
                device_id=member_coords(dst, axes, sizes),
                device_id_type=pl.DeviceIdType.MESH,
            )
            copy.start()
            copies.append(copy)
        local = pltpu.make_async_copy(x_ref if gather else x_ref.at[me], o_ref.at[me], local_sem)
        local.start()
        locals_.append(local)
    for copy in copies:
        copy.wait_send()
        copy.wait_recv()
    for local in locals_:
        local.wait()


def exchange_many(items, sizes, cid):
    jobs, shapes, scratch = [], [], []
    for x, axes, gather in items:
        n = math.prod(sizes[a] for a in axes)
        slab = x.shape if gather else x.shape[1:]
        jobs.append((axes, gather))
        shapes.append(jax.ShapeDtypeStruct((n,) + slab, x.dtype))
        scratch += [
            pltpu.SemaphoreType.DMA((max(n - 1, 1),)),
            pltpu.SemaphoreType.DMA((max(n - 1, 1),)),
            pltpu.SemaphoreType.DMA,
        ]
    return pl.pallas_call(
        functools.partial(exchange_kernel, jobs=tuple(jobs), sizes=sizes),
        out_shape=tuple(shapes),
        in_specs=[pl.BlockSpec(memory_space=pltpu.VMEM)] * len(items),
        out_specs=tuple(pl.BlockSpec(memory_space=pltpu.VMEM) for _ in items),
        scratch_shapes=scratch,
        compiler_params=pltpu.CompilerParams(
            collective_id=cid, has_side_effects=True, vmem_limit_bytes=48 * 1024 * 1024
        ),
    )(*[x for x, _, _ in items])


def exchange(x, axes, sizes, cid, gather=False):
    return exchange_many([(x, axes, gather)], sizes, cid)[0]


HALO_MOVES = ((1, 0), (-1, 0), (0, 1), (0, -1), (1, 1), (1, -1), (-1, 1), (-1, -1))


def halo_kernel(*refs, sizes):
    sends, recvs = refs[:3], refs[3:6]
    send_sem, recv_sem = refs[6:8]
    row, col = lax.axis_index("row"), lax.axis_index("col")

    def target(dr, dc):
        return {"row": lax.rem(row + dr + sizes["row"], sizes["row"]), "col": lax.rem(col + dc + sizes["col"], sizes["col"])}

    barrier = pltpu.get_barrier_semaphore()
    for dr, dc in HALO_MOVES:
        pl.semaphore_signal(barrier, inc=1, device_id=target(dr, dc), device_id_type=pl.DeviceIdType.MESH)
    pl.semaphore_wait(barrier, len(HALO_MOVES))
    copies = []
    for k, (dr, dc) in enumerate(HALO_MOVES):
        kind, slot = (0, k) if k < 2 else ((1, k - 2) if k < 4 else (2, k - 4))
        copy = pltpu.make_async_remote_copy(
            src_ref=sends[kind].at[slot],
            dst_ref=recvs[kind].at[slot],
            send_sem=send_sem.at[k],
            recv_sem=recv_sem.at[k],
            device_id=target(dr, dc),
            device_id_type=pl.DeviceIdType.MESH,
        )
        copy.start()
        copies.append(copy)
    for copy in copies:
        copy.wait_send()
        copy.wait_recv()


def padded_pair(tiles, sizes):
    rows_out = jnp.stack([tiles[:, -1], tiles[:, 0]])
    cols_out = jnp.stack([tiles[:, :, -1], tiles[:, :, 0]])
    corners_out = jnp.stack([tiles[:, -1, -1], tiles[:, -1, 0], tiles[:, 0, -1], tiles[:, 0, 0]])
    sends = (rows_out, cols_out, corners_out)
    recvs = pl.pallas_call(
        functools.partial(halo_kernel, sizes=sizes),
        out_shape=tuple(jax.ShapeDtypeStruct(x.shape, x.dtype) for x in sends),
        in_specs=[pl.BlockSpec(memory_space=pltpu.VMEM)] * 3,
        out_specs=tuple(pl.BlockSpec(memory_space=pltpu.VMEM) for _ in sends),
        scratch_shapes=[pltpu.SemaphoreType.DMA((len(HALO_MOVES),)), pltpu.SemaphoreType.DMA((len(HALO_MOVES),))],
        compiler_params=pltpu.CompilerParams(collective_id=8, has_side_effects=True),
    )(*sends)
    rows_in, cols_in, corners_in = recvs
    row, col = lax.axis_index("row"), lax.axis_index("col")
    up, down = row > 0, row < sizes["row"] - 1
    left, right = col > 0, col < sizes["col"] - 1
    zero = jnp.zeros((), tiles.dtype)
    top = jnp.where(up, rows_in[0], zero)
    bottom = jnp.where(down, rows_in[1], zero)
    west = jnp.where(left, cols_in[0], zero)
    east = jnp.where(right, cols_in[1], zero)
    top_left = jnp.where(up & left, corners_in[0], zero)
    top_right = jnp.where(up & right, corners_in[1], zero)
    bottom_left = jnp.where(down & left, corners_in[2], zero)
    bottom_right = jnp.where(down & right, corners_in[3], zero)
    padded = []
    for k in range(tiles.shape[0]):
        first = jnp.concatenate([top_left[k, None], top[k], top_right[k, None]], axis=0)
        middle = jnp.concatenate([west[k, :, None], tiles[k], east[k, :, None]], axis=1)
        last = jnp.concatenate([bottom_left[k, None], bottom[k], bottom_right[k, None]], axis=0)
        padded.append(jnp.concatenate([first[None], middle, last[None]], axis=0))
    return padded


def silu_slope(pre_float):
    sigma = jax.nn.sigmoid(pre_float)
    return sigma * (1.0 + pre_float * (1.0 - sigma))


def exact_dot(left, right, contract):
    return lax.dot_general(
        left.astype(jnp.float32),
        right.astype(jnp.float32),
        (contract, ((), ())),
        precision=lax.Precision.HIGHEST,
        preferred_element_type=jnp.float32,
    )


TAPS = [(a, b) for a in (-1, 0, 1) for b in (-1, 0, 1)]


def on_device(x_input, pre_act, out_grad, conv_weight, q_prev, sizes):
    height, breadth, channels = (x_input.shape[1], x_input.shape[2], x_input.shape[3])
    pixels = height * breadth
    rank = q_prev.shape[2]
    taps = len(TAPS)
    pre_float = pre_act.reshape(pixels, channels).astype(jnp.float32)
    hidden = jax.nn.silu(pre_float).astype(jnp.bfloat16)
    both_pad = padded_pair(
        jnp.stack([out_grad.reshape(height, breadth, channels), x_input.reshape(height, breadth, channels)]), sizes
    )
    grad_pad, input_pad = both_pad
    back_grad = jnp.zeros((pixels, channels), jnp.float32)
    for a, b in TAPS:
        window = grad_pad[1 - a : 1 - a + height, 1 - b : 1 - b + breadth].reshape(pixels, channels)
        back_grad = back_grad + lax.dot_general(
            window, conv_weight[a + 1, b + 1], (((1,), (1,)), ((), ())), preferred_element_type=jnp.float32
        )
    pre_grad = (back_grad * silu_slope(pre_float)).astype(jnp.bfloat16)

    grid = (height + 2, breadth + 2)
    grad_flat = grad_pad.reshape(-1, channels)
    input_flat = input_pad.reshape(-1, channels)
    q_taps = q_prev.reshape(taps, channels, 2, rank).transpose(2, 1, 0, 3).reshape(2, channels, taps * rank)

    first_terms = exact_dot(input_flat, q_taps[0], ((1,), (0,))).reshape(grid + (taps * rank,))
    first_sum = sum(
        first_terms[1 + a : 1 + a + height, 1 + b : 1 + b + breadth, k * rank : (k + 1) * rank]
        for k, (a, b) in enumerate(TAPS)
    ).reshape(pixels, rank)
    first_raw = exact_dot(pre_grad, first_sum, ((0,), (0,)))
    second_terms = exact_dot(hidden, q_taps[1], ((1,), (0,))).reshape(height, breadth, taps * rank)
    second_sum = sum(
        jnp.pad(second_terms[:, :, k * rank : (k + 1) * rank], ((1 - a, 1 + a), (1 - b, 1 + b), (0, 0)))
        for k, (a, b) in enumerate(TAPS)
    ).reshape(-1, rank)
    second_raw = exact_dot(grad_flat, second_sum, ((0,), (0,)))

    power_raw = all_sum_small(jnp.stack([first_raw, second_raw], axis=1), sizes)

    first_image = exact_dot(pre_grad, power_raw[:, 0], ((1,), (0,))).reshape(height, breadth, rank)
    first_spread = jnp.concatenate(
        [
            jnp.pad(first_image, ((1 + a, 1 - a), (1 + b, 1 - b), (0, 0))).reshape(-1, rank)
            for a, b in TAPS
        ],
        axis=1,
    )
    first_rows = exact_dot(input_flat, first_spread, ((0,), (0,)))
    second_image = exact_dot(grad_flat, power_raw[:, 1], ((1,), (0,))).reshape(grid + (rank,))
    second_spread = jnp.concatenate(
        [
            second_image[1 - a : 1 - a + height, 1 - b : 1 - b + breadth].reshape(pixels, rank)
            for a, b in TAPS
        ],
        axis=1,
    )
    second_rows = exact_dot(hidden, second_spread, ((0,), (0,)))
    rows = jnp.concatenate(
        [
            first_rows.reshape(channels, taps, rank).transpose(1, 0, 2),
            second_rows.reshape(channels, taps, rank).transpose(1, 0, 2),
        ],
        axis=-1,
    ).reshape(taps * channels, 2, rank)
    row_block = block_sum(rows, sizes)

    gram = jnp.einsum(
        "mqn,mqg->qng", power_raw, power_raw, precision=lax.Precision.HIGHEST, preferred_element_type=jnp.float32
    )
    lower = jnp.linalg.cholesky(gram)
    basis_count = channels // sizes["dp"]
    raw_part = lax.dynamic_slice_in_dim(power_raw, lax.axis_index("dp") * basis_count, basis_count, 0)
    basis_out = lax.linalg.triangular_solve(
        lower, raw_part.transpose(1, 0, 2), left_side=False, lower=True, transpose_a=True
    ).transpose(1, 0, 2)
    factor_out = lax.linalg.triangular_solve(
        lower, row_block.transpose(1, 0, 2), left_side=False, lower=True, transpose_a=True
    ).transpose(1, 0, 2)
    return (basis_out, factor_out)


def allsum_kernel(p_ref, o_ref, recv1, send2, recv2, piece, recv3, chunk, *sems, sizes):
    group_axes, ring_axes = ("row", "col"), ("dp",)
    n_group = sizes["row"] * sizes["col"]
    n_ring = sizes["dp"]
    me_group = lax.axis_index("row") * sizes["col"] + lax.axis_index("col")
    me_ring = lax.axis_index("dp")
    barrier = pltpu.get_barrier_semaphore()
    for s in range(1, n_group):
        peer = member_coords(lax.rem(me_group + s, n_group), group_axes, sizes)
        pl.semaphore_signal(barrier, inc=1, device_id=peer, device_id_type=pl.DeviceIdType.MESH)
    for s in range(1, n_ring):
        peer = member_coords(lax.rem(me_ring + s, n_ring), ring_axes, sizes)
        pl.semaphore_signal(barrier, inc=1, device_id=peer, device_id_type=pl.DeviceIdType.MESH)
    pl.semaphore_wait(barrier, n_group - 1 + n_ring - 1)

    def phase(source, target, me, n, axes, send_sem, recv_sem, local_sem, gather):
        copies = []
        for s in range(1, n):
            dst = lax.rem(me + s, n)
            copy = pltpu.make_async_remote_copy(
                src_ref=source if gather else source.at[dst],
                dst_ref=target.at[me],
                send_sem=send_sem.at[s - 1],
                recv_sem=recv_sem.at[s - 1],
                device_id=member_coords(dst, axes, sizes),
                device_id_type=pl.DeviceIdType.MESH,
            )
            copy.start()
            copies.append(copy)
        local = pltpu.make_async_copy(source if gather else source.at[me], target.at[me], local_sem)
        local.start()
        for copy in copies:
            copy.wait_send()
            copy.wait_recv()
        local.wait()

    phase(p_ref, recv1, me_group, n_group, group_axes, sems[0], sems[1], sems[8], False)
    total = recv1[0]
    for j in range(1, n_group):
        total = total + recv1[j]
    for j in range(n_ring):
        send2[j] = total[j : j + 1]
    phase(send2, recv2, me_ring, n_ring, ring_axes, sems[2], sems[3], sems[9], False)
    reduced = recv2[0]
    for j in range(1, n_ring):
        reduced = reduced + recv2[j]
    piece[...] = reduced
    phase(piece, recv3, me_ring, n_ring, ring_axes, sems[4], sems[5], sems[10], True)
    for j in range(n_ring):
        chunk[j : j + 1] = recv3[j]
    phase(chunk, o_ref, me_group, n_group, group_axes, sems[6], sems[7], sems[11], True)


def all_sum_small(value, sizes):
    shape = value.shape
    n_group = sizes["row"] * sizes["col"]
    n_ring = sizes["dp"]
    width = value.size // (n_group * n_ring)
    parts = value.reshape(n_group, n_ring, width)
    vmem = pl.BlockSpec(memory_space=pltpu.VMEM)
    out = pl.pallas_call(
        functools.partial(allsum_kernel, sizes=sizes),
        out_shape=jax.ShapeDtypeStruct(parts.shape, parts.dtype),
        in_specs=[vmem],
        out_specs=vmem,
        scratch_shapes=[
            pltpu.VMEM((n_group, n_ring, width), jnp.float32),
            pltpu.VMEM((n_ring, 1, width), jnp.float32),
            pltpu.VMEM((n_ring, 1, width), jnp.float32),
            pltpu.VMEM((1, width), jnp.float32),
            pltpu.VMEM((n_ring, 1, width), jnp.float32),
            pltpu.VMEM((n_ring, width), jnp.float32),
        ]
        + [pltpu.SemaphoreType.DMA((n - 1,)) for n in (n_group, n_group, n_ring, n_ring, n_ring, n_ring, n_group, n_group)]
        + [pltpu.SemaphoreType.DMA] * 4,
        compiler_params=pltpu.CompilerParams(collective_id=0, has_side_effects=True),
    )(parts)
    return out.reshape(shape)


def permute_sum(value, axis, sizes):
    n = sizes[axis]
    me = lax.axis_index(axis)
    total = lax.dynamic_index_in_dim(value, me, 0, keepdims=False)
    for shift in range(1, n):
        slab = lax.dynamic_index_in_dim(value, lax.rem(me + shift, n), 0, keepdims=False)
        total = total + lax.ppermute(slab, axis, [(i, (i + shift) % n) for i in range(n)])
    return total


def block_sum(value, sizes):
    shape = value.shape
    blocks, rows_n, cols_n = sizes["dp"], sizes["row"], sizes["col"]
    group = rows_n * cols_n
    block_rows = shape[0] // blocks
    piece_rows = -(-block_rows // (group * 8)) * 8
    lanes = math.prod(shape[1:])
    padded = jnp.pad(value.reshape(blocks, block_rows, lanes), ((0, 0), (0, piece_rows * group - block_rows), (0, 0)))
    pieces = padded.reshape(blocks, rows_n, cols_n, piece_rows, lanes)
    half = blocks * 5 // 16
    first = pieces[:half].transpose(1, 2, 0, 3, 4)
    second = pieces[half:].transpose(2, 1, 0, 3, 4)
    first, second = permute_sum(first, "row", sizes), permute_sum(second, "col", sizes)
    first, second = exchange_many([(first, ("col",), False), (second, ("row",), False)], sizes, 5)
    pieces = jnp.concatenate([first.sum(0), second.sum(0)])
    piece = exchange(pieces, ("dp",), sizes, 6).sum(0)
    block = exchange(piece, ("row", "col"), sizes, 7, gather=True)
    return block.reshape(group * piece_rows, lanes)[:block_rows].reshape((block_rows,) + shape[1:])


def solution(mesh):
    placed = (
        P("dp", "row", "col", None),
        P("dp", "row", "col", None),
        P("dp", "row", "col", None),
        P(),
        P(),
    )
    sizes = dict(mesh.shape)
    return jax.shard_map(
        functools.partial(on_device, sizes=sizes),
        mesh=mesh,
        in_specs=placed,
        out_specs=(P("dp", None, None), P("dp", None, None)),
        check_vma=False,
    )
```
